32 devices in a mesh: seq: 8 (over z, core), tp: 4 (over y, x).
Axes of the slice: x: 2, y: 2, z: 4, core: 2. Of those that a mesh axis runs over, the one named last changes fastest.
Arguments:
- layer_in: bfloat16 [4096, 2048], P('seq'), may hold values from -6 to 6
- positions: int32 [4096], P('seq'), may hold values from 0 to 2047, as said below
- seq_ids: int32 [4096], P('seq'), may hold values from 0 to 1, as said below
- norm1_gain: float32 [2048], replicated, may hold values from 0.5 to 1.5
- norm2_gain: float32 [2048], replicated, may hold values from 0.5 to 1.5
- w_query: float32 [2048, 2048], P('seq', 'tp'), may hold values from -0.125 to 0.125
- w_key: float32 [2048, 2048], P('seq', 'tp'), may hold values from -0.125 to 0.125
- w_value: float32 [2048, 2048], P('seq', 'tp'), may hold values from -0.125 to 0.125
- w_out: float32 [2048, 2048], P('tp', 'seq'), may hold values from -4 to 4
- w_gate: float32 [2048, 8192], P('seq', 'tp'), may hold values from -0.125 to 0.125
- w_up: float32 [2048, 8192], P('seq', 'tp'), may hold values from -0.125 to 0.125
- w_down: float32 [8192, 2048], P('tp', 'seq'), may hold values from -0.0625 to 0.0625
- out_grad: bfloat16 [4096, 2048], P('seq'), may hold values from -6 to 6
Outputs:
- layer_out: bfloat16 [4096, 2048], P('seq')
- in_grad: float32 [4096, 2048], P('seq')
- grad_norm1: float32 [2048], P('seq')
- grad_norm2: float32 [2048], P('seq')
- grad_w_query: float32 [2048, 2048], P('seq', 'tp')
- grad_w_key: float32 [2048, 2048], P('seq', 'tp')
- grad_w_value: float32 [2048, 2048], P('seq', 'tp')
- grad_w_out: float32 [2048, 2048], P('tp', 'seq')
- grad_w_gate: float32 [2048, 8192], P('seq', 'tp')
- grad_w_up: float32 [2048, 8192], P('seq', 'tp')
- grad_w_down: float32 [8192, 2048], P('tp', 'seq')
The draws below stay inside these ranges and needn't reach their ends.
Inputs may be any that keep to these rules, and one draw needn't show every extreme that they name: The shard of 512 rows at index r of seq holds, in an order that varies from shard to shard, four blocks of 128 consecutive positions: for each of the two sequences its blocks number r and 15 - r. Each position of each sequence appears once. `seq_ids`: the sequence of each row, constant over each block of 128 rows described for positions; each shard holds two such blocks of each sequence, and each sequence has 2048 rows.
All inputs are finite; a program needn't handle non-finite values.
Results may differ from the reference program's by a relative error of at most 0.024.
Values may be sent and summed in bfloat16 or wider, within the bound.
No kernel may reach another device: no remote copies, remote signals or barrier semaphores. Data moves between devices by JAX's collectives and lax.ppermute only.
A program may use at most 192 MiB of HBM per device.

```python
import math
import jax
import jax.numpy as jnp
from jax import lax

D = 2048
HEADS = 16
HD = 128
FF = 8192
TOK_DEV = 512
TOKENS = 4096
LENGTH = 2048


def group_layout(key):
    shard_count = TOKENS // TOK_DEV
    block_width = TOK_DEV // 4
    order_keys = jax.random.split(jax.random.fold_in(key, 7), shard_count)
    orders = jax.vmap(lambda sub_key: jax.random.permutation(sub_key, 4))(order_keys)
    flip_bit = jax.random.randint(jax.random.fold_in(key, 11), (), 0, 2)
    shard_rank = jnp.arange(shard_count, dtype=jnp.int32)[:, None]
    block_index = jnp.where(orders % 2 == 0, shard_rank, 2 * shard_count - 1 - shard_rank)
    sequence = (orders // 2 + flip_bit) % 2
    places = block_index[:, :, None] * block_width + jnp.arange(block_width, dtype=jnp.int32)[None, None, :]
    labels = jnp.broadcast_to(sequence[:, :, None], (shard_count, 4, block_width))
    return (places.reshape(-1).astype(jnp.int32), labels.reshape(-1).astype(jnp.int32))


def draw_positions(key, part):
    return group_layout(key)[0]


def draw_seq_ids(key, part):
    return group_layout(key)[1]


def block_levels(stream_key, dims, shards, smallest, largest):
    factor_of = 1.0
    for position, parts in shards:
        draws = jax.random.uniform(jax.random.fold_in(jax.random.fold_in(stream_key, 6), position), (parts,), jnp.float32, smallest / len(shards), largest / len(shards))
        factor_of = factor_of * jnp.repeat(jnp.exp(draws), dims[position] // parts).reshape((-1,) + (1,) * (len(dims) - 1 - position))
    return factor_of


def gaussian(own_key, shape, deviation, most, cuts=(), held_as=jnp.bfloat16):
    entries = jax.random.normal(own_key, shape, jnp.float32) * deviation
    if len(cuts) > 0:
        entries = block_levels(own_key, shape, cuts, -0.22, 0.18) * entries
    return jnp.clip(entries, min=-most, max=most).astype(held_as)


def setup_inputs(seed: int = 0) -> dict:
    keys = jax.random.split(jax.random.key(seed), 14)
    return {
        "layer_in": gaussian(keys[0], (TOKENS, D), 1.0, 6.0, ((0, 8),)),
        "positions": draw_positions(jax.random.fold_in(keys[13], 71), 0),
        "seq_ids": draw_seq_ids(jax.random.fold_in(keys[13], 71), 0),
        "norm1_gain": jnp.clip(1.0 + 0.1 * jax.random.normal(keys[3], (D,), jnp.float32), 0.5, 1.5),
        "norm2_gain": jnp.clip(1.0 + 0.1 * jax.random.normal(keys[4], (D,), jnp.float32), 0.5, 1.5),
        "w_query": gaussian(keys[5], (D, D), D ** -0.5, 0.125, ((0, 8), (1, 4)), jnp.float32),
        "w_key": gaussian(keys[6], (D, D), D ** -0.5, 0.125, ((0, 8), (1, 4)), jnp.float32),
        "w_value": gaussian(keys[7], (D, D), D ** -0.5, 0.125, ((0, 8), (1, 4)), jnp.float32),
        "w_out": gaussian(keys[8], (D, D), 2 ** -0.5, 4.0, ((0, 4), (1, 8)), jnp.float32),
        "w_gate": gaussian(keys[9], (D, FF), D ** -0.5, 0.125, ((0, 8), (1, 4)), jnp.float32),
        "w_up": gaussian(keys[10], (D, FF), D ** -0.5, 0.125, ((0, 8), (1, 4)), jnp.float32),
        "w_down": gaussian(keys[11], (FF, D), FF ** -0.5, 0.0625, ((0, 4), (1, 8)), jnp.float32),
        "out_grad": gaussian(keys[12], (TOKENS, D), 1.0, 6.0, ((0, 8),)),
    }


PRECISE = lax.Precision.HIGHEST
EPSILON = 1e-06

@jax.custom_vjp
def low(v):
    return lax.optimization_barrier(v.astype(jnp.bfloat16)).astype(jnp.float32)

@jax.custom_vjp
def low_back(v):
    return v

def low_keep(v):
    return (low(v), None)

def low_pass(kept, grad):
    return (grad,)

def back_keep(v):
    return (v, None)

def back_low(kept, grad):
    return (low(grad),)
low.defvjp(low_keep, low_pass)
low_back.defvjp(back_keep, back_low)

def matmul(left, right):
    return jnp.dot(left, right, precision=PRECISE, preferred_element_type=jnp.float32)

def normalize(values, gain):
    return values * lax.rsqrt(lax.optimization_barrier(jnp.mean(values * values, axis=-1, keepdims=True)) + EPSILON) * gain

def angles(places):
    half_width = HD // 2
    frequency = jnp.power(jnp.float32(10000.0), -jnp.arange(half_width, dtype=jnp.float32) / half_width)
    phase_angle = places.astype(jnp.float32)[:, None] * frequency[None, :]
    return (jnp.cos(phase_angle)[:, None, :], jnp.sin(phase_angle)[:, None, :])

def rotate(heads, rot_cos, rot_sin):
    half_width = heads.shape[-1] // 2
    front_half = heads[..., :half_width]
    back_half = heads[..., half_width:]
    return jnp.concatenate([front_half * rot_cos - back_half * rot_sin, back_half * rot_cos + front_half * rot_sin], axis=-1)

def reference(layer_in, positions, seq_ids, norm1_gain, norm2_gain, w_query, w_key, w_value, w_out, w_gate, w_up, w_down, out_grad):
    rot_cos, rot_sin = angles(positions)
    score_scale = 1.0 / math.sqrt(HD)
    score_bias = -math.log(LENGTH)

    def forward(inputs, gain_one, gain_two, query_w, key_w, value_w, out_w, gate_w, up_w, down_w):
        row_count = inputs.shape[0]
        normed_one = low(normalize(inputs, gain_one))
        query_heads = low(rotate(low_back(matmul(normed_one, low(query_w))).reshape(row_count, HEADS, HD), rot_cos, rot_sin))
        key_heads = low(rotate(low_back(matmul(normed_one, low(key_w))).reshape(row_count, HEADS, HD), rot_cos, rot_sin))
        value_heads = low(low_back(matmul(normed_one, low(value_w)))).reshape(row_count, HEADS, HD)
        block_rows = math.gcd(row_count, 512)
        block_count = row_count // block_rows

        def attend(block_args):
            query_block, pos_block, seq_block = block_args
            raw = jnp.einsum('qhd,khd->hqk', query_block, key_heads, precision=PRECISE) * score_scale + score_bias
            scores = low_back(raw)
            allowed = (seq_block[:, None] == seq_ids[None, :]) & (positions[None, :] <= pos_block[:, None])
            weights = low(jax.nn.sigmoid(scores)) * allowed.astype(jnp.float32)[None]
            return jnp.einsum('hqk,khd->qhd', weights, value_heads, precision=PRECISE)
        mixed = lax.map(jax.checkpoint(attend), (query_heads.reshape(block_count, block_rows, HEADS, HD), positions.reshape(block_count, block_rows), seq_ids.reshape(block_count, block_rows)))
        mixed = low(low_back(mixed.reshape(row_count, D)))
        residual = inputs + low_back(matmul(mixed, low(out_w)))
        normed_two = low(normalize(residual, gain_two))
        gate = low_back(matmul(normed_two, low(gate_w)))
        up_proj = low_back(matmul(normed_two, low(up_w)))
        hidden = low(jax.nn.silu(gate) * up_proj)
        return residual + low_back(matmul(hidden, low(down_w)))
    primals = (layer_in.astype(jnp.float32), norm1_gain, norm2_gain, w_query, w_key, w_value, w_out, w_gate, w_up, w_down)
    result, pullback = jax.vjp(forward, *primals)
    gradients = pullback(out_grad.astype(jnp.float32))
    return (result.astype(jnp.bfloat16), gradients[0], gradients[1], gradients[2], gradients[3], gradients[4], gradients[5], gradients[6], gradients[7], gradients[8], gradients[9])
```

```python
import functools
import math

import jax
import jax.numpy as jnp
from jax import lax
from jax.experimental import pallas as pl
from jax.experimental.pallas import tpu as pltpu
from jax.sharding import Mesh
from jax.sharding import PartitionSpec as P

HD = 128
EPSILON = 1e-06
LOG2E = 1.4426950408889634
BF = jnp.bfloat16
F32 = jnp.float32


def dot_nt(left, right):
    return lax.dot_general(left, right, (((1,), (1,)), ((), ())), preferred_element_type=F32)


def dot_nn(left, right):
    return lax.dot_general(left, right, (((1,), (0,)), ((), ())), preferred_element_type=F32)


def dot_tn(left, right):
    return lax.dot_general(left, right, (((0,), (0,)), ((), ())), preferred_element_type=F32)


def attend_kernel(
    tab_ref, qkv_ref, cos_ref, sin_ref, out_ref, q_ref, k_ref, v_ref, acc_ref, *, chunk, tile, bias2
):
    groups, rows, _ = qkv_ref.shape
    per_group = rows // chunk
    length = groups * rows
    for j in range(length // chunk):
        g, s = divmod(j, per_group)
        here = pl.ds(s * chunk, chunk)
        there = pl.ds(pl.multiple_of(tab_ref[j] * chunk, chunk), chunk)
        cos = cos_ref[there, :]
        sin = sin_ref[there, :]
        q = qkv_ref[g, here, 0:HD].astype(F32)
        k = qkv_ref[g, here, HD : 2 * HD].astype(F32)
        q_ref[there, :] = (q * cos - pltpu.roll(q, HD // 2, 1) * sin).astype(BF)
        k_ref[there, :] = (k * cos - pltpu.roll(k, HD // 2, 1) * sin).astype(BF)
        v_ref[there, :] = qkv_ref[g, here, 2 * HD : 3 * HD]
    slope = -LOG2E / math.sqrt(HD)

    def part(i, j, masked):
        qs = q_ref[pl.ds(i * tile, tile), :]
        ks = k_ref[pl.ds(j * tile, tile), :]
        vs = v_ref[pl.ds(j * tile, tile), :]
        sig = 1.0 / (1.0 + jnp.exp2(dot_nt(qs, ks) * slope + bias2))
        if masked:
            row = lax.broadcasted_iota(jnp.int32, (tile, tile), 0)
            col = lax.broadcasted_iota(jnp.int32, (tile, tile), 1)
            sig = jnp.where(col <= row, sig, 0.0)
        return dot_nn(sig.astype(BF), vs)

    def query(i, carry):
        own = pl.ds(pl.multiple_of(i * tile, tile), tile)
        acc_ref[own, :] = part(i, i, True)

        def key(j, carry):
            acc_ref[own, :] += part(i, j, False)
            return carry

        lax.fori_loop(0, i, key, 0)
        return carry

    lax.fori_loop(0, length // tile, query, 0)
    for j in range(length // chunk):
        g, s = divmod(j, per_group)
        there = pl.ds(pl.multiple_of(tab_ref[j] * chunk, chunk), chunk)
        out_ref[g, pl.ds(s * chunk, chunk), :] = acc_ref[there, :].astype(BF)


def attend_back_kernel(
    tab_ref,
    grad_ref,
    q_ref,
    k_ref,
    v_ref,
    cos_ref,
    sin_ref,
    out_ref,
    do_ref,
    dq_ref,
    dk_ref,
    dv_ref,
    *,
    chunk,
    tile,
    bias2,
):
    groups, rows, _ = grad_ref.shape
    per_group = rows // chunk
    length = groups * rows
    for j in range(length // chunk):
        g, s = divmod(j, per_group)
        there = pl.ds(pl.multiple_of(tab_ref[j] * chunk, chunk), chunk)
        do_ref[there, :] = grad_ref[g, pl.ds(s * chunk, chunk), :]
    slope = -LOG2E / math.sqrt(HD)
    scale = 1.0 / math.sqrt(HD)

    def part(i, j, masked):
        qi = pl.ds(pl.multiple_of(i * tile, tile), tile)
        kj = pl.ds(pl.multiple_of(j * tile, tile), tile)
        qs, ks, vs, dos = q_ref[qi, :], k_ref[kj, :], v_ref[kj, :], do_ref[qi, :]
        sig = 1.0 / (1.0 + jnp.exp2(dot_nt(ks, qs) * slope + bias2))
        dsc = dot_nt(vs, dos) * sig * (1.0 - sig)
        if masked:
            row = lax.broadcasted_iota(jnp.int32, (tile, tile), 0)
            col = lax.broadcasted_iota(jnp.int32, (tile, tile), 1)
            sig = jnp.where(row <= col, sig, 0.0)
            dsc = jnp.where(row <= col, dsc, 0.0)
        dsc = dsc.astype(BF)
        dv = dot_nn(sig.astype(BF), dos)
        dk = dot_nn(dsc, qs)
        dq = dot_tn(dsc, ks)
        if masked:
            dq_ref[qi, :] = dq
            dk_ref[kj, :] = dk
            dv_ref[kj, :] = dv
        else:
            dq_ref[qi, :] += dq
            dk_ref[kj, :] += dk
            dv_ref[kj, :] += dv

    def query(i, carry):
        part(i, i, True)

        def key(j, carry):
            part(i, j, False)
            return carry

        lax.fori_loop(0, i, key, 0)
        return carry

    lax.fori_loop(0, length // tile, query, 0)
    for j in range(length // chunk):
        g, s = divmod(j, per_group)
        here = pl.ds(s * chunk, chunk)
        there = pl.ds(pl.multiple_of(tab_ref[j] * chunk, chunk), chunk)
        cos = cos_ref[there, :] * scale
        sin = sin_ref[there, :] * scale
        dq = dq_ref[there, :]
        dk = dk_ref[there, :]
        out_ref[g, here, 0:HD] = (dq * cos + pltpu.roll(dq, HD // 2, 1) * sin).astype(BF)
        out_ref[g, here, HD : 2 * HD] = (dk * cos + pltpu.roll(dk, HD // 2, 1) * sin).astype(BF)
        out_ref[g, here, 2 * HD : 3 * HD] = dv_ref[there, :].astype(BF)


def attend(table, qkv, cos, sin, chunk, length):
    groups, rows, _ = qkv.shape
    tile = min(512, length)
    full = jax.ShapeDtypeStruct((length, HD), BF)
    vm = pl.BlockSpec(memory_space=pltpu.VMEM)
    return pl.pallas_call(
        functools.partial(attend_kernel, chunk=chunk, tile=tile, bias2=math.log2(length)),
        out_shape=(jax.ShapeDtypeStruct((groups, rows, HD), BF), full, full, full),
        in_specs=[pl.BlockSpec(memory_space=pltpu.SMEM), vm, vm, vm],
        out_specs=(vm, vm, vm, vm),
        scratch_shapes=[pltpu.VMEM((length, HD), F32)],
        compiler_params=pltpu.CompilerParams(vmem_limit_bytes=40 << 20),
        cost_estimate=pl.CostEstimate(
            flops=2 * length * length * HD,
            transcendentals=length * length,
            bytes_accessed=length * HD * 24,
        ),
        name="attend",
    )(table, qkv, cos, sin)


def attend_back(table, grad, q, k, v, cos, sin, chunk, length):
    groups, rows, _ = grad.shape
    tile = min(512, length)
    vm = pl.BlockSpec(memory_space=pltpu.VMEM)
    return pl.pallas_call(
        functools.partial(attend_back_kernel, chunk=chunk, tile=tile, bias2=math.log2(length)),
        out_shape=jax.ShapeDtypeStruct((groups, rows, 3 * HD), BF),
        in_specs=[pl.BlockSpec(memory_space=pltpu.SMEM)] + [vm] * 6,
        out_specs=vm,
        scratch_shapes=[pltpu.VMEM((length, HD), BF)] + [pltpu.VMEM((length, HD), F32)] * 3,
        compiler_params=pltpu.CompilerParams(vmem_limit_bytes=40 << 20),
        cost_estimate=pl.CostEstimate(
            flops=5 * length * length * HD,
            transcendentals=length * length,
            bytes_accessed=length * HD * 24,
        ),
        name="attend_back",
    )(table, grad, q, k, v, cos, sin)


def build(z_size, tp_size):
    shards = 2 * z_size
    ring = list(range(0, 1)) + list(range(1, z_size, 2)) + list(range(z_size - 2, 0, -2))
    place = [ring.index(z) for z in range(z_size)]
    forward = [(ring[i], ring[(i + 1) % z_size]) for i in range(z_size)]
    backward = [(b, a) for a, b in forward]
    half_ring = z_size // 2
    offsets = [0]
    for k in range(1, half_ring):
        offsets += [-k, k]
    offsets += [half_ring]
    holder = [[ring[(place[z] + off) % z_size] for off in offsets] for z in range(z_size)]
    swap_core = [(0, 1), (1, 0)]

    def gather_ring(x):
        chunks = [x]
        ahead = back = x
        for _ in range(1, half_ring):
            ahead = lax.ppermute(ahead, "z", forward)
            back = lax.ppermute(back, "z", backward)
            chunks += [ahead, back]
        mid = x.shape[0] // 2
        one = lax.ppermute(ahead[:mid], "z", forward)
        two = lax.ppermute(back[mid:], "z", backward)
        return jnp.concatenate(chunks + [one, two], axis=0)

    def scatter_ring(parts):
        mid = parts.shape[1] // 2
        last = len(offsets) - 1
        one = lax.ppermute(parts[last, :mid].astype(BF), "z", forward)
        two = lax.ppermute(parts[last, mid:].astype(BF), "z", backward)
        for k in range(half_ring - 1, 0, -1):
            fwd, bwd = parts[offsets.index(k)], parts[offsets.index(-k)]
            if k == half_ring - 1:
                fwd = jnp.concatenate([fwd[:mid] + one.astype(F32), fwd[mid:]], axis=0)
                bwd = jnp.concatenate([bwd[:mid], bwd[mid:] + two.astype(F32)], axis=0)
            else:
                fwd = fwd + one.astype(F32)
                bwd = bwd + two.astype(F32)
            one = lax.ppermute(fwd.astype(BF), "z", forward)
            two = lax.ppermute(bwd.astype(BF), "z", backward)
        return parts[0] + one.astype(F32) + two.astype(F32)

    def gather_tp(x):
        if tp_size != 4:
            return lax.all_gather(x, "tp", axis=0)
        index = lax.axis_index("tp")
        over_x = [(0, 1), (1, 0), (2, 3), (3, 2)]
        over_y = [(0, 2), (2, 0), (1, 3), (3, 1)]
        mid = x.shape[0] // 2
        near_x = lax.ppermute(x, "tp", over_x)
        near_y = lax.ppermute(x, "tp", over_y)
        far = jnp.concatenate(
            [lax.ppermute(near_y[:mid], "tp", over_x), lax.ppermute(near_x[mid:], "tp", over_y)]
        )
        return jnp.take(
            jnp.stack([x, near_x, near_y, far]),
            jnp.bitwise_xor(jnp.arange(4, dtype=jnp.int32), index),
            axis=0,
            mode="clip",
        )

    def on_device(
        layer_in,
        positions,
        seq_ids,
        norm1_gain,
        norm2_gain,
        w_query,
        w_key,
        w_value,
        w_out,
        w_gate,
        w_up,
        w_down,
        out_grad,
    ):
        z, core, tp = lax.axis_index("z"), lax.axis_index("core"), lax.axis_index("tp")
        rows, width = layer_in.shape
        block = rows // 4
        own = rows // tp_size
        group = own * z_size
        length = rows * shards // 2
        k_rows = width // shards
        heads = w_query.shape[1] * tp_size // HD
        heads_here = heads // z_size
        plain = w_query.shape[1] == z_size * HD and heads_here == tp_size

        def permute(x):
            lead = x.shape[:-1]
            return jnp.swapaxes(x.reshape(lead + (z_size, 2, k_rows)), -3, -2).reshape(x.shape)

        def restore(x):
            lead = x.shape[:-1]
            return jnp.swapaxes(x.reshape(lead + (2, z_size, k_rows)), -3, -2).reshape(x.shape)

        key = seq_ids.reshape(4, block)[:, 0] * (4 * length) + positions.reshape(4, block)[:, 0]
        rank = jnp.sum((key[None, :] < key[:, None]).astype(jnp.int32), axis=1)
        source_core = tp // (tp_size // 2)
        offset = (tp % (tp_size // 2)) * own

        def piece(x, seq):
            wanted = 2 * seq + offset // block
            start = jnp.sum(jnp.where(rank == wanted, jnp.arange(4, dtype=jnp.int32), 0)) * block
            return lax.dynamic_slice(x, (start + offset % block, 0), (own, width))

        both_self = jnp.stack([piece(layer_in, core), piece(out_grad, core)])
        both_other = jnp.stack([piece(layer_in, 1 - core), piece(out_grad, 1 - core)])
        both_other = lax.ppermute(both_other, "core", swap_core)
        both = permute(jnp.where(core == source_core, both_self, both_other))
        x_own = both[0].astype(F32)
        gy_own = both[1]
        gain1 = permute(norm1_gain)
        gain2 = permute(norm2_gain)
        scale1 = lax.rsqrt(jnp.mean(x_own * x_own, axis=-1, keepdims=True) + EPSILON)
        xn1 = gather_ring((x_own * scale1 * gain1).astype(BF))

        def exchange(w, split, concat):
            return lax.all_to_all(w, "z", split_axis=split, concat_axis=concat, tiled=True)

        def gather_rows(w):
            return lax.all_gather(w, ("core", "tp"), axis=0, tiled=False).reshape(
                (2, tp_size) + w.shape
            )

        def gather_cols(w):
            return lax.all_gather(w, ("tp", "core"), axis=0, tiled=False).reshape(
                tp_size, 2 * w.shape[0], w.shape[1]
            )

        if plain:
            qkv_low = jnp.stack([w_query, w_key, w_value], axis=1).astype(BF)
            qkv_low = qkv_low.reshape(k_rows, 3, z_size, HD).swapaxes(1, 2)
            qkv_low = exchange(qkv_low.reshape(k_rows, z_size * 3 * HD), 1, 0)
            qkv_w = gather_cols(qkv_low)
            out_w = gather_rows(exchange(w_out.astype(BF), 0, 1))
            out_w = out_w.reshape(2, tp_size * HD, width // 2)
        else:
            first = z * heads_here * HD

            def whole(w, cols):
                w = lax.all_gather(w.astype(BF), "tp", axis=cols, tiled=True)
                return lax.all_gather(w, ("z", "core"), axis=1 - cols, tiled=True)

            def columns(w):
                w = lax.dynamic_slice(whole(w, 1), (0, first), (width, heads_here * HD))
                return permute(w.T).reshape(heads_here, HD, width).swapaxes(1, 2)

            qkv_w = jnp.concatenate([columns(w_query), columns(w_key), columns(w_value)], axis=2)
            out_w = lax.dynamic_slice(whole(w_out, 0), (first, 0), (heads_here * HD, width))
            out_w = permute(out_w).reshape(heads_here * HD, 2, width // 2).swapaxes(0, 1)
        gate_w = gather_cols(exchange(w_gate.astype(BF), 1, 0))
        up_w = gather_cols(exchange(w_up.astype(BF), 1, 0))
        down_w = gather_rows(exchange(w_down.astype(BF), 0, 1))

        half = HD // 2
        frequency = jnp.power(F32(10000.0), -jnp.arange(half, dtype=F32) / half)
        phase = jnp.arange(length, dtype=jnp.int32).astype(F32)[:, None] * frequency[None, :]
        rot_cos, rot_sin = jnp.cos(phase), jnp.sin(phase)
        cos = jnp.concatenate([rot_cos, rot_cos], axis=1)
        sin = jnp.concatenate([rot_sin, -rot_sin], axis=1)
        t_all = jnp.arange(tp_size, dtype=jnp.int32)[:, None]
        z_all = jnp.asarray(holder, jnp.int32)[z][None, :]
        off_all = (t_all % (tp_size // 2)) * own
        shard_all = 2 * z_all + t_all // (tp_size // 2)
        block_all = jnp.where(off_all < block, shard_all, 2 * shards - 1 - shard_all)
        table = ((block_all * block + off_all % block) // own).reshape(-1)

        def to_heads(x):
            if heads_here == tp_size:
                return lax.all_to_all(x, "tp", split_axis=0, concat_axis=0, tiled=True)
            every = lax.all_gather(x, "tp", axis=0)
            return lax.dynamic_index_in_dim(
                every, tp * heads_here // tp_size, axis=1, keepdims=False
            )

        def to_tokens(x):
            if heads_here == tp_size:
                return lax.all_to_all(x, "tp", split_axis=0, concat_axis=0, tiled=True)
            every = lax.all_gather(x, "tp", axis=0)[:: tp_size // heads_here]
            return lax.dynamic_index_in_dim(every, tp, axis=1, keepdims=False)

        qkv = jnp.einsum("mk,tkn->tmn", xn1, qkv_w, preferred_element_type=F32).astype(BF)
        heads_out, q, k, v = attend(table, to_heads(qkv), cos, sin, own, length)
        mixed = jnp.swapaxes(to_tokens(heads_out), 0, 1).reshape(group, heads_here * HD)
        attn = jnp.einsum("mh,chd->mcd", mixed, out_w, preferred_element_type=F32)
        hres = x_own + scatter_ring(attn.reshape(z_size, own, width))

        scale2 = lax.rsqrt(jnp.mean(hres * hres, axis=-1, keepdims=True) + EPSILON)
        gy = gather_ring(gy_own)
        xn2 = gather_ring((hres * scale2 * gain2).astype(BF))
        dhid = jnp.einsum(
            "mcd,ctfd->tmf",
            gy.reshape(group, 2, width // 2),
            down_w,
            preferred_element_type=F32,
        )
        gate = jnp.einsum("mk,tkn->tmn", xn2, gate_w, preferred_element_type=F32)
        up = jnp.einsum("mk,tkn->tmn", xn2, up_w, preferred_element_type=F32)
        sig = jax.nn.sigmoid(gate)
        hid = (gate * sig * up).astype(BF)
        dgate = (dhid * up * sig * (1.0 + gate * (1.0 - sig))).astype(BF)
        dup = (dhid * gate * sig).astype(BF)
        dxn2 = jnp.einsum("tmn,tkn->mk", dgate, gate_w, preferred_element_type=F32) + jnp.einsum(
            "tmn,tkn->mk", dup, up_w, preferred_element_type=F32
        )
        dxn2 = scatter_ring(dxn2.reshape(z_size, own, width))
        ffn = jnp.einsum("tmf,ctfd->mcd", hid, down_w, preferred_element_type=F32)
        layer_own = hres + scatter_ring(ffn.reshape(z_size, own, width))

        def reduce_cols(part, out_cols):
            part = part.astype(BF).reshape(2 * tp_size, width // 2, part.shape[2])
            part = lax.psum_scatter(part, ("tp", "core"), scatter_dimension=0, tiled=False)
            return exchange(part, 0, 1)

        def reduce_rows(part):
            part = part.astype(BF).reshape((2 * tp_size,) + part.shape[2:])
            part = lax.psum_scatter(part, ("core", "tp"), scatter_dimension=0, tiled=False)
            return exchange(part, 1, 0)

        g_down = reduce_rows(
            jnp.einsum(
                "tmf,mcd->ctfd",
                hid,
                gy.reshape(group, 2, width // 2),
                preferred_element_type=F32,
            )
        ).astype(F32)
        g_gate = reduce_cols(
            jnp.einsum("mk,tmn->tkn", xn2, dgate, preferred_element_type=F32), None
        ).astype(F32)
        g_up = reduce_cols(
            jnp.einsum("mk,tmn->tkn", xn2, dup, preferred_element_type=F32), None
        ).astype(F32)

        gain2_part = jnp.sum(dxn2 * hres * scale2, axis=0)
        e2 = dxn2 * gain2
        dres = (
            gy_own.astype(F32)
            + scale2 * e2
            - hres
            * (scale2 * scale2 * scale2)
            * jnp.mean(e2 * hres, axis=-1, keepdims=True)
        )
        dres_all = gather_ring(dres.astype(BF))
        dres_split = dres_all.reshape(group, 2, width // 2)
        dmix = jnp.einsum("mcd,chd->mh", dres_split, out_w, preferred_element_type=F32).astype(BF)
        dmix = jnp.swapaxes(dmix.reshape(group, heads_here, HD), 0, 1)
        dqkv = to_tokens(attend_back(table, to_heads(dmix), q, k, v, cos, sin, own, length))
        dxn1 = jnp.einsum("tmn,tkn->mk", dqkv, qkv_w, preferred_element_type=F32)
        dxn1 = scatter_ring(dxn1.reshape(z_size, own, width))
        g_out = jnp.einsum("mh,mcd->chd", mixed, dres_split, preferred_element_type=F32)
        g_qkv = jnp.einsum("mk,tmn->tkn", xn1, dqkv, preferred_element_type=F32)
        if plain:
            g_out = reduce_rows(g_out.reshape(2, tp_size, HD, width // 2)).astype(F32)
            g_qkv = reduce_cols(g_qkv, None).reshape(k_rows, z_size, 3, HD)
            g_query, g_key, g_value = (
                g_qkv[:, :, i].reshape(k_rows, z_size * HD).astype(F32) for i in range(3)
            )
        else:

            def spread(part, cols):
                if cols:
                    out = lax.dynamic_update_slice(
                        jnp.zeros((width, heads * HD), BF), part.astype(BF), (0, first)
                    )
                else:
                    out = lax.dynamic_update_slice(
                        jnp.zeros((heads * HD, width), BF), part.astype(BF), (first, 0)
                    )
                out = lax.psum_scatter(
                    out, ("z", "core"), scatter_dimension=0 if cols else 1, tiled=True
                )
                return lax.psum_scatter(
                    out, "tp", scatter_dimension=1 if cols else 0, tiled=True
                ).astype(F32)

            def back_columns(i):
                part = g_qkv[:, :, i * HD : (i + 1) * HD].swapaxes(1, 2)
                return spread(restore(part).reshape(heads_here * HD, width).T, True)

            g_query, g_key, g_value = back_columns(0), back_columns(1), back_columns(2)
            g_out = jnp.swapaxes(g_out, 0, 1).reshape(heads_here * HD, width)
            g_out = spread(restore(g_out), False)
        gain1_part = jnp.sum(dxn1 * x_own * scale1, axis=0)
        e1 = dxn1 * gain1
        in_own = (
            dres
            + scale1 * e1
            - x_own
            * (scale1 * scale1 * scale1)
            * jnp.mean(e1 * x_own, axis=-1, keepdims=True)
        )

        gains = restore(jnp.stack([gain1_part, gain2_part])).reshape(2, shards, 1, k_rows)
        gains = jnp.broadcast_to(gains, (2, shards, tp_size, k_rows)).reshape(
            2, shards * tp_size, k_rows
        )
        gains = lax.all_to_all(
            gains, ("z", "core", "tp"), split_axis=1, concat_axis=1, tiled=True
        )
        gains = jnp.sum(gains, axis=1)

        def spread_rows(x):
            every = gather_tp(restore(x.astype(BF))).reshape(2, rows // 2, width)
            kept = lax.dynamic_index_in_dim(every, core, axis=0, keepdims=False)
            sent = lax.dynamic_index_in_dim(every, 1 - core, axis=0, keepdims=False)
            came = lax.ppermute(sent, "core", swap_core)
            first_seq = jnp.where(core == 0, kept, came)
            second_seq = jnp.where(core == 0, came, kept)
            blocks = jnp.concatenate([first_seq, second_seq]).reshape(4, block, width)
            return jnp.take(blocks, rank, axis=0, mode="clip").reshape(rows, width)

        layer_out = spread_rows(layer_own)
        in_grad = spread_rows(in_own).astype(F32)
        return (
            layer_out,
            in_grad,
            gains[0],
            gains[1],
            g_query,
            g_key,
            g_value,
            g_out,
            g_gate,
            g_up,
            g_down,
        )

    return on_device


def solution(mesh):
    tp_size = mesh.shape["tp"]
    z_size = mesh.shape["seq"] // 2
    split = Mesh(mesh.devices.reshape(z_size, 2, tp_size), ("z", "core", "tp"))
    seq = ("z", "core")
    in_specs = (
        P(seq, None),
        P(seq),
        P(seq),
        P(),
        P(),
        P(seq, "tp"),
        P(seq, "tp"),
        P(seq, "tp"),
        P("tp", seq),
        P(seq, "tp"),
        P(seq, "tp"),
        P("tp", seq),
        P(seq, None),
    )
    out_specs = (
        P(seq, None),
        P(seq, None),
        P(seq),
        P(seq),
        P(seq, "tp"),
        P(seq, "tp"),
        P(seq, "tp"),
        P("tp", seq),
        P(seq, "tp"),
        P(seq, "tp"),
        P("tp", seq),
    )
    return jax.shard_map(
        build(z_size, tp_size), mesh=split, in_specs=in_specs, out_specs=out_specs, check_vma=False
    )
```

```python
import functools
import math

import jax
import jax.numpy as jnp
from jax import lax
from jax.experimental import pallas as pl
from jax.experimental.pallas import tpu as pltpu
from jax.sharding import Mesh
from jax.sharding import PartitionSpec as P

HD = 128
EPSILON = 1e-06
LOG2E = 1.4426950408889634
BF = jnp.bfloat16
F32 = jnp.float32
SHARE = 1
VM = pl.BlockSpec(memory_space=pltpu.VMEM)
SM = pl.BlockSpec(memory_space=pltpu.SMEM)


def dot_nt(left, right):
    return lax.dot_general(left, right, (((1,), (1,)), ((), ())), preferred_element_type=F32)


def dot_nn(left, right):
    return lax.dot_general(left, right, (((1,), (0,)), ((), ())), preferred_element_type=F32)


def dot_tn(left, right):
    return lax.dot_general(left, right, (((0,), (0,)), ((), ())), preferred_element_type=F32)


def call(body, grid, in_specs, out_specs, out_shape, scratch, flops, bytes_accessed, name, deps):
    known = len(in_specs)
    skip = len(deps)

    def run(*refs):
        body(*refs[:known], *refs[known + skip :])

    made = pl.pallas_call(
        run,
        grid=grid,
        in_specs=list(in_specs) + [pl.BlockSpec(memory_space=pl.ANY)] * skip,
        out_specs=out_specs,
        out_shape=out_shape,
        scratch_shapes=scratch,
        compiler_params=pltpu.CompilerParams(
            vmem_limit_bytes=48 << 20,
            dimension_semantics=("arbitrary",) * len(grid),
        ),
        cost_estimate=pl.CostEstimate(
            flops=flops // SHARE, transcendentals=0, bytes_accessed=bytes_accessed // SHARE
        ),
        name=name,
    )
    return lambda *args: made(*args, *deps)


def shape(dims, dtype):
    return jax.ShapeDtypeStruct(dims, dtype)


def attend_kernel(tab_ref, *refs, groups, chunk, tile, bias2):
    qkv_refs, (cos_ref, sin_ref) = refs[:groups], refs[groups : groups + 2]
    out_refs = refs[groups + 2 : 2 * groups + 2]
    q_ref, k_ref, v_ref, acc_ref = refs[2 * groups + 2 :]
    rows = qkv_refs[0].shape[0]
    per_group = rows // chunk
    length = groups * rows
    for j in range(length // chunk):
        g, s = divmod(j, per_group)
        here = pl.ds(s * chunk, chunk)
        there = pl.ds(pl.multiple_of(tab_ref[j] * chunk, chunk), chunk)
        cos = cos_ref[there, :]
        sin = sin_ref[there, :]
        q = qkv_refs[g][here, 0:HD].astype(F32)
        k = qkv_refs[g][here, HD : 2 * HD].astype(F32)
        q_ref[there, :] = (q * cos - pltpu.roll(q, HD // 2, 1) * sin).astype(BF)
        k_ref[there, :] = (k * cos - pltpu.roll(k, HD // 2, 1) * sin).astype(BF)
        v_ref[there, :] = qkv_refs[g][here, 2 * HD : 3 * HD]
    slope = -LOG2E / math.sqrt(HD)

    def part(i, j, masked):
        qs = q_ref[pl.ds(i * tile, tile), :]
        ks = k_ref[pl.ds(j * tile, tile), :]
        vs = v_ref[pl.ds(j * tile, tile), :]
        sig = 1.0 / (1.0 + jnp.exp2(dot_nt(qs, ks) * slope + bias2))
        if masked:
            row = lax.broadcasted_iota(jnp.int32, (tile, tile), 0)
            col = lax.broadcasted_iota(jnp.int32, (tile, tile), 1)
            sig = jnp.where(col <= row, sig, 0.0)
        return dot_nn(sig.astype(BF), vs)

    def query(i, carry):
        own = pl.ds(pl.multiple_of(i * tile, tile), tile)
        acc_ref[own, :] = part(i, i, True)

        def key(j, carry):
            acc_ref[own, :] += part(i, j, False)
            return carry

        lax.fori_loop(0, i, key, 0)
        return carry

    lax.fori_loop(0, length // tile, query, 0)
    for j in range(length // chunk):
        g, s = divmod(j, per_group)
        there = pl.ds(pl.multiple_of(tab_ref[j] * chunk, chunk), chunk)
        out_refs[g][pl.ds(s * chunk, chunk), :] = acc_ref[there, :].astype(BF)


def attend_back_kernel(tab_ref, *refs, groups, chunk, tile, bias2):
    grad_refs = refs[:groups]
    q_ref, k_ref, v_ref, cos_ref, sin_ref = refs[groups : groups + 5]
    out_refs = refs[groups + 5 : 2 * groups + 5]
    do_ref, dq_ref, dk_ref, dv_ref = refs[2 * groups + 5 :]
    rows = grad_refs[0].shape[0]
    per_group = rows // chunk
    length = groups * rows
    for j in range(length // chunk):
        g, s = divmod(j, per_group)
        there = pl.ds(pl.multiple_of(tab_ref[j] * chunk, chunk), chunk)
        do_ref[there, :] = grad_refs[g][pl.ds(s * chunk, chunk), :]
    slope = -LOG2E / math.sqrt(HD)
    scale = 1.0 / math.sqrt(HD)

    def part(i, j, masked):
        qi = pl.ds(pl.multiple_of(i * tile, tile), tile)
        kj = pl.ds(pl.multiple_of(j * tile, tile), tile)
        qs, ks, vs, dos = q_ref[qi, :], k_ref[kj, :], v_ref[kj, :], do_ref[qi, :]
        sig = 1.0 / (1.0 + jnp.exp2(dot_nt(ks, qs) * slope + bias2))
        dsc = dot_nt(vs, dos) * sig * (1.0 - sig)
        if masked:
            row = lax.broadcasted_iota(jnp.int32, (tile, tile), 0)
            col = lax.broadcasted_iota(jnp.int32, (tile, tile), 1)
            sig = jnp.where(row <= col, sig, 0.0)
            dsc = jnp.where(row <= col, dsc, 0.0)
        dsc = dsc.astype(BF)
        dv = dot_nn(sig.astype(BF), dos)
        dk = dot_nn(dsc, qs)
        dq = dot_tn(dsc, ks)
        if masked:
            dq_ref[qi, :] = dq
            dk_ref[kj, :] = dk
            dv_ref[kj, :] = dv
        else:
            dq_ref[qi, :] += dq
            dk_ref[kj, :] += dk
            dv_ref[kj, :] += dv

    def query(i, carry):
        part(i, i, True)

        def key(j, carry):
            part(i, j, False)
            return carry

        lax.fori_loop(0, i, key, 0)
        return carry

    lax.fori_loop(0, length // tile, query, 0)
    for j in range(length // chunk):
        g, s = divmod(j, per_group)
        here = pl.ds(s * chunk, chunk)
        there = pl.ds(pl.multiple_of(tab_ref[j] * chunk, chunk), chunk)
        cos = cos_ref[there, :] * scale
        sin = sin_ref[there, :] * scale
        dq = dq_ref[there, :]
        dk = dk_ref[there, :]
        out_refs[g][here, 0:HD] = (dq * cos + pltpu.roll(dq, HD // 2, 1) * sin).astype(BF)
        out_refs[g][here, HD : 2 * HD] = (dk * cos + pltpu.roll(dk, HD // 2, 1) * sin).astype(BF)
        out_refs[g][here, 2 * HD : 3 * HD] = dv_ref[there, :].astype(BF)


def attend(table, qkv, cos, sin, chunk, length):
    groups = len(qkv)
    rows = qkv[0].shape[0]
    tile = min(512, length)
    full = shape((length, HD), BF)
    out = pl.pallas_call(
        functools.partial(
            attend_kernel, groups=groups, chunk=chunk, tile=tile, bias2=math.log2(length)
        ),
        out_shape=(shape((rows, HD), BF),) * groups + (full,) * 3,
        in_specs=[SM] + [VM] * (groups + 2),
        out_specs=(VM,) * (groups + 3),
        scratch_shapes=[pltpu.VMEM((length, HD), F32)],
        compiler_params=pltpu.CompilerParams(vmem_limit_bytes=40 << 20),
        cost_estimate=pl.CostEstimate(
            flops=2 * length * length * HD * 2,
            transcendentals=length * length * 2,
            bytes_accessed=length * HD * 24 * 2,
        ),
        name="attend",
    )(table, *qkv, cos, sin)
    return out[:groups], out[groups:]


def attend_back(table, grad, saved, cos, sin, chunk, length, deps):
    groups = len(grad)
    rows = grad[0].shape[0]
    tile = min(512, length)
    known = groups + 6
    kernel = functools.partial(
        attend_back_kernel, groups=groups, chunk=chunk, tile=tile, bias2=math.log2(length)
    )

    def body(*refs):
        kernel(*refs[:known], *refs[known + len(deps) :])

    return pl.pallas_call(
        body,
        out_shape=(shape((rows, 3 * HD), BF),) * groups,
        in_specs=[SM] + [VM] * (groups + 5) + [pl.BlockSpec(memory_space=pl.ANY)] * len(deps),
        out_specs=(VM,) * groups,
        scratch_shapes=[pltpu.VMEM((length, HD), BF)] + [pltpu.VMEM((length, HD), F32)] * 3,
        compiler_params=pltpu.CompilerParams(vmem_limit_bytes=40 << 20),
        cost_estimate=pl.CostEstimate(
            flops=5 * length * length * HD * 2,
            transcendentals=length * length * 2,
            bytes_accessed=length * HD * 24 * 2,
        ),
        name="attend_back",
    )(table, *grad, *saved, cos, sin, *deps)


def ring_shapes(own, slots, half):
    return (
        (shape((2, own, half), F32),)
        + (shape((2, own, half), BF),) * (slots - 2)
        + (shape((2, own // 2, half), BF),) * 2
    )


def ring_store(refs, h, rows, own):
    refs[0][h] = rows[:own]
    at = own
    for ref in refs[1:]:
        n = ref.shape[1]
        ref[h] = rows[at : at + n].astype(BF)
        at += n


def project(x, w0, w1, at, n, name, deps=()):
    _, g, half = x.shape
    t = w0.shape[0]

    def body(x_ref, a_ref, b_ref, *outs):
        k = pl.program_id(0)
        rows = (dot_nn(x_ref[0], a_ref[0]) + dot_nn(x_ref[1], b_ref[0])).astype(BF)
        for i, out_ref in enumerate(outs):

            @pl.when(k == i)
            def _():
                out_ref[...] = rows

    w_spec = pl.BlockSpec((1, half, n), lambda k: (k, 0, at // n))
    return call(
        body,
        (t,),
        [pl.BlockSpec((2, g, half), lambda k: (0, 0, 0)), w_spec, w_spec],
        (pl.BlockSpec((g, n), lambda k: (0, 0)),) * t,
        (shape((g, n), BF),) * t,
        [],
        4 * g * half * t * n,
        4 * half * t * n + 4 * g * half + 2 * g * t * n,
        name,
        deps,
    )(x, w0, w1)


def mm_back(parts, w0, w1, at, own, name, deps=()):
    t, g, n = parts.shape
    half = w0.shape[1]
    th = min(half, 256)

    def body(p_ref, a_ref, b_ref, *outs):
        for h, w_ref in enumerate((a_ref, b_ref)):
            acc = dot_nt(p_ref[0], w_ref[0])
            for k in range(1, t):
                acc += dot_nt(p_ref[k], w_ref[k])
            ring_store(outs, h, acc, own)

    w_spec = pl.BlockSpec((t, th, n), lambda j: (0, j, at // n))
    shapes = ring_shapes(own, g // own, half)
    return call(
        body,
        (half // th,),
        [pl.BlockSpec((t, g, n), lambda j: (0, 0, 0)), w_spec, w_spec],
        tuple(pl.BlockSpec(o.shape[:2] + (th,), lambda j: (0, 0, j)) for o in shapes),
        shapes,
        [],
        4 * g * half * t * n,
        4 * half * t * n + 2 * g * t * n + 4 * g * half,
        name,
        deps,
    )(parts, w0, w1)


def gate_up(x, w0, w1, deps=()):
    _, g, half = x.shape
    t, _, n = w0.shape
    n //= 2
    tn = min(n, 256)
    steps = n // tn

    def body(x_ref, g0_ref, g1_ref, u0_ref, u1_ref, hid_ref, to_gate_ref, to_up_ref):
        gate = dot_nn(x_ref[0], g0_ref[0]) + dot_nn(x_ref[1], g1_ref[0])
        up = dot_nn(x_ref[0], u0_ref[0]) + dot_nn(x_ref[1], u1_ref[0])
        sig = 1.0 / (1.0 + jnp.exp(-gate))
        act = gate * sig
        hid_ref[0] = (act * up).astype(BF)
        to_gate_ref[0] = (up * (sig * (1.0 + gate * (1.0 - sig)))).astype(BF)
        to_up_ref[0] = act.astype(BF)

    g_spec = pl.BlockSpec((1, half, tn), lambda k, j: (k, 0, j))
    u_spec = pl.BlockSpec((1, half, tn), lambda k, j: (k, 0, j + steps))
    f_spec = pl.BlockSpec((1, g, tn), lambda k, j: (k, 0, j))
    return call(
        body,
        (t, steps),
        [pl.BlockSpec((2, g, half), lambda k, j: (0, 0, 0)), g_spec, g_spec, u_spec, u_spec],
        (f_spec,) * 3,
        (shape((t, g, n), BF),) * 3,
        [],
        1000,
        1000,
        "gate_up",
        deps,
    )(x, w0, w1, w0, w1)


def feed_back(gy, to_gate, to_up, w0, w1, d0, d1, own, deps=()):
    _, g, half = gy.shape
    t, _, n = d0.shape
    tn = min(n, 256)
    steps = n // tn

    def body(y_ref, a_ref, b_ref, g0_ref, g1_ref, u0_ref, u1_ref, d0_ref, d1_ref, *rest):
        out_ref, outs, acc_ref = rest[0], rest[1:-1], rest[-1]
        k, j = pl.program_id(0), pl.program_id(1)
        dh = dot_nn(y_ref[0], d0_ref[0]) + dot_nn(y_ref[1], d1_ref[0])
        dgate = (dh * a_ref[0].astype(F32)).astype(BF)
        dup = (dh * b_ref[0].astype(F32)).astype(BF)
        out_ref[0, 0] = dgate
        out_ref[0, 1] = dup
        first = jnp.logical_and(k == 0, j == 0)
        for h, (p_ref, q_ref) in enumerate(((g0_ref, u0_ref), (g1_ref, u1_ref))):
            part = dot_nt(dgate, p_ref[0]) + dot_nt(dup, q_ref[0])

            @pl.when(first)
            def _():
                acc_ref[h] = part

            @pl.when(jnp.logical_not(first))
            def _():
                acc_ref[h] += part

        @pl.when(jnp.logical_and(k == t - 1, j == steps - 1))
        def _():
            for h in range(2):
                ring_store(outs, h, acc_ref[h], own)

    g_spec = pl.BlockSpec((1, half, tn), lambda k, j: (k, 0, j))
    u_spec = pl.BlockSpec((1, half, tn), lambda k, j: (k, 0, j + steps))
    f_spec = pl.BlockSpec((1, g, tn), lambda k, j: (k, 0, j))
    shapes = ring_shapes(own, g // own, half)
    return call(
        body,
        (t, steps),
        [pl.BlockSpec((2, g, half), lambda k, j: (0, 0, 0)), f_spec, f_spec]
        + [g_spec, g_spec, u_spec, u_spec, g_spec, g_spec],
        (pl.BlockSpec((1, 2, g, tn), lambda k, j: (k, 0, 0, j)),)
        + tuple(pl.BlockSpec(o.shape, lambda k, j: (0, 0, 0)) for o in shapes),
        (shape((t, 2, g, n), BF),) + shapes,
        [pltpu.VMEM((2, g, half), F32)],
        12 * g * half * t * n,
        12 * half * t * n + 8 * g * t * n + 8 * g * half,
        "feed_back",
        deps,
    )(gy, to_gate, to_up, w0, w1, w0, w1, d0, d1)


def weight_grad(place, left, left_peer, right, right_peer, name, deps=()):
    g, half = left.shape
    t, m, _, n = right.shape
    tn = n if n % 256 else 256

    def body(s_ref, a_ref, b_ref, c_ref, d_ref, out_ref):
        del s_ref
        out_ref[0] = (
            dot_tn(a_ref[...], c_ref[0, 0]) + dot_tn(b_ref[...], d_ref[0, 0])
        ).astype(BF)

    l_spec = pl.BlockSpec((g, half), lambda k, i, j, s: (0, 0))
    r_spec = pl.BlockSpec((1, 1, g, tn), lambda k, i, j, s: (k, i, 0, j))
    return placed_call(
        body,
        (t, m, n // tn),
        [l_spec, l_spec, r_spec, r_spec],
        pl.BlockSpec((1, half, tn), lambda k, i, j, s: (k ^ s[0], 0, i * (n // tn) + j)),
        shape((t, half, m * n), BF),
        4 * g * half * t * m * n,
        4 * g * t * m * n + 4 * g * half + 2 * half * t * m * n,
        name,
        deps,
    )(place, left, left_peer, right, right_peer)


def weight_grad_heads(xn, xn_peer, dqkv, dqkv_peer, dres, dres_peer, mixed, mixed_peer, deps=()):
    g, half = xn.shape
    t, _, n = dqkv.shape
    m = mixed.shape[2]

    def body(a_ref, b_ref, c_ref, d_ref, e_ref, f_ref, g_ref, h_ref, out_ref):
        out_ref[0, :, :n] = (
            dot_tn(a_ref[...], c_ref[0]) + dot_tn(b_ref[...], d_ref[0])
        ).astype(BF)
        out_ref[0, :, n:] = (
            dot_tn(e_ref[...], g_ref[0]) + dot_tn(f_ref[...], h_ref[0])
        ).astype(BF)

    l_spec = pl.BlockSpec((g, half), lambda k: (0, 0))
    n_spec = pl.BlockSpec((1, g, n), lambda k: (k, 0, 0))
    m_spec = pl.BlockSpec((1, g, m), lambda k: (k, 0, 0))
    return call(
        body,
        (t,),
        [l_spec, l_spec, n_spec, n_spec, l_spec, l_spec, m_spec, m_spec],
        pl.BlockSpec((1, half, n + m), lambda k: (k, 0, 0)),
        shape((t, half, n + m), BF),
        [],
        4 * g * half * t * (n + m),
        4 * g * t * (n + m) + 8 * g * half + 2 * half * t * (n + m),
        "g_heads",
        deps,
    )(xn, xn_peer, dqkv, dqkv_peer, dres, dres_peer, mixed, mixed_peer)


def placed_call(body, grid, in_specs, out_specs, out_shape, flops, bytes_accessed, name, deps):
    known = len(in_specs) + 1
    skip = len(deps)

    def run(*refs):
        body(*refs[:known], *refs[known + skip :])

    made = pl.pallas_call(
        run,
        grid_spec=pltpu.PrefetchScalarGridSpec(
            num_scalar_prefetch=1,
            grid=grid,
            in_specs=list(in_specs) + [pl.BlockSpec(memory_space=pl.ANY)] * skip,
            out_specs=out_specs,
        ),
        out_shape=out_shape,
        compiler_params=pltpu.CompilerParams(
            vmem_limit_bytes=48 << 20,
            dimension_semantics=("arbitrary",) * len(grid),
        ),
        cost_estimate=pl.CostEstimate(
            flops=flops // SHARE, transcendentals=0, bytes_accessed=bytes_accessed // SHARE
        ),
        name=name,
    )
    return lambda *args: made(*args, *deps)


def pack_weights(columns, rows, parts, apart, name, deps=()):
    k, n = columns[0].shape
    n //= parts
    count = len(columns)

    def body(*refs):
        out_ref = refs[count + 1]
        for i, ref in enumerate(refs[:count]):
            out_ref[0, :, i * n : (i + 1) * n] = ref[...].astype(BF)
        turned = jnp.transpose(refs[count][...]).astype(BF)
        if apart:
            refs[-1][0] = turned
        else:
            out_ref[0, :, count * n :] = turned

    widths = (count * n, n) if apart else ((count + 1) * n,)
    return call(
        body,
        (parts,),
        [pl.BlockSpec((k, n), lambda p: (0, p))] * count + [pl.BlockSpec((n, k), lambda p: (p, 0))],
        tuple(pl.BlockSpec((1, k, w), lambda p: (p, 0, 0)) for w in widths),
        tuple(shape((parts, k, w), BF) for w in widths),
        [],
        1000,
        1000,
        name,
        deps,
    )(*columns, rows)


def unpack_columns(parts, count, transposed, name):
    z, k, n = parts.shape
    n //= count

    def body(in_ref, *outs):
        for i, ref in enumerate(outs):
            part = in_ref[0, :, i * n : (i + 1) * n].astype(F32)
            ref[...] = jnp.transpose(part) if transposed and i == count - 1 else part

    straight = (pl.BlockSpec((k, n), lambda p: (0, p)), shape((k, z * n), F32))
    turned = (pl.BlockSpec((n, k), lambda p: (p, 0)), shape((z * n, k), F32))
    outs = [straight] * (count - 1) + [turned if transposed else straight]
    return call(
        body,
        (z,),
        [pl.BlockSpec((1, k, count * n), lambda p: (p, 0, 0))],
        tuple(o[0] for o in outs),
        tuple(o[1] for o in outs),
        [],
        1000,
        1000,
        name,
        (),
    )(parts)


def place_blocks(index, sources, dtype):
    counts = [x.shape[0] for x in sources]
    rows, width = sources[0].shape[1:]
    blocks = index.shape[0]

    def body(s_ref, *refs):
        out_ref = refs[-1]
        wanted = s_ref[pl.program_id(0)]
        at = 0
        for n, ref in zip(counts, refs):
            for i in range(n):

                @pl.when(wanted == at)
                def _():
                    out_ref[0] = ref[i].astype(dtype)

                at += 1

    return placed_call(
        body,
        (blocks,),
        [pl.BlockSpec(x.shape, lambda b, s: (0, 0, 0)) for x in sources],
        pl.BlockSpec((1, rows, width), lambda b, s: (b, 0, 0)),
        shape((blocks, rows, width), dtype),
        0,
        12 * blocks * rows * width,
        "place",
        (),
    )(index, *sources)


def after(x, *deps):
    for d in deps:
        corner = lax.slice(d, [n - 1 for n in d.shape], d.shape).reshape(())
        x = x + (corner.astype(F32) * 0.0).astype(x.dtype)
    return x


def tie(x, *deps):
    anywhere = pl.BlockSpec(memory_space=pl.ANY)
    return pl.pallas_call(
        lambda *refs: None,
        in_specs=[anywhere] * (1 + len(deps)),
        out_specs=anywhere,
        out_shape=shape(x.shape, x.dtype),
        input_output_aliases={0: 0},
        name="tie",
    )(x, *deps)


def build(z_size, tp_size):
    shards = 2 * z_size
    ring = [0] + list(range(1, z_size, 2)) + list(range(z_size - 2, 0, -2))
    place = [ring.index(z) for z in range(z_size)]
    forward = [(ring[i], ring[(i + 1) % z_size]) for i in range(z_size)]
    backward = [(b, a) for a, b in forward]
    half_ring = z_size // 2
    offsets = [0]
    for k in range(1, half_ring):
        offsets += [-k, k]
    offsets += [half_ring]
    holder = [[ring[(place[z] + off) % z_size] for off in offsets] for z in range(z_size)]
    swap_core = [(0, 1), (1, 0)]

    def hop(x, bit):
        return lax.ppermute(x, "tp", [(t, t ^ bit) for t in range(tp_size)])

    def swap(x):
        return lax.ppermute(x, "core", swap_core)

    def ring_first(x):
        chunks = [x]
        ahead = back = x
        for _ in range(1, half_ring):
            ahead = lax.ppermute(ahead, "z", forward)
            back = lax.ppermute(back, "z", backward)
            chunks += [ahead, back]
        return chunks

    def ring_last(chunks, *deps):
        ahead, back = chunks[-2:]
        mid = ahead.shape[1] // 2
        one = lax.ppermute(after(ahead[:, :mid], back, *deps), "z", forward)
        two = lax.ppermute(after(back[:, mid:], ahead, *deps), "z", backward)
        return chunks + [one, two]

    def gather_ring(x, *deps):
        return ring_last(ring_first(x), *deps)

    def join_rows(chunks):
        return jnp.concatenate(chunks, axis=1)

    def scatter_first(parts):
        return (
            lax.ppermute(parts[-2], "z", forward),
            lax.ppermute(parts[-1], "z", backward),
        )

    def scatter_last(parts, came, *deps):
        one, two = came
        mid = parts[0].shape[1] // 2
        for k in range(half_ring - 1, 0, -1):
            fwd, bwd = parts[offsets.index(k)], parts[offsets.index(-k)]
            if k == half_ring - 1:
                fwd = jnp.concatenate([fwd[:, :mid] + one, fwd[:, mid:]], axis=1)
                bwd = jnp.concatenate([bwd[:, :mid], bwd[:, mid:] + two], axis=1)
            else:
                fwd = fwd + one
                bwd = bwd + two
            one = lax.ppermute(fwd, "z", forward)
            two = lax.ppermute(bwd, "z", backward)
        return after(parts[0] + one.astype(F32) + two.astype(F32), *deps)

    def scatter_ring(parts, *deps):
        return scatter_last(parts, scatter_first(parts), *deps)

    def tick(x):
        corner = lax.slice(x.reshape((-1,) + x.shape[-1:]), (0, 0), (16, 128))
        return swap(corner.astype(BF))

    def near_tp(x):
        return (hop(x, 1), hop(x, 2)) if tp_size == 4 else ()

    def far_tp(x, near, *deps):
        if tp_size != 4:
            return ()
        mid = x.shape[0] // 2
        return (
            hop(after(near[1][:mid], *deps), 1),
            hop(after(near[0][mid:], *deps), 2),
        )

    def stack_tp(x, near, far, *deps):
        if tp_size == 4:
            return after(jnp.stack([x, *near, jnp.concatenate(far, axis=0)]), *deps)
        held = x[None]
        bit = 1
        while bit < tp_size:
            held = jnp.concatenate([held, hop(held, bit)], axis=0)
            bit *= 2
        return held

    def gather_tp(x):
        near = near_tp(x)
        return stack_tp(x, near, far_tp(x, near))

    def scatter_tp_first(part):
        if tp_size == 4:
            mid = part.shape[1] // 2
            top, low = part[:, :mid], part[:, mid:]
            return hop(jnp.stack([top[1], top[3]]), 1), hop(jnp.stack([low[2], low[3]]), 2)
        return ()

    def scatter_tp_last(part, came):
        if tp_size == 4:
            over_x, over_y = came
            mid = part.shape[1] // 2
            top, low = part[:, :mid], part[:, mid:]
            top2 = hop(top[2] + over_x[1], 2)
            low1 = hop(low[1] + over_y[1], 1)
            return jnp.concatenate([top[0] + over_x[0] + top2, low[0] + over_y[0] + low1], axis=0)
        bit = tp_size // 2
        while bit:
            part = part[:bit] + hop(part[bit:], bit)
            bit //= 2
        return part[0]

    def to_z(x):
        return lax.all_to_all(x, "z", split_axis=0, concat_axis=0, tiled=True)

    def on_device(
        layer_in,
        positions,
        seq_ids,
        norm1_gain,
        norm2_gain,
        w_query,
        w_key,
        w_value,
        w_out,
        w_gate,
        w_up,
        w_down,
        out_grad,
    ):
        z, core, tp = lax.axis_index("z"), lax.axis_index("core"), lax.axis_index("tp")
        rows, width = layer_in.shape
        half = width // 2
        block = rows // 4
        own = rows // tp_size
        group = own * z_size
        length = rows * shards // 2
        k_rows = width // shards
        heads = w_query.shape[1] * tp_size // HD
        heads_here = heads // z_size
        plain = w_query.shape[1] == z_size * HD and heads_here == tp_size
        flipped = core == 1

        def split(x):
            lead = x.shape[:-1]
            x = x.reshape(lead + (z_size, 2, k_rows))
            even, odd = x[..., 0, :].reshape(lead + (half,)), x[..., 1, :].reshape(lead + (half,))
            return jnp.stack([jnp.where(flipped, odd, even), jnp.where(flipped, even, odd)])

        def join(x):
            lead = x.shape[1:-1]
            even, odd = jnp.where(flipped, x[1], x[0]), jnp.where(flipped, x[0], x[1])
            even = even.reshape(lead + (z_size, 1, k_rows))
            odd = odd.reshape(lead + (z_size, 1, k_rows))
            return jnp.concatenate([even, odd], axis=-2).reshape(lead + (width,))

        sound = positions[0] >= 0

        def stage(run):
            outs = jax.eval_shape(run)
            blank = lambda: jax.tree.map(lambda o: jnp.zeros(o.shape, o.dtype), outs)
            return lax.cond(sound, run, blank)

        key = seq_ids.reshape(4, block)[:, 0] * (4 * length) + positions.reshape(4, block)[:, 0]
        rank = jnp.sum((key[None, :] < key[:, None]).astype(jnp.int32), axis=1)
        source_core = tp // (tp_size // 2)
        offset = (tp % (tp_size // 2)) * own

        def piece(x, seq):
            wanted = 2 * seq + offset // block
            start = jnp.sum(jnp.where(rank == wanted, jnp.arange(4, dtype=jnp.int32), 0)) * block
            return lax.dynamic_slice(x, (start + offset % block, 0), (own, width))

        def take_own(x):
            return split(jnp.where(core == source_core, piece(x, core), swap(piece(x, 1 - core))))

        x_own = take_own(layer_in).astype(F32)
        gy_own = take_own(out_grad)
        gain1 = split(norm1_gain)[:, None]
        gain2 = split(norm2_gain)[:, None]
        scale1 = lax.rsqrt(jnp.mean(x_own * x_own, axis=(0, 2), keepdims=True) + EPSILON)
        xn1_own = x_own * scale1 * gain1

        quarter = HD // 2
        frequency = jnp.power(F32(10000.0), -jnp.arange(quarter, dtype=F32) / quarter)
        phase = jnp.arange(length, dtype=jnp.int32).astype(F32)[:, None] * frequency[None, :]

        def rotations(*deps):
            turned = after(phase, *deps)
            rot_cos, rot_sin = jnp.cos(turned), jnp.sin(turned)
            cos = jnp.concatenate([rot_cos, rot_cos], axis=1)
            return cos, jnp.concatenate([rot_sin, -rot_sin], axis=1)

        def exchange(w):
            return to_z(w).reshape(half, w.shape[2])

        if plain:
            (low,) = pack_weights(
                (w_query, w_key, w_value), w_out, z_size, False, "pack_heads"
            )
            low = exchange(low)
            xn1_low = after(xn1_own, low).astype(BF)

            def begin():
                chunks = ring_first(xn1_low)
                near = near_tp(low)
                started = tick(low)
                turns = rotations(started)
                far = far_tp(low, near, *chunks[1:3], turns[0])
                ffn_low = pack_weights(
                    (w_gate, w_up), w_down, z_size, True, "pack_ffn", (tick(chunks[-1]),)
                )
                chunks = ring_last(chunks)
                full = stack_tp(low, near, far, *chunks[-2:])
                return join_rows(chunks), (full, swap(full)), turns, ffn_low

            xn1, head_w, (cos, sin), ffn_low = stage(begin)
        else:
            at_head = z * heads_here * HD

            def columns(w):
                w = lax.all_gather(w.astype(BF), "tp", axis=1, tiled=True)
                w = lax.all_gather(w, ("z", "core"), axis=0, tiled=True)
                w = lax.dynamic_slice(w, (0, at_head), (width, heads_here * HD))
                return jnp.swapaxes(split(w.T).reshape(2, heads_here, HD, half), 2, 3)

            low = [columns(w) for w in (w_query, w_key, w_value, w_out.T)]
            low = jnp.concatenate(low, axis=3)
            head_w = (low[0], low[1])
            xn1 = join_rows(gather_ring(xn1_own.astype(BF)))
            cos, sin = rotations()
            ffn_low = pack_weights((w_gate, w_up), w_down, z_size, True, "pack_ffn")
        gate_up_one = exchange(ffn_low[0])

        t_all = jnp.arange(tp_size, dtype=jnp.int32)[:, None]
        if plain:
            t_all = jnp.bitwise_xor(t_all, tp)
        z_all = jnp.asarray(holder, jnp.int32)[z][None, :]
        off_all = (t_all % (tp_size // 2)) * own
        shard_all = 2 * z_all + t_all // (tp_size // 2)
        block_all = jnp.where(off_all < block, shard_all, 2 * shards - 1 - shard_all)
        table = ((block_all * block + off_all % block) // own).reshape(-1)

        def to_heads(x):
            if plain:
                return [x[0]] + [hop(x[k], k) for k in range(1, tp_size)]
            every = lax.all_gather(jnp.stack(x), "tp", axis=0)
            every = lax.dynamic_index_in_dim(
                every, tp * heads_here // tp_size, axis=1, keepdims=False
            )
            return [every[k] for k in range(tp_size)]

        def to_tokens(x):
            if plain:
                return jnp.stack([x[0]] + [hop(x[k], k) for k in range(1, tp_size)])
            every = lax.all_gather(jnp.stack(x), "tp", axis=0)[:: tp_size // heads_here]
            return lax.dynamic_index_in_dim(every, tp, axis=1, keepdims=False)

        qkv = project(xn1, *head_w, 0, 3 * HD, "qkv")
        heads_out, saved = attend(table, to_heads(qkv), cos, sin, own, length)
        mixed = to_tokens(heads_out)
        attn = mm_back(mixed, *head_w, 3 * HD, own, "attn_out")

        def first():
            return x_own + scatter_ring(attn), near_tp(gate_up_one)

        hres, gate_up_near = stage(first)
        down_one = exchange(tie(ffn_low[1], hres))

        scale2 = lax.rsqrt(jnp.mean(hres * hres, axis=(0, 2), keepdims=True) + EPSILON)
        xn2_own = (hres * scale2 * gain2).astype(BF)

        def second():
            chunks = ring_first(xn2_own)
            far = far_tp(gate_up_one, gate_up_near, tick(xn2_own))
            low = stack_tp(gate_up_one, gate_up_near, far, *(tick(x) for x in chunks[1:3]))
            peer = swap(low)
            return join_rows(ring_last(chunks)), (low, peer)

        xn2, gate_up_w = stage(second)

        def third():
            chunks = ring_first(gy_own)
            near = near_tp(down_one)
            xn2_peer = swap(xn2[1])
            out = gate_up(xn2, *gate_up_w)
            far = far_tp(down_one, near, *chunks[1:3], out[0])
            chunks = ring_last(chunks, out[0])
            low = stack_tp(down_one, near, far)
            return join_rows(chunks), (low, swap(low)), out, xn2_peer

        gy, down_w, (hid, to_gate, to_up), xn2_peer = stage(third)
        dgu, *dx = feed_back(gy, to_gate, to_up, *gate_up_w, *down_w, own)
        here = jnp.broadcast_to(tp, (1,)).astype(jnp.int32)

        def fourth():
            came = scatter_first(dx)
            gy_peer, hid_peer, dgu_peer = swap(gy[1]), swap(hid), swap(dgu)
            g_down = weight_grad(here, gy[0], gy_peer, hid[:, None], hid_peer[:, None], "g_down")
            g_gu = weight_grad(here, xn2[0], xn2_peer, dgu, dgu_peer, "g_gate_up", (g_down, *came))
            return scatter_last(dx, came, g_gu), g_down, g_gu

        dxn2, g_down, g_gu = stage(fourth)

        def sum_tp(part):
            return lax.psum_scatter(part, "tp", scatter_dimension=0, tiled=False)

        def place_columns(part, *deps):
            return to_z(after(part.reshape(z_size, k_rows, part.shape[1]), *deps))

        gain2_part = jnp.sum(dxn2 * hres * scale2, axis=1)
        e2 = dxn2 * gain2
        dres = (
            gy_own.astype(F32)
            + scale2 * e2
            - hres
            * (scale2 * scale2 * scale2)
            * jnp.mean(e2 * hres, axis=(0, 2), keepdims=True)
        )
        dres_low = dres.astype(BF)
        g_down, g_gu = tie(sum_tp(g_down)), tie(sum_tp(g_gu))

        def fifth():
            chunks = ring_first(dres_low)
            ffn = mm_back(hid, *down_w, 0, own, "ffn_out", (tick(dres_low),))
            return join_rows(ring_last(chunks)), ffn

        dres_all, ffn = stage(fifth)
        dmix = project(dres_all, *head_w, 3 * HD, HD, "dmix")
        dmix, came = stage(lambda: (to_heads(dmix), scatter_first(ffn)))
        dheads = attend_back(table, dmix, saved, cos, sin, own, length, ())

        def sixth():
            return to_tokens(dheads), hres + scatter_last(ffn, came), place_columns(g_down)

        dqkv, layer_own, g_down = stage(sixth)
        dx = mm_back(dqkv, *head_w, 0, own, "dxn1")

        def seventh():
            came = scatter_first(dx)
            peers = swap(xn1[1]), swap(dqkv), swap(dres_all[1]), swap(mixed)
            g_heads = weight_grad_heads(
                xn1[0], peers[0], dqkv, peers[1], dres_all[0], peers[2], mixed, peers[3]
            )
            heads_came = scatter_tp_first(g_heads) if plain else ()
            return scatter_last(dx, came), g_heads, heads_came

        dxn1, g_heads, heads_came = stage(seventh)
        gain1_part = jnp.sum(dxn1 * x_own * scale1, axis=1)
        e1 = dxn1 * gain1
        in_own = (
            dres
            + scale1 * e1
            - x_own
            * (scale1 * scale1 * scale1)
            * jnp.mean(e1 * x_own, axis=(0, 2), keepdims=True)
        )

        in_own = join(in_own).astype(BF)
        layer_own = join(layer_own).astype(BF)

        gains = join(jnp.stack([gain1_part, gain2_part], axis=1)).reshape(2, shards, 1, k_rows)
        gains = jnp.broadcast_to(gains, (2, shards, tp_size, k_rows))
        gains = jnp.swapaxes(gains.reshape(2, shards * tp_size, k_rows), 0, 1)

        def eighth():
            near = near_tp(in_own)
            heads = scatter_tp_last(g_heads, heads_came) if plain else g_heads
            in_all = spread_over(in_own, near, heads)
            layer_low = after(layer_own, heads)
            layer_all = spread_over(layer_low, near_tp(layer_low))
            placed = place_columns(g_gu)
            if plain:
                heads = place_columns(heads, placed)
            return in_all, layer_all, placed, heads

        def spread_over(x, near, *deps):
            far = far_tp(x, near, *deps)
            if not (tp_size == 4 and own == block):
                return stack_tp(x, near, far)
            far = jnp.concatenate(far, axis=0)
            matched = core == tp // 2
            sent = jnp.where(matched, jnp.stack([near[1], far]), jnp.stack([x, near[0]]))
            return x[None], near[0][None], near[1][None], far[None], swap(sent)

        in_all, layer_all, g_gu, g_heads = stage(eighth)
        gains = lax.all_to_all(
            gains, ("z", "core", "tp"), split_axis=0, concat_axis=0, tiled=True
        )
        gains = jnp.sum(gains, axis=0)
        g_gate, g_up = unpack_columns(g_gu, 2, False, "unpack_gate_up")
        (g_down,) = unpack_columns(g_down, 1, True, "unpack_down")
        if plain:
            g_query, g_key, g_value, g_out = unpack_columns(g_heads, 4, True, "unpack_heads")
        else:

            def back_columns(i):
                part = jnp.swapaxes(g_heads[:, :, i * HD : (i + 1) * HD], 1, 2)
                part = join(jnp.stack([part, swap(part)])).reshape(heads_here * HD, width).T
                out = jnp.zeros((width, heads * HD), BF)
                out = lax.dynamic_update_slice(out, part, (0, at_head))
                out = jnp.where(flipped, jnp.zeros_like(out), out)
                out = lax.psum_scatter(out, ("z", "core"), scatter_dimension=0, tiled=True)
                return lax.psum_scatter(out, "tp", scatter_dimension=1, tiled=True).astype(F32)

            g_query, g_key, g_value, g_out = (back_columns(i) for i in range(4))
            g_out = g_out.T
        def spread_rows(every, dtype):
            if tp_size == 4 and own == block:
                slot = jnp.bitwise_xor(rank % 2, tp % 2)
                kept = slot + jnp.where(core == tp // 2, 0, 2)
                index = jnp.where(rank // 2 == core, kept, slot + 4)
                return place_blocks(index, every, dtype).reshape(rows, width)
            order = jnp.bitwise_xor(jnp.arange(tp_size, dtype=jnp.int32), tp)
            every = jnp.take(every, order, axis=0, mode="clip").reshape(2, rows // 2, width)
            kept = lax.dynamic_index_in_dim(every, core, axis=0, keepdims=False)
            sent = lax.dynamic_index_in_dim(every, 1 - core, axis=0, keepdims=False)
            blocks = jnp.concatenate([kept, swap(sent)]).reshape(4, block, width)
            index = jnp.where(flipped, jnp.bitwise_xor(rank, 2), rank)
            return jnp.take(blocks, index, axis=0, mode="clip").reshape(rows, width).astype(dtype)

        in_grad = spread_rows(in_all, F32)
        layer_out = spread_rows(layer_all, BF)
        return (
            layer_out,
            in_grad,
            gains[0],
            gains[1],
            g_query,
            g_key,
            g_value,
            g_out,
            g_gate,
            g_up,
            g_down,
        )

    return on_device


def solution(mesh):
    tp_size = mesh.shape["tp"]
    z_size = mesh.shape["seq"] // 2
    split = Mesh(mesh.devices.reshape(z_size, 2, tp_size), ("z", "core", "tp"))
    seq = ("z", "core")
    in_specs = (
        P(seq, None),
        P(seq),
        P(seq),
        P(),
        P(),
        P(seq, "tp"),
        P(seq, "tp"),
        P(seq, "tp"),
        P("tp", seq),
        P(seq, "tp"),
        P(seq, "tp"),
        P("tp", seq),
        P(seq, None),
    )
    out_specs = (
        P(seq, None),
        P(seq, None),
        P(seq),
        P(seq),
        P(seq, "tp"),
        P(seq, "tp"),
        P(seq, "tp"),
        P("tp", seq),
        P(seq, "tp"),
        P(seq, "tp"),
        P("tp", seq),
    )
    return jax.shard_map(
        build(z_size, tp_size), mesh=split, in_specs=in_specs, out_specs=out_specs, check_vma=False
    )
```

```python
import functools
import math

import jax
import jax.numpy as jnp
from jax import lax
from jax.experimental import pallas as pl
from jax.experimental.pallas import tpu as pltpu
from jax.sharding import Mesh
from jax.sharding import PartitionSpec as P

HD = 128
EPSILON = 1e-06
LOG2E = 1.4426950408889634
BF = jnp.bfloat16
F32 = jnp.float32
SHARE = 1
VM = pl.BlockSpec(memory_space=pltpu.VMEM)
SM = pl.BlockSpec(memory_space=pltpu.SMEM)


def dot_nt(left, right):
    return lax.dot_general(left, right, (((1,), (1,)), ((), ())), preferred_element_type=F32)


def dot_nn(left, right):
    return lax.dot_general(left, right, (((1,), (0,)), ((), ())), preferred_element_type=F32)


def dot_tn(left, right):
    return lax.dot_general(left, right, (((0,), (0,)), ((), ())), preferred_element_type=F32)


def call(body, grid, in_specs, out_specs, out_shape, scratch, flops, bytes_accessed, name, deps):
    known = len(in_specs)
    skip = len(deps)

    def run(*refs):
        body(*refs[:known], *refs[known + skip :])

    made = pl.pallas_call(
        run,
        grid=grid,
        in_specs=list(in_specs) + [pl.BlockSpec(memory_space=pl.ANY)] * skip,
        out_specs=out_specs,
        out_shape=out_shape,
        scratch_shapes=scratch,
        compiler_params=pltpu.CompilerParams(
            vmem_limit_bytes=48 << 20,
            dimension_semantics=("arbitrary",) * len(grid),
        ),
        cost_estimate=pl.CostEstimate(
            flops=flops // SHARE, transcendentals=0, bytes_accessed=bytes_accessed // SHARE
        ),
        name=name,
    )
    return lambda *args: made(*args, *deps)


def shape(dims, dtype):
    return jax.ShapeDtypeStruct(dims, dtype)


def attend_kernel(tab_ref, *refs, groups, chunk, tile, bias2):
    qkv_refs, (cos_ref, sin_ref) = refs[:groups], refs[groups : groups + 2]
    out_refs = refs[groups + 2 : 2 * groups + 2]
    q_ref, k_ref, v_ref, acc_ref = refs[2 * groups + 2 :]
    rows = qkv_refs[0].shape[0]
    per_group = rows // chunk
    length = groups * rows
    for j in range(length // chunk):
        g, s = divmod(j, per_group)
        here = pl.ds(s * chunk, chunk)
        there = pl.ds(pl.multiple_of(tab_ref[j] * chunk, chunk), chunk)
        cos = cos_ref[there, :]
        sin = sin_ref[there, :]
        q = qkv_refs[g][here, 0:HD].astype(F32)
        k = qkv_refs[g][here, HD : 2 * HD].astype(F32)
        q_ref[there, :] = (q * cos - pltpu.roll(q, HD // 2, 1) * sin).astype(BF)
        k_ref[there, :] = (k * cos - pltpu.roll(k, HD // 2, 1) * sin).astype(BF)
        v_ref[there, :] = qkv_refs[g][here, 2 * HD : 3 * HD]
    slope = -LOG2E / math.sqrt(HD)

    def part(i, j, masked):
        qs = q_ref[pl.ds(i * tile, tile), :]
        ks = k_ref[pl.ds(j * tile, tile), :]
        vs = v_ref[pl.ds(j * tile, tile), :]
        sig = 1.0 / (1.0 + jnp.exp2(dot_nt(qs, ks) * slope + bias2))
        if masked:
            row = lax.broadcasted_iota(jnp.int32, (tile, tile), 0)
            col = lax.broadcasted_iota(jnp.int32, (tile, tile), 1)
            sig = jnp.where(col <= row, sig, 0.0)
        return dot_nn(sig.astype(BF), vs)

    def query(i, carry):
        own = pl.ds(pl.multiple_of(i * tile, tile), tile)
        acc_ref[own, :] = part(i, i, True)

        def key(j, carry):
            acc_ref[own, :] += part(i, j, False)
            return carry

        lax.fori_loop(0, i, key, 0)
        return carry

    lax.fori_loop(0, length // tile, query, 0)
    for j in range(length // chunk):
        g, s = divmod(j, per_group)
        there = pl.ds(pl.multiple_of(tab_ref[j] * chunk, chunk), chunk)
        out_refs[g][pl.ds(s * chunk, chunk), :] = acc_ref[there, :].astype(BF)


def attend_back_kernel(tab_ref, *refs, groups, chunk, tile, bias2):
    grad_refs = refs[:groups]
    q_ref, k_ref, v_ref, cos_ref, sin_ref = refs[groups : groups + 5]
    out_refs = refs[groups + 5 : 2 * groups + 5]
    do_ref, dq_ref, dk_ref, dv_ref = refs[2 * groups + 5 :]
    rows = grad_refs[0].shape[0]
    per_group = rows // chunk
    length = groups * rows
    for j in range(length // chunk):
        g, s = divmod(j, per_group)
        there = pl.ds(pl.multiple_of(tab_ref[j] * chunk, chunk), chunk)
        do_ref[there, :] = grad_refs[g][pl.ds(s * chunk, chunk), :]
    slope = -LOG2E / math.sqrt(HD)
    scale = 1.0 / math.sqrt(HD)

    def part(i, j, masked):
        qi = pl.ds(pl.multiple_of(i * tile, tile), tile)
        kj = pl.ds(pl.multiple_of(j * tile, tile), tile)
        qs, ks, vs, dos = q_ref[qi, :], k_ref[kj, :], v_ref[kj, :], do_ref[qi, :]
        sig = 1.0 / (1.0 + jnp.exp2(dot_nt(ks, qs) * slope + bias2))
        dsc = dot_nt(vs, dos) * sig * (1.0 - sig)
        if masked:
            row = lax.broadcasted_iota(jnp.int32, (tile, tile), 0)
            col = lax.broadcasted_iota(jnp.int32, (tile, tile), 1)
            sig = jnp.where(row <= col, sig, 0.0)
            dsc = jnp.where(row <= col, dsc, 0.0)
        dsc = dsc.astype(BF)
        dv = dot_nn(sig.astype(BF), dos)
        dk = dot_nn(dsc, qs)
        dq = dot_tn(dsc, ks)
        if masked:
            dq_ref[qi, :] = dq
            dk_ref[kj, :] = dk
            dv_ref[kj, :] = dv
        else:
            dq_ref[qi, :] += dq
            dk_ref[kj, :] += dk
            dv_ref[kj, :] += dv

    def query(i, carry):
        part(i, i, True)

        def key(j, carry):
            part(i, j, False)
            return carry

        lax.fori_loop(0, i, key, 0)
        return carry

    lax.fori_loop(0, length // tile, query, 0)
    for j in range(length // chunk):
        g, s = divmod(j, per_group)
        here = pl.ds(s * chunk, chunk)
        there = pl.ds(pl.multiple_of(tab_ref[j] * chunk, chunk), chunk)
        cos = cos_ref[there, :] * scale
        sin = sin_ref[there, :] * scale
        dq = dq_ref[there, :]
        dk = dk_ref[there, :]
        out_refs[g][here, 0:HD] = (dq * cos + pltpu.roll(dq, HD // 2, 1) * sin).astype(BF)
        out_refs[g][here, HD : 2 * HD] = (dk * cos + pltpu.roll(dk, HD // 2, 1) * sin).astype(BF)
        out_refs[g][here, 2 * HD : 3 * HD] = dv_ref[there, :].astype(BF)


def attend(table, qkv, cos, sin, chunk, length):
    groups = len(qkv)
    rows = qkv[0].shape[0]
    tile = min(512, length)
    full = shape((length, HD), BF)
    out = pl.pallas_call(
        functools.partial(
            attend_kernel, groups=groups, chunk=chunk, tile=tile, bias2=math.log2(length)
        ),
        out_shape=(shape((rows, HD), BF),) * groups + (full,) * 3,
        in_specs=[SM] + [VM] * (groups + 2),
        out_specs=(VM,) * (groups + 3),
        scratch_shapes=[pltpu.VMEM((length, HD), F32)],
        compiler_params=pltpu.CompilerParams(vmem_limit_bytes=40 << 20),
        cost_estimate=pl.CostEstimate(
            flops=2 * length * length * HD * 2,
            transcendentals=length * length * 2,
            bytes_accessed=length * HD * 24 * 2,
        ),
        name="attend",
    )(table, *qkv, cos, sin)
    return out[:groups], out[groups:]


def attend_back(table, grad, saved, cos, sin, chunk, length, deps):
    groups = len(grad)
    rows = grad[0].shape[0]
    tile = min(512, length)
    known = groups + 6
    kernel = functools.partial(
        attend_back_kernel, groups=groups, chunk=chunk, tile=tile, bias2=math.log2(length)
    )

    def body(*refs):
        kernel(*refs[:known], *refs[known + len(deps) :])

    return pl.pallas_call(
        body,
        out_shape=(shape((rows, 3 * HD), BF),) * groups,
        in_specs=[SM] + [VM] * (groups + 5) + [pl.BlockSpec(memory_space=pl.ANY)] * len(deps),
        out_specs=(VM,) * groups,
        scratch_shapes=[pltpu.VMEM((length, HD), BF)] + [pltpu.VMEM((length, HD), F32)] * 3,
        compiler_params=pltpu.CompilerParams(vmem_limit_bytes=40 << 20),
        cost_estimate=pl.CostEstimate(
            flops=5 * length * length * HD * 2,
            transcendentals=length * length * 2,
            bytes_accessed=length * HD * 24 * 2,
        ),
        name="attend_back",
    )(table, *grad, *saved, cos, sin, *deps)


def ring_shapes(own, slots, half):
    return (
        (shape((2, own, half), F32),)
        + (shape((2, own, half), BF),) * (slots - 2)
        + (shape((2, own // 2, half), BF),) * 2
    )


def ring_store(refs, h, rows, own):
    refs[0][h] = rows[:own]
    at = own
    for ref in refs[1:]:
        n = ref.shape[1]
        ref[h] = rows[at : at + n].astype(BF)
        at += n


def project(x, w0, w1, at, n, name, deps=()):
    _, g, half = x.shape
    t = w0.shape[0]

    def body(x_ref, a_ref, b_ref, *outs):
        k = pl.program_id(0)
        rows = (dot_nn(x_ref[0], a_ref[0]) + dot_nn(x_ref[1], b_ref[0])).astype(BF)
        for i, out_ref in enumerate(outs):

            @pl.when(k == i)
            def _():
                out_ref[...] = rows

    w_spec = pl.BlockSpec((1, half, n), lambda k: (k, 0, at // n))
    return call(
        body,
        (t,),
        [pl.BlockSpec((2, g, half), lambda k: (0, 0, 0)), w_spec, w_spec],
        (pl.BlockSpec((g, n), lambda k: (0, 0)),) * t,
        (shape((g, n), BF),) * t,
        [],
        4 * g * half * t * n,
        4 * half * t * n + 4 * g * half + 2 * g * t * n,
        name,
        deps,
    )(x, w0, w1)


def mm_back(parts, w0, w1, at, own, name, deps=()):
    t, g, n = parts.shape
    half = w0.shape[1]
    th = min(half, 256)

    def body(p_ref, a_ref, b_ref, *outs):
        for h, w_ref in enumerate((a_ref, b_ref)):
            acc = dot_nt(p_ref[0], w_ref[0])
            for k in range(1, t):
                acc += dot_nt(p_ref[k], w_ref[k])
            ring_store(outs, h, acc, own)

    w_spec = pl.BlockSpec((t, th, n), lambda j: (0, j, at // n))
    shapes = ring_shapes(own, g // own, half)
    return call(
        body,
        (half // th,),
        [pl.BlockSpec((t, g, n), lambda j: (0, 0, 0)), w_spec, w_spec],
        tuple(pl.BlockSpec(o.shape[:2] + (th,), lambda j: (0, 0, j)) for o in shapes),
        shapes,
        [],
        4 * g * half * t * n,
        4 * half * t * n + 2 * g * t * n + 4 * g * half,
        name,
        deps,
    )(parts, w0, w1)


def gate_up(x, w0, w1, deps=()):
    _, g, half = x.shape
    t, _, n = w0.shape
    n //= 2
    tn = min(n, 256)
    steps = n // tn

    def body(x_ref, g0_ref, g1_ref, u0_ref, u1_ref, hid_ref, to_gate_ref, to_up_ref):
        gate = dot_nn(x_ref[0], g0_ref[0]) + dot_nn(x_ref[1], g1_ref[0])
        up = dot_nn(x_ref[0], u0_ref[0]) + dot_nn(x_ref[1], u1_ref[0])
        sig = 1.0 / (1.0 + jnp.exp(-gate))
        act = gate * sig
        hid_ref[0] = (act * up).astype(BF)
        to_gate_ref[0] = (up * (sig * (1.0 + gate * (1.0 - sig)))).astype(BF)
        to_up_ref[0] = act.astype(BF)

    g_spec = pl.BlockSpec((1, half, tn), lambda k, j: (k, 0, j))
    u_spec = pl.BlockSpec((1, half, tn), lambda k, j: (k, 0, j + steps))
    f_spec = pl.BlockSpec((1, g, tn), lambda k, j: (k, 0, j))
    return call(
        body,
        (t, steps),
        [pl.BlockSpec((2, g, half), lambda k, j: (0, 0, 0)), g_spec, g_spec, u_spec, u_spec],
        (f_spec,) * 3,
        (shape((t, g, n), BF),) * 3,
        [],
        1000,
        1000,
        "gate_up",
        deps,
    )(x, w0, w1, w0, w1)


def feed_back(gy, to_gate, to_up, w0, w1, d0, d1, own, deps=()):
    _, g, half = gy.shape
    t, _, n = d0.shape
    tn = min(n, 256)
    steps = n // tn

    def body(y_ref, a_ref, b_ref, g0_ref, g1_ref, u0_ref, u1_ref, d0_ref, d1_ref, *rest):
        out_ref, outs, acc_ref = rest[0], rest[1:-1], rest[-1]
        k, j = pl.program_id(0), pl.program_id(1)
        dh = dot_nn(y_ref[0], d0_ref[0]) + dot_nn(y_ref[1], d1_ref[0])
        dgate = (dh * a_ref[0].astype(F32)).astype(BF)
        dup = (dh * b_ref[0].astype(F32)).astype(BF)
        out_ref[0, 0] = dgate
        out_ref[0, 1] = dup
        first = jnp.logical_and(k == 0, j == 0)
        for h, (p_ref, q_ref) in enumerate(((g0_ref, u0_ref), (g1_ref, u1_ref))):
            part = dot_nt(dgate, p_ref[0]) + dot_nt(dup, q_ref[0])

            @pl.when(first)
            def _():
                acc_ref[h] = part

            @pl.when(jnp.logical_not(first))
            def _():
                acc_ref[h] += part

        @pl.when(jnp.logical_and(k == t - 1, j == steps - 1))
        def _():
            for h in range(2):
                ring_store(outs, h, acc_ref[h], own)

    g_spec = pl.BlockSpec((1, half, tn), lambda k, j: (k, 0, j))
    u_spec = pl.BlockSpec((1, half, tn), lambda k, j: (k, 0, j + steps))
    f_spec = pl.BlockSpec((1, g, tn), lambda k, j: (k, 0, j))
    shapes = ring_shapes(own, g // own, half)
    return call(
        body,
        (t, steps),
        [pl.BlockSpec((2, g, half), lambda k, j: (0, 0, 0)), f_spec, f_spec]
        + [g_spec, g_spec, u_spec, u_spec, g_spec, g_spec],
        (pl.BlockSpec((1, 2, g, tn), lambda k, j: (k, 0, 0, j)),)
        + tuple(pl.BlockSpec(o.shape, lambda k, j: (0, 0, 0)) for o in shapes),
        (shape((t, 2, g, n), BF),) + shapes,
        [pltpu.VMEM((2, g, half), F32)],
        12 * g * half * t * n,
        12 * half * t * n + 8 * g * t * n + 8 * g * half,
        "feed_back",
        deps,
    )(gy, to_gate, to_up, w0, w1, w0, w1, d0, d1)


def weight_grad(place, left, left_peer, right, right_peer, name, deps=()):
    g, half = left.shape
    t, m, _, n = right.shape
    tn = n if n % 256 else 256

    def body(s_ref, a_ref, b_ref, c_ref, d_ref, out_ref):
        del s_ref
        out_ref[0] = (
            dot_tn(a_ref[...], c_ref[0, 0]) + dot_tn(b_ref[...], d_ref[0, 0])
        ).astype(BF)

    l_spec = pl.BlockSpec((g, half), lambda k, i, j, s: (0, 0))
    r_spec = pl.BlockSpec((1, 1, g, tn), lambda k, i, j, s: (k, i, 0, j))
    return placed_call(
        body,
        (t, m, n // tn),
        [l_spec, l_spec, r_spec, r_spec],
        pl.BlockSpec((1, half, tn), lambda k, i, j, s: (k ^ s[0], 0, i * (n // tn) + j)),
        shape((t, half, m * n), BF),
        4 * g * half * t * m * n,
        4 * g * t * m * n + 4 * g * half + 2 * half * t * m * n,
        name,
        deps,
    )(place, left, left_peer, right, right_peer)


def weight_grad_heads(xn, xn_peer, dqkv, dqkv_peer, dres, dres_peer, mixed, mixed_peer, deps=()):
    g, half = xn.shape
    t, _, n = dqkv.shape
    m = mixed.shape[2]

    def body(a_ref, b_ref, c_ref, d_ref, e_ref, f_ref, g_ref, h_ref, out_ref):
        out_ref[0, :, :n] = (
            dot_tn(a_ref[...], c_ref[0]) + dot_tn(b_ref[...], d_ref[0])
        ).astype(BF)
        out_ref[0, :, n:] = (
            dot_tn(e_ref[...], g_ref[0]) + dot_tn(f_ref[...], h_ref[0])
        ).astype(BF)

    l_spec = pl.BlockSpec((g, half), lambda k: (0, 0))
    n_spec = pl.BlockSpec((1, g, n), lambda k: (k, 0, 0))
    m_spec = pl.BlockSpec((1, g, m), lambda k: (k, 0, 0))
    return call(
        body,
        (t,),
        [l_spec, l_spec, n_spec, n_spec, l_spec, l_spec, m_spec, m_spec],
        pl.BlockSpec((1, half, n + m), lambda k: (k, 0, 0)),
        shape((t, half, n + m), BF),
        [],
        4 * g * half * t * (n + m),
        4 * g * t * (n + m) + 8 * g * half + 2 * half * t * (n + m),
        "g_heads",
        deps,
    )(xn, xn_peer, dqkv, dqkv_peer, dres, dres_peer, mixed, mixed_peer)


def placed_call(body, grid, in_specs, out_specs, out_shape, flops, bytes_accessed, name, deps):
    known = len(in_specs) + 1
    skip = len(deps)

    def run(*refs):
        body(*refs[:known], *refs[known + skip :])

    made = pl.pallas_call(
        run,
        grid_spec=pltpu.PrefetchScalarGridSpec(
            num_scalar_prefetch=1,
            grid=grid,
            in_specs=list(in_specs) + [pl.BlockSpec(memory_space=pl.ANY)] * skip,
            out_specs=out_specs,
        ),
        out_shape=out_shape,
        compiler_params=pltpu.CompilerParams(
            vmem_limit_bytes=48 << 20,
            dimension_semantics=("arbitrary",) * len(grid),
        ),
        cost_estimate=pl.CostEstimate(
            flops=flops // SHARE, transcendentals=0, bytes_accessed=bytes_accessed // SHARE
        ),
        name=name,
    )
    return lambda *args: made(*args, *deps)


def pack_weights(columns, rows, parts, apart, name, deps=()):
    k, n = columns[0].shape
    n //= parts
    count = len(columns)

    def body(*refs):
        out_ref = refs[count + 1]
        for i, ref in enumerate(refs[:count]):
            out_ref[0, :, i * n : (i + 1) * n] = ref[...].astype(BF)
        turned = jnp.transpose(refs[count][...]).astype(BF)
        if apart:
            refs[-1][0] = turned
        else:
            out_ref[0, :, count * n :] = turned

    widths = (count * n, n) if apart else ((count + 1) * n,)
    return call(
        body,
        (parts,),
        [pl.BlockSpec((k, n), lambda p: (0, p))] * count + [pl.BlockSpec((n, k), lambda p: (p, 0))],
        tuple(pl.BlockSpec((1, k, w), lambda p: (p, 0, 0)) for w in widths),
        tuple(shape((parts, k, w), BF) for w in widths),
        [],
        1000,
        1000,
        name,
        deps,
    )(*columns, rows)


def unpack_columns(parts, count, transposed, name):
    z, k, n = parts.shape
    n //= count

    def body(in_ref, *outs):
        for i, ref in enumerate(outs):
            part = in_ref[0, :, i * n : (i + 1) * n].astype(F32)
            ref[...] = jnp.transpose(part) if transposed and i == count - 1 else part

    straight = (pl.BlockSpec((k, n), lambda p: (0, p)), shape((k, z * n), F32))
    turned = (pl.BlockSpec((n, k), lambda p: (p, 0)), shape((z * n, k), F32))
    outs = [straight] * (count - 1) + [turned if transposed else straight]
    return call(
        body,
        (z,),
        [pl.BlockSpec((1, k, count * n), lambda p: (p, 0, 0))],
        tuple(o[0] for o in outs),
        tuple(o[1] for o in outs),
        [],
        1000,
        1000,
        name,
        (),
    )(parts)


def place_blocks(index, sources, dtype):
    counts = [x.shape[0] for x in sources]
    rows, width = sources[0].shape[1:]
    blocks = index.shape[0]

    def body(s_ref, *refs):
        out_ref = refs[-1]
        wanted = s_ref[pl.program_id(0)]
        at = 0
        for n, ref in zip(counts, refs):
            for i in range(n):

                @pl.when(wanted == at)
                def _():
                    out_ref[0] = ref[i].astype(dtype)

                at += 1

    return placed_call(
        body,
        (blocks,),
        [pl.BlockSpec(x.shape, lambda b, s: (0, 0, 0)) for x in sources],
        pl.BlockSpec((1, rows, width), lambda b, s: (b, 0, 0)),
        shape((blocks, rows, width), dtype),
        0,
        12 * blocks * rows * width,
        "place",
        (),
    )(index, *sources)


def after(x, *deps):
    for d in deps:
        corner = lax.slice(d, [n - 1 for n in d.shape], d.shape).reshape(())
        x = x + (corner.astype(F32) * 0.0).astype(x.dtype)
    return x


def tie(x, *deps):
    anywhere = pl.BlockSpec(memory_space=pl.ANY)
    return pl.pallas_call(
        lambda *refs: None,
        in_specs=[anywhere] * (1 + len(deps)),
        out_specs=anywhere,
        out_shape=shape(x.shape, x.dtype),
        input_output_aliases={0: 0},
        name="tie",
    )(x, *deps)


def build(z_size, tp_size):
    shards = 2 * z_size
    ring = [0] + list(range(1, z_size, 2)) + list(range(z_size - 2, 0, -2))
    place = [ring.index(z) for z in range(z_size)]
    forward = [(ring[i], ring[(i + 1) % z_size]) for i in range(z_size)]
    backward = [(b, a) for a, b in forward]
    half_ring = z_size // 2
    offsets = [0]
    for k in range(1, half_ring):
        offsets += [-k, k]
    offsets += [half_ring]
    holder = [[ring[(place[z] + off) % z_size] for off in offsets] for z in range(z_size)]
    swap_core = [(0, 1), (1, 0)]

    def hop(x, bit):
        return lax.ppermute(x, "tp", [(t, t ^ bit) for t in range(tp_size)])

    def swap(x):
        return lax.ppermute(x, "core", swap_core)

    def ring_first(x):
        chunks = [x]
        ahead = back = x
        for _ in range(1, half_ring):
            ahead = lax.ppermute(ahead, "z", forward)
            back = lax.ppermute(back, "z", backward)
            chunks += [ahead, back]
        return chunks

    def ring_last(chunks, *deps):
        ahead, back = chunks[-2:]
        mid = ahead.shape[1] // 2
        one = lax.ppermute(after(ahead[:, :mid], back, *deps), "z", forward)
        two = lax.ppermute(after(back[:, mid:], ahead, *deps), "z", backward)
        return chunks + [one, two]

    def gather_ring(x, *deps):
        return ring_last(ring_first(x), *deps)

    def join_rows(chunks, *deps):
        return after(jnp.concatenate(chunks, axis=1), *deps)

    def scatter_first(parts):
        return (
            lax.ppermute(parts[-2], "z", forward),
            lax.ppermute(parts[-1], "z", backward),
        )

    def scatter_last(parts, came, *deps):
        one, two = came
        mid = parts[0].shape[1] // 2
        for k in range(half_ring - 1, 0, -1):
            fwd, bwd = parts[offsets.index(k)], parts[offsets.index(-k)]
            if k == half_ring - 1:
                fwd = jnp.concatenate([fwd[:, :mid] + one, fwd[:, mid:]], axis=1)
                bwd = jnp.concatenate([bwd[:, :mid], bwd[:, mid:] + two], axis=1)
            else:
                fwd = fwd + one
                bwd = bwd + two
            one = lax.ppermute(fwd, "z", forward)
            two = lax.ppermute(bwd, "z", backward)
        return after(parts[0] + one.astype(F32) + two.astype(F32), *deps)

    def scatter_ring(parts, *deps):
        return scatter_last(parts, scatter_first(parts), *deps)

    def tick(x):
        corner = lax.slice(x.reshape((-1,) + x.shape[-1:]), (0, 0), (16, 128))
        return swap(corner.astype(BF))

    def near_tp(x):
        return (hop(x, 1), hop(x, 2)) if tp_size == 4 else ()

    def far_tp(x, near, *deps):
        if tp_size != 4:
            return ()
        mid = x.shape[0] // 2
        return (
            hop(after(near[1][:mid], *deps), 1),
            hop(after(near[0][mid:], *deps), 2),
        )

    def stack_tp(x, near, far, *deps):
        if tp_size == 4:
            return after(jnp.stack([x, *near, jnp.concatenate(far, axis=0)]), *deps)
        held = x[None]
        bit = 1
        while bit < tp_size:
            held = jnp.concatenate([held, hop(held, bit)], axis=0)
            bit *= 2
        return held

    def gather_tp(x):
        near = near_tp(x)
        return stack_tp(x, near, far_tp(x, near))

    def scatter_tp_first(part):
        if tp_size == 4:
            mid = part.shape[1] // 2
            top, low = part[:, :mid], part[:, mid:]
            return hop(jnp.stack([top[1], top[3]]), 1), hop(jnp.stack([low[2], low[3]]), 2)
        return ()

    def scatter_tp_sums(part, came):
        if tp_size != 4:
            return (part,)
        over_x, over_y = came
        mid = part.shape[1] // 2
        top, low = part[:, :mid], part[:, mid:]
        return top[0] + over_x[0], low[0] + over_y[0], top[2] + over_x[1], low[1] + over_y[1]

    def scatter_tp_last(sums):
        if tp_size == 4:
            top, low, top_on, low_on = sums
            return jnp.concatenate([top + hop(top_on, 2), low + hop(low_on, 1)], axis=0)
        (part,) = sums
        bit = tp_size // 2
        while bit:
            part = part[:bit] + hop(part[bit:], bit)
            bit //= 2
        return part[0]

    def to_z(x):
        return lax.all_to_all(x, "z", split_axis=0, concat_axis=0, tiled=True)

    def on_device(
        layer_in,
        positions,
        seq_ids,
        norm1_gain,
        norm2_gain,
        w_query,
        w_key,
        w_value,
        w_out,
        w_gate,
        w_up,
        w_down,
        out_grad,
    ):
        z, core, tp = lax.axis_index("z"), lax.axis_index("core"), lax.axis_index("tp")
        rows, width = layer_in.shape
        half = width // 2
        block = rows // 4
        own = rows // tp_size
        group = own * z_size
        length = rows * shards // 2
        k_rows = width // shards
        heads = w_query.shape[1] * tp_size // HD
        heads_here = heads // z_size
        plain = w_query.shape[1] == z_size * HD and heads_here == tp_size
        flipped = core == 1

        def split(x):
            lead = x.shape[:-1]
            x = x.reshape(lead + (z_size, 2, k_rows))
            even, odd = x[..., 0, :].reshape(lead + (half,)), x[..., 1, :].reshape(lead + (half,))
            return jnp.stack([jnp.where(flipped, odd, even), jnp.where(flipped, even, odd)])

        def join(x):
            lead = x.shape[1:-1]
            even, odd = jnp.where(flipped, x[1], x[0]), jnp.where(flipped, x[0], x[1])
            even = even.reshape(lead + (z_size, 1, k_rows))
            odd = odd.reshape(lead + (z_size, 1, k_rows))
            return jnp.concatenate([even, odd], axis=-2).reshape(lead + (width,))

        sound = positions[0] >= 0

        def stage(run):
            outs = jax.eval_shape(run)
            blank = lambda: jax.tree.map(lambda o: jnp.zeros(o.shape, o.dtype), outs)
            return lax.cond(sound, run, blank)

        key = seq_ids.reshape(4, block)[:, 0] * (4 * length) + positions.reshape(4, block)[:, 0]
        rank = jnp.sum((key[None, :] < key[:, None]).astype(jnp.int32), axis=1)
        source_core = tp // (tp_size // 2)
        offset = (tp % (tp_size // 2)) * own

        def piece(x, seq):
            wanted = 2 * seq + offset // block
            start = jnp.sum(jnp.where(rank == wanted, jnp.arange(4, dtype=jnp.int32), 0)) * block
            return lax.dynamic_slice(x, (start + offset % block, 0), (own, width))

        def take_own(x):
            return split(jnp.where(core == source_core, piece(x, core), swap(piece(x, 1 - core))))

        x_own = take_own(layer_in).astype(F32)
        gy_own = take_own(out_grad)
        gain1 = split(norm1_gain)[:, None]
        gain2 = split(norm2_gain)[:, None]
        scale1 = lax.rsqrt(jnp.mean(x_own * x_own, axis=(0, 2), keepdims=True) + EPSILON)
        xn1_own = x_own * scale1 * gain1

        quarter = HD // 2
        frequency = jnp.power(F32(10000.0), -jnp.arange(quarter, dtype=F32) / quarter)
        phase = jnp.arange(length, dtype=jnp.int32).astype(F32)[:, None] * frequency[None, :]

        def rotations(*deps):
            turned = after(phase, *deps)
            rot_cos, rot_sin = jnp.cos(turned), jnp.sin(turned)
            cos = jnp.concatenate([rot_cos, rot_cos], axis=1)
            return cos, jnp.concatenate([rot_sin, -rot_sin], axis=1)

        def exchange(w):
            return to_z(w).reshape(half, w.shape[2])

        if plain:
            (low,) = pack_weights(
                (w_query, w_key, w_value), w_out, z_size, False, "pack_heads"
            )
            low = exchange(low)
            xn1_low = after(xn1_own, low).astype(BF)

            def begin():
                chunks = ring_first(xn1_low)
                near = near_tp(low)
                started = tick(low)
                turns = rotations(started)
                far = far_tp(low, near, *chunks[1:3], turns[0])
                ffn_low = pack_weights(
                    (w_gate, w_up), w_down, z_size, True, "pack_ffn", (tick(chunks[-1]),)
                )
                chunks = ring_last(chunks)
                full = stack_tp(low, near, far, *chunks[-2:])
                return join_rows(chunks), (full, swap(full)), turns, ffn_low

            xn1, head_w, (cos, sin), ffn_low = stage(begin)
        else:
            at_head = z * heads_here * HD

            def columns(w):
                w = lax.all_gather(w.astype(BF), "tp", axis=1, tiled=True)
                w = lax.all_gather(w, ("z", "core"), axis=0, tiled=True)
                w = lax.dynamic_slice(w, (0, at_head), (width, heads_here * HD))
                return jnp.swapaxes(split(w.T).reshape(2, heads_here, HD, half), 2, 3)

            low = [columns(w) for w in (w_query, w_key, w_value, w_out.T)]
            low = jnp.concatenate(low, axis=3)
            head_w = (low[0], low[1])
            xn1 = join_rows(gather_ring(xn1_own.astype(BF)))
            cos, sin = rotations()
            ffn_low = pack_weights((w_gate, w_up), w_down, z_size, True, "pack_ffn")
        gate_up_one = exchange(ffn_low[0])

        t_all = jnp.arange(tp_size, dtype=jnp.int32)[:, None]
        if plain:
            t_all = jnp.bitwise_xor(t_all, tp)
        z_all = jnp.asarray(holder, jnp.int32)[z][None, :]
        off_all = (t_all % (tp_size // 2)) * own
        shard_all = 2 * z_all + t_all // (tp_size // 2)
        block_all = jnp.where(off_all < block, shard_all, 2 * shards - 1 - shard_all)
        table = ((block_all * block + off_all % block) // own).reshape(-1)

        def to_heads(x):
            if plain:
                return [x[0]] + [hop(x[k], k) for k in range(1, tp_size)]
            every = lax.all_gather(jnp.stack(x), "tp", axis=0)
            every = lax.dynamic_index_in_dim(
                every, tp * heads_here // tp_size, axis=1, keepdims=False
            )
            return [every[k] for k in range(tp_size)]

        def to_tokens(x):
            if plain:
                return jnp.stack([x[0]] + [hop(x[k], k) for k in range(1, tp_size)])
            every = lax.all_gather(jnp.stack(x), "tp", axis=0)[:: tp_size // heads_here]
            return lax.dynamic_index_in_dim(every, tp, axis=1, keepdims=False)

        qkv = project(xn1, *head_w, 0, 3 * HD, "qkv")
        heads_out, saved = attend(table, to_heads(qkv), cos, sin, own, length)
        mixed = to_tokens(heads_out)
        attn = mm_back(mixed, *head_w, 3 * HD, own, "attn_out")

        def first():
            return x_own + scatter_ring(attn), near_tp(gate_up_one)

        hres, gate_up_near = stage(first)
        down_one = exchange(tie(ffn_low[1], hres))

        scale2 = lax.rsqrt(jnp.mean(hres * hres, axis=(0, 2), keepdims=True) + EPSILON)
        xn2_own = (hres * scale2 * gain2).astype(BF)

        def second():
            chunks = ring_first(xn2_own)
            far = far_tp(gate_up_one, gate_up_near, tick(xn2_own))
            low = stack_tp(gate_up_one, gate_up_near, far, *(tick(x) for x in chunks[1:3]))
            peer = swap(low)
            return join_rows(ring_last(chunks)), (low, peer)

        xn2, gate_up_w = stage(second)

        def third():
            chunks = ring_first(gy_own)
            near = near_tp(down_one)
            xn2_peer = swap(xn2[1])
            out = gate_up(xn2, *gate_up_w)
            far = far_tp(down_one, near, *chunks[1:3], out[0])
            chunks = ring_last(chunks, out[0])
            low = stack_tp(down_one, near, far)
            return join_rows(chunks), (low, swap(low)), out, xn2_peer

        gy, down_w, (hid, to_gate, to_up), xn2_peer = stage(third)
        dgu, *dx = feed_back(gy, to_gate, to_up, *gate_up_w, *down_w, own)
        here = jnp.broadcast_to(tp, (1,)).astype(jnp.int32)

        def fourth():
            came = scatter_first(dx)
            gy_peer, hid_peer, dgu_peer = swap(gy[1]), swap(hid), swap(dgu)
            g_down = weight_grad(here, gy[0], gy_peer, hid[:, None], hid_peer[:, None], "g_down")
            return scatter_last(dx, came, g_down), g_down, dgu_peer

        dxn2, g_down, dgu_peer = stage(fourth)

        def sum_tp(part):
            return lax.psum_scatter(part, "tp", scatter_dimension=0, tiled=False)

        def place_columns(part, *deps):
            return to_z(after(part.reshape(z_size, k_rows, part.shape[1]), *deps))

        gain2_part = jnp.sum(dxn2 * hres * scale2, axis=1)
        e2 = dxn2 * gain2
        dres = (
            gy_own.astype(F32)
            + scale2 * e2
            - hres
            * (scale2 * scale2 * scale2)
            * jnp.mean(e2 * hres, axis=(0, 2), keepdims=True)
        )
        dres_low = dres.astype(BF)
        g_down = tie(sum_tp(g_down))

        def fifth():
            chunks = ring_first(dres_low)
            started = (tick(dres_low),)
            ffn = mm_back(hid, *down_w, 0, own, "ffn_out", started)
            g_gu = weight_grad(here, xn2[0], xn2_peer, dgu, dgu_peer, "g_gate_up", started)
            return join_rows(ring_last(chunks), g_gu), ffn, g_gu

        dres_all, ffn, g_gu = stage(fifth)
        g_gu = tie(sum_tp(g_gu))
        dmix = project(dres_all, *head_w, 3 * HD, HD, "dmix")
        dmix, came = stage(lambda: (to_heads(dmix), scatter_first(ffn)))
        dheads = attend_back(table, dmix, saved, cos, sin, own, length, ())

        def sixth():
            return to_tokens(dheads), hres + scatter_last(ffn, came), place_columns(g_down)

        dqkv, layer_own, g_down = stage(sixth)
        dx = mm_back(dqkv, *head_w, 0, own, "dxn1")

        def seventh():
            came = scatter_first(dx)
            peers = swap(xn1[1]), swap(dqkv), swap(dres_all[1]), swap(mixed)
            g_heads = weight_grad_heads(
                xn1[0], peers[0], dqkv, peers[1], dres_all[0], peers[2], mixed, peers[3]
            )
            if plain:
                g_heads = scatter_tp_sums(g_heads, scatter_tp_first(g_heads))
            return scatter_last(dx, came), g_heads

        dxn1, g_heads = stage(seventh)
        gain1_part = jnp.sum(dxn1 * x_own * scale1, axis=1)
        e1 = dxn1 * gain1
        in_own = (
            dres
            + scale1 * e1
            - x_own
            * (scale1 * scale1 * scale1)
            * jnp.mean(e1 * x_own, axis=(0, 2), keepdims=True)
        )

        in_own = join(in_own).astype(BF)
        layer_own = join(layer_own).astype(BF)

        gains = join(jnp.stack([gain1_part, gain2_part], axis=1)).reshape(2, shards, 1, k_rows)
        gains = jnp.broadcast_to(gains, (2, shards, tp_size, k_rows))
        gains = jnp.swapaxes(gains.reshape(2, shards * tp_size, k_rows), 0, 1)

        def spread_rows(every, dtype):
            if tp_size == 4 and own == block:
                slot = jnp.bitwise_xor(rank % 2, tp % 2)
                kept = slot + jnp.where(core == tp // 2, 0, 2)
                index = jnp.where(rank // 2 == core, kept, slot + 4)
                return place_blocks(index, every, dtype).reshape(rows, width)
            order = jnp.bitwise_xor(jnp.arange(tp_size, dtype=jnp.int32), tp)
            every = jnp.take(every, order, axis=0, mode="clip").reshape(2, rows // 2, width)
            kept = lax.dynamic_index_in_dim(every, core, axis=0, keepdims=False)
            sent = lax.dynamic_index_in_dim(every, 1 - core, axis=0, keepdims=False)
            blocks = jnp.concatenate([kept, swap(sent)]).reshape(4, block, width)
            index = jnp.where(flipped, jnp.bitwise_xor(rank, 2), rank)
            return jnp.take(blocks, index, axis=0, mode="clip").reshape(rows, width).astype(dtype)

        def eighth():
            near = near_tp(in_own)
            heads = scatter_tp_last(g_heads) if plain else g_heads
            in_all = spread_over(in_own, near)
            layer_all = spread_over(layer_own, near_tp(layer_own))
            placed = place_columns(g_gu)
            if plain:
                heads = place_columns(heads)
            in_grad, layer_out = spread_rows(in_all, F32), spread_rows(layer_all, BF)
            gate_up = unpack_columns(placed, 2, False, "unpack_gate_up")
            down = unpack_columns(g_down, 1, True, "unpack_down")
            return in_grad, layer_out, (*gate_up, *down), heads

        def spread_over(x, near, *deps):
            far = far_tp(x, near, *deps)
            if not (tp_size == 4 and own == block):
                return stack_tp(x, near, far)
            far = jnp.concatenate(far, axis=0)
            matched = core == tp // 2
            sent = jnp.where(matched, jnp.stack([near[1], far]), jnp.stack([x, near[0]]))
            return x[None], near[0][None], near[1][None], far[None], swap(sent)

        in_grad, layer_out, (g_gate, g_up, g_down), g_heads = stage(eighth)
        gains = lax.all_to_all(
            gains, ("z", "core", "tp"), split_axis=0, concat_axis=0, tiled=True
        )
        gains = jnp.sum(gains, axis=0)
        if plain:
            g_query, g_key, g_value, g_out = unpack_columns(g_heads, 4, True, "unpack_heads")
        else:

            def back_columns(i):
                part = jnp.swapaxes(g_heads[:, :, i * HD : (i + 1) * HD], 1, 2)
                part = join(jnp.stack([part, swap(part)])).reshape(heads_here * HD, width).T
                out = jnp.zeros((width, heads * HD), BF)
                out = lax.dynamic_update_slice(out, part, (0, at_head))
                out = jnp.where(flipped, jnp.zeros_like(out), out)
                out = lax.psum_scatter(out, ("z", "core"), scatter_dimension=0, tiled=True)
                return lax.psum_scatter(out, "tp", scatter_dimension=1, tiled=True).astype(F32)

            g_query, g_key, g_value, g_out = (back_columns(i) for i in range(4))
            g_out = g_out.T
        return (
            layer_out,
            in_grad,
            gains[0],
            gains[1],
            g_query,
            g_key,
            g_value,
            g_out,
            g_gate,
            g_up,
            g_down,
        )

    return on_device


def solution(mesh):
    tp_size = mesh.shape["tp"]
    z_size = mesh.shape["seq"] // 2
    split = Mesh(mesh.devices.reshape(z_size, 2, tp_size), ("z", "core", "tp"))
    seq = ("z", "core")
    in_specs = (
        P(seq, None),
        P(seq),
        P(seq),
        P(),
        P(),
        P(seq, "tp"),
        P(seq, "tp"),
        P(seq, "tp"),
        P("tp", seq),
        P(seq, "tp"),
        P(seq, "tp"),
        P("tp", seq),
        P(seq, None),
    )
    out_specs = (
        P(seq, None),
        P(seq, None),
        P(seq),
        P(seq),
        P(seq, "tp"),
        P(seq, "tp"),
        P(seq, "tp"),
        P("tp", seq),
        P(seq, "tp"),
        P(seq, "tp"),
        P("tp", seq),
    )
    return jax.shard_map(
        build(z_size, tp_size), mesh=split, in_specs=in_specs, out_specs=out_specs, check_vma=False
    )
```

```python
import functools
import math

import jax
import jax.numpy as jnp
from jax import lax
from jax.experimental import pallas as pl
from jax.experimental.pallas import tpu as pltpu
from jax.sharding import Mesh
from jax.sharding import PartitionSpec as P

HD = 128
EPSILON = 1e-06
LOG2E = 1.4426950408889634
BF = jnp.bfloat16
F32 = jnp.float32
SHARE = 1
VM = pl.BlockSpec(memory_space=pltpu.VMEM)
SM = pl.BlockSpec(memory_space=pltpu.SMEM)


def dot_nt(left, right):
    return lax.dot_general(left, right, (((1,), (1,)), ((), ())), preferred_element_type=F32)


def dot_nn(left, right):
    return lax.dot_general(left, right, (((1,), (0,)), ((), ())), preferred_element_type=F32)


def dot_tn(left, right):
    return lax.dot_general(left, right, (((0,), (0,)), ((), ())), preferred_element_type=F32)


def call(body, grid, in_specs, out_specs, out_shape, scratch, flops, bytes_accessed, name, deps):
    known = len(in_specs)
    skip = len(deps)

    def run(*refs):
        body(*refs[:known], *refs[known + skip :])

    made = pl.pallas_call(
        run,
        grid=grid,
        in_specs=list(in_specs) + [pl.BlockSpec(memory_space=pl.ANY)] * skip,
        out_specs=out_specs,
        out_shape=out_shape,
        scratch_shapes=scratch,
        compiler_params=pltpu.CompilerParams(
            vmem_limit_bytes=48 << 20,
            dimension_semantics=("arbitrary",) * len(grid),
        ),
        cost_estimate=pl.CostEstimate(
            flops=flops // SHARE, transcendentals=0, bytes_accessed=bytes_accessed // SHARE
        ),
        name=name,
    )
    return lambda *args: made(*args, *deps)


def shape(dims, dtype):
    return jax.ShapeDtypeStruct(dims, dtype)


def attend_kernel(tab_ref, *refs, groups, chunk, tile, bias2):
    qkv_refs, (cos_ref, sin_ref) = refs[:groups], refs[groups : groups + 2]
    out_refs = refs[groups + 2 : 2 * groups + 2]
    q_ref, k_ref, v_ref, acc_ref = refs[2 * groups + 2 :]
    rows = qkv_refs[0].shape[0]
    per_group = rows // chunk
    length = groups * rows
    for j in range(length // chunk):
        g, s = divmod(j, per_group)
        here = pl.ds(s * chunk, chunk)
        there = pl.ds(pl.multiple_of(tab_ref[j] * chunk, chunk), chunk)
        cos = cos_ref[there, :]
        sin = sin_ref[there, :]
        q = qkv_refs[g][here, 0:HD].astype(F32)
        k = qkv_refs[g][here, HD : 2 * HD].astype(F32)
        q_ref[there, :] = (q * cos - pltpu.roll(q, HD // 2, 1) * sin).astype(BF)
        k_ref[there, :] = (k * cos - pltpu.roll(k, HD // 2, 1) * sin).astype(BF)
        v_ref[there, :] = qkv_refs[g][here, 2 * HD : 3 * HD]
    slope = -LOG2E / math.sqrt(HD)

    def part(i, j, masked):
        qs = q_ref[pl.ds(i * tile, tile), :]
        ks = k_ref[pl.ds(j * tile, tile), :]
        vs = v_ref[pl.ds(j * tile, tile), :]
        sig = 1.0 / (1.0 + jnp.exp2(dot_nt(qs, ks) * slope + bias2))
        if masked:
            row = lax.broadcasted_iota(jnp.int32, (tile, tile), 0)
            col = lax.broadcasted_iota(jnp.int32, (tile, tile), 1)
            sig = jnp.where(col <= row, sig, 0.0)
        return dot_nn(sig.astype(BF), vs)

    def query(i, carry):
        own = pl.ds(pl.multiple_of(i * tile, tile), tile)
        acc_ref[own, :] = part(i, i, True)

        def key(j, carry):
            acc_ref[own, :] += part(i, j, False)
            return carry

        lax.fori_loop(0, i, key, 0)
        return carry

    lax.fori_loop(0, length // tile, query, 0)
    for j in range(length // chunk):
        g, s = divmod(j, per_group)
        there = pl.ds(pl.multiple_of(tab_ref[j] * chunk, chunk), chunk)
        out_refs[g][pl.ds(s * chunk, chunk), :] = acc_ref[there, :].astype(BF)


def attend_back_kernel(tab_ref, *refs, groups, chunk, tile, bias2):
    grad_refs = refs[:groups]
    q_ref, k_ref, v_ref, cos_ref, sin_ref = refs[groups : groups + 5]
    out_refs = refs[groups + 5 : 2 * groups + 5]
    do_ref, dq_ref, dk_ref, dv_ref = refs[2 * groups + 5 :]
    rows = grad_refs[0].shape[0]
    per_group = rows // chunk
    length = groups * rows
    for j in range(length // chunk):
        g, s = divmod(j, per_group)
        there = pl.ds(pl.multiple_of(tab_ref[j] * chunk, chunk), chunk)
        do_ref[there, :] = grad_refs[g][pl.ds(s * chunk, chunk), :]
    slope = -LOG2E / math.sqrt(HD)
    scale = 1.0 / math.sqrt(HD)

    def part(i, j, masked):
        qi = pl.ds(pl.multiple_of(i * tile, tile), tile)
        kj = pl.ds(pl.multiple_of(j * tile, tile), tile)
        qs, ks, vs, dos = q_ref[qi, :], k_ref[kj, :], v_ref[kj, :], do_ref[qi, :]
        sig = 1.0 / (1.0 + jnp.exp2(dot_nt(ks, qs) * slope + bias2))
        dsc = dot_nt(vs, dos) * sig * (1.0 - sig)
        if masked:
            row = lax.broadcasted_iota(jnp.int32, (tile, tile), 0)
            col = lax.broadcasted_iota(jnp.int32, (tile, tile), 1)
            sig = jnp.where(row <= col, sig, 0.0)
            dsc = jnp.where(row <= col, dsc, 0.0)
        dsc = dsc.astype(BF)
        dv = dot_nn(sig.astype(BF), dos)
        dk = dot_nn(dsc, qs)
        dq = dot_tn(dsc, ks)
        if masked:
            dq_ref[qi, :] = dq
            dk_ref[kj, :] = dk
            dv_ref[kj, :] = dv
        else:
            dq_ref[qi, :] += dq
            dk_ref[kj, :] += dk
            dv_ref[kj, :] += dv

    def query(i, carry):
        part(i, i, True)

        def key(j, carry):
            part(i, j, False)
            return carry

        lax.fori_loop(0, i, key, 0)
        return carry

    lax.fori_loop(0, length // tile, query, 0)
    for j in range(length // chunk):
        g, s = divmod(j, per_group)
        here = pl.ds(s * chunk, chunk)
        there = pl.ds(pl.multiple_of(tab_ref[j] * chunk, chunk), chunk)
        cos = cos_ref[there, :] * scale
        sin = sin_ref[there, :] * scale
        dq = dq_ref[there, :]
        dk = dk_ref[there, :]
        out_refs[g][here, 0:HD] = (dq * cos + pltpu.roll(dq, HD // 2, 1) * sin).astype(BF)
        out_refs[g][here, HD : 2 * HD] = (dk * cos + pltpu.roll(dk, HD // 2, 1) * sin).astype(BF)
        out_refs[g][here, 2 * HD : 3 * HD] = dv_ref[there, :].astype(BF)


def attend(table, qkv, cos, sin, chunk, length):
    groups = len(qkv)
    rows = qkv[0].shape[0]
    tile = min(512, length)
    full = shape((length, HD), BF)
    out = pl.pallas_call(
        functools.partial(
            attend_kernel, groups=groups, chunk=chunk, tile=tile, bias2=math.log2(length)
        ),
        out_shape=(shape((rows, HD), BF),) * groups + (full,) * 3,
        in_specs=[SM] + [VM] * (groups + 2),
        out_specs=(VM,) * (groups + 3),
        scratch_shapes=[pltpu.VMEM((length, HD), F32)],
        compiler_params=pltpu.CompilerParams(vmem_limit_bytes=40 << 20),
        cost_estimate=pl.CostEstimate(
            flops=2 * length * length * HD * 2,
            transcendentals=length * length * 2,
            bytes_accessed=length * HD * 24 * 2,
        ),
        name="attend",
    )(table, *qkv, cos, sin)
    return out[:groups], out[groups:]


def attend_back(table, grad, saved, cos, sin, chunk, length, deps):
    groups = len(grad)
    rows = grad[0].shape[0]
    tile = min(512, length)
    known = groups + 6
    kernel = functools.partial(
        attend_back_kernel, groups=groups, chunk=chunk, tile=tile, bias2=math.log2(length)
    )

    def body(*refs):
        kernel(*refs[:known], *refs[known + len(deps) :])

    return pl.pallas_call(
        body,
        out_shape=(shape((rows, 3 * HD), BF),) * groups,
        in_specs=[SM] + [VM] * (groups + 5) + [pl.BlockSpec(memory_space=pl.ANY)] * len(deps),
        out_specs=(VM,) * groups,
        scratch_shapes=[pltpu.VMEM((length, HD), BF)] + [pltpu.VMEM((length, HD), F32)] * 3,
        compiler_params=pltpu.CompilerParams(vmem_limit_bytes=40 << 20),
        cost_estimate=pl.CostEstimate(
            flops=5 * length * length * HD * 2,
            transcendentals=length * length * 2,
            bytes_accessed=length * HD * 24 * 2,
        ),
        name="attend_back",
    )(table, *grad, *saved, cos, sin, *deps)


def ring_shapes(own, slots, half):
    return (
        (shape((2, own, half), F32),)
        + (shape((2, own, half), BF),) * (slots - 2)
        + (shape((2, own // 2, half), BF),) * 2
    )


def ring_store(refs, h, rows, own):
    refs[0][h] = rows[:own]
    at = own
    for ref in refs[1:]:
        n = ref.shape[1]
        ref[h] = rows[at : at + n].astype(BF)
        at += n


def project(x, w0, w1, at, n, name, deps=()):
    _, g, half = x.shape
    t = w0.shape[0]

    def body(x_ref, a_ref, b_ref, *outs):
        k = pl.program_id(0)
        rows = (dot_nn(x_ref[0], a_ref[0]) + dot_nn(x_ref[1], b_ref[0])).astype(BF)
        for i, out_ref in enumerate(outs):

            @pl.when(k == i)
            def _():
                out_ref[...] = rows

    w_spec = pl.BlockSpec((1, half, n), lambda k: (k, 0, at // n))
    return call(
        body,
        (t,),
        [pl.BlockSpec((2, g, half), lambda k: (0, 0, 0)), w_spec, w_spec],
        (pl.BlockSpec((g, n), lambda k: (0, 0)),) * t,
        (shape((g, n), BF),) * t,
        [],
        4 * g * half * t * n,
        4 * half * t * n + 4 * g * half + 2 * g * t * n,
        name,
        deps,
    )(x, w0, w1)


def mm_back(parts, w0, w1, at, own, name, deps=()):
    t, g, n = parts.shape
    half = w0.shape[1]
    th = min(half, 256)

    def body(p_ref, a_ref, b_ref, *outs):
        for h, w_ref in enumerate((a_ref, b_ref)):
            acc = dot_nt(p_ref[0], w_ref[0])
            for k in range(1, t):
                acc += dot_nt(p_ref[k], w_ref[k])
            ring_store(outs, h, acc, own)

    w_spec = pl.BlockSpec((t, th, n), lambda j: (0, j, at // n))
    shapes = ring_shapes(own, g // own, half)
    return call(
        body,
        (half // th,),
        [pl.BlockSpec((t, g, n), lambda j: (0, 0, 0)), w_spec, w_spec],
        tuple(pl.BlockSpec(o.shape[:2] + (th,), lambda j: (0, 0, j)) for o in shapes),
        shapes,
        [],
        4 * g * half * t * n,
        4 * half * t * n + 2 * g * t * n + 4 * g * half,
        name,
        deps,
    )(parts, w0, w1)


def gate_up(x, w0, w1, deps=()):
    _, g, half = x.shape
    t, _, n = w0.shape
    n //= 2
    tn = min(n, 256)
    steps = n // tn

    def body(x_ref, g0_ref, g1_ref, u0_ref, u1_ref, hid_ref, to_gate_ref, to_up_ref):
        gate = dot_nn(x_ref[0], g0_ref[0]) + dot_nn(x_ref[1], g1_ref[0])
        up = dot_nn(x_ref[0], u0_ref[0]) + dot_nn(x_ref[1], u1_ref[0])
        sig = 1.0 / (1.0 + jnp.exp(-gate))
        act = gate * sig
        hid_ref[0] = (act * up).astype(BF)
        to_gate_ref[0] = (up * (sig * (1.0 + gate * (1.0 - sig)))).astype(BF)
        to_up_ref[0] = act.astype(BF)

    g_spec = pl.BlockSpec((1, half, tn), lambda k, j: (k, 0, j))
    u_spec = pl.BlockSpec((1, half, tn), lambda k, j: (k, 0, j + steps))
    f_spec = pl.BlockSpec((1, g, tn), lambda k, j: (k, 0, j))
    return call(
        body,
        (t, steps),
        [pl.BlockSpec((2, g, half), lambda k, j: (0, 0, 0)), g_spec, g_spec, u_spec, u_spec],
        (f_spec,) * 3,
        (shape((t, g, n), BF),) * 3,
        [],
        1000,
        1000,
        "gate_up",
        deps,
    )(x, w0, w1, w0, w1)


def feed_back(gy, to_gate, to_up, w0, w1, d0, d1, own, deps=()):
    _, g, half = gy.shape
    t, _, n = d0.shape
    tn = min(n, 256)
    steps = n // tn

    def body(y_ref, a_ref, b_ref, g0_ref, g1_ref, u0_ref, u1_ref, d0_ref, d1_ref, *rest):
        out_ref, outs, acc_ref = rest[0], rest[1:-1], rest[-1]
        k, j = pl.program_id(0), pl.program_id(1)
        dh = dot_nn(y_ref[0], d0_ref[0]) + dot_nn(y_ref[1], d1_ref[0])
        dgate = (dh * a_ref[0].astype(F32)).astype(BF)
        dup = (dh * b_ref[0].astype(F32)).astype(BF)
        out_ref[0, 0] = dgate
        out_ref[0, 1] = dup
        first = jnp.logical_and(k == 0, j == 0)
        for h, (p_ref, q_ref) in enumerate(((g0_ref, u0_ref), (g1_ref, u1_ref))):
            part = dot_nt(dgate, p_ref[0]) + dot_nt(dup, q_ref[0])

            @pl.when(first)
            def _():
                acc_ref[h] = part

            @pl.when(jnp.logical_not(first))
            def _():
                acc_ref[h] += part

        @pl.when(jnp.logical_and(k == t - 1, j == steps - 1))
        def _():
            for h in range(2):
                ring_store(outs, h, acc_ref[h], own)

    g_spec = pl.BlockSpec((1, half, tn), lambda k, j: (k, 0, j))
    u_spec = pl.BlockSpec((1, half, tn), lambda k, j: (k, 0, j + steps))
    f_spec = pl.BlockSpec((1, g, tn), lambda k, j: (k, 0, j))
    shapes = ring_shapes(own, g // own, half)
    return call(
        body,
        (t, steps),
        [pl.BlockSpec((2, g, half), lambda k, j: (0, 0, 0)), f_spec, f_spec]
        + [g_spec, g_spec, u_spec, u_spec, g_spec, g_spec],
        (pl.BlockSpec((1, 2, g, tn), lambda k, j: (k, 0, 0, j)),)
        + tuple(pl.BlockSpec(o.shape, lambda k, j: (0, 0, 0)) for o in shapes),
        (shape((t, 2, g, n), BF),) + shapes,
        [pltpu.VMEM((2, g, half), F32)],
        12 * g * half * t * n,
        12 * half * t * n + 8 * g * t * n + 8 * g * half,
        "feed_back",
        deps,
    )(gy, to_gate, to_up, w0, w1, w0, w1, d0, d1)


def weight_grad(place, left, left_peer, right, right_peer, name, deps=()):
    g, half = left.shape
    t, m, _, n = right.shape
    tn = n if n % 256 else 256

    def body(s_ref, a_ref, b_ref, c_ref, d_ref, out_ref):
        del s_ref
        out_ref[0] = (
            dot_tn(a_ref[...], c_ref[0, 0]) + dot_tn(b_ref[...], d_ref[0, 0])
        ).astype(BF)

    l_spec = pl.BlockSpec((g, half), lambda k, i, j, s: (0, 0))
    r_spec = pl.BlockSpec((1, 1, g, tn), lambda k, i, j, s: (k, i, 0, j))
    return placed_call(
        body,
        (t, m, n // tn),
        [l_spec, l_spec, r_spec, r_spec],
        pl.BlockSpec((1, half, tn), lambda k, i, j, s: (k ^ s[0], 0, i * (n // tn) + j)),
        shape((t, half, m * n), BF),
        4 * g * half * t * m * n,
        4 * g * t * m * n + 4 * g * half + 2 * half * t * m * n,
        name,
        deps,
    )(place, left, left_peer, right, right_peer)


def weight_grad_heads(xn, xn_peer, dqkv, dqkv_peer, dres, dres_peer, mixed, mixed_peer, deps=()):
    g, half = xn.shape
    t, _, n = dqkv.shape
    m = mixed.shape[2]

    def body(a_ref, b_ref, c_ref, d_ref, e_ref, f_ref, g_ref, h_ref, out_ref):
        out_ref[0, :, :n] = (
            dot_tn(a_ref[...], c_ref[0]) + dot_tn(b_ref[...], d_ref[0])
        ).astype(BF)
        out_ref[0, :, n:] = (
            dot_tn(e_ref[...], g_ref[0]) + dot_tn(f_ref[...], h_ref[0])
        ).astype(BF)

    l_spec = pl.BlockSpec((g, half), lambda k: (0, 0))
    n_spec = pl.BlockSpec((1, g, n), lambda k: (k, 0, 0))
    m_spec = pl.BlockSpec((1, g, m), lambda k: (k, 0, 0))
    return call(
        body,
        (t,),
        [l_spec, l_spec, n_spec, n_spec, l_spec, l_spec, m_spec, m_spec],
        pl.BlockSpec((1, half, n + m), lambda k: (k, 0, 0)),
        shape((t, half, n + m), BF),
        [],
        4 * g * half * t * (n + m),
        4 * g * t * (n + m) + 8 * g * half + 2 * half * t * (n + m),
        "g_heads",
        deps,
    )(xn, xn_peer, dqkv, dqkv_peer, dres, dres_peer, mixed, mixed_peer)


def placed_call(body, grid, in_specs, out_specs, out_shape, flops, bytes_accessed, name, deps):
    known = len(in_specs) + 1
    skip = len(deps)

    def run(*refs):
        body(*refs[:known], *refs[known + skip :])

    made = pl.pallas_call(
        run,
        grid_spec=pltpu.PrefetchScalarGridSpec(
            num_scalar_prefetch=1,
            grid=grid,
            in_specs=list(in_specs) + [pl.BlockSpec(memory_space=pl.ANY)] * skip,
            out_specs=out_specs,
        ),
        out_shape=out_shape,
        compiler_params=pltpu.CompilerParams(
            vmem_limit_bytes=48 << 20,
            dimension_semantics=("arbitrary",) * len(grid),
        ),
        cost_estimate=pl.CostEstimate(
            flops=flops // SHARE, transcendentals=0, bytes_accessed=bytes_accessed // SHARE
        ),
        name=name,
    )
    return lambda *args: made(*args, *deps)


def pack_weights(columns, rows, parts, apart, name, deps=()):
    k, n = columns[0].shape
    n //= parts
    count = len(columns)

    def body(*refs):
        out_ref = refs[count + 1]
        for i, ref in enumerate(refs[:count]):
            out_ref[0, :, i * n : (i + 1) * n] = ref[...].astype(BF)
        turned = jnp.transpose(refs[count][...]).astype(BF)
        if apart:
            refs[-1][0] = turned
        else:
            out_ref[0, :, count * n :] = turned

    widths = (count * n, n) if apart else ((count + 1) * n,)
    return call(
        body,
        (parts,),
        [pl.BlockSpec((k, n), lambda p: (0, p))] * count + [pl.BlockSpec((n, k), lambda p: (p, 0))],
        tuple(pl.BlockSpec((1, k, w), lambda p: (p, 0, 0)) for w in widths),
        tuple(shape((parts, k, w), BF) for w in widths),
        [],
        1000,
        1000,
        name,
        deps,
    )(*columns, rows)


def unpack_columns(parts, count, transposed, name):
    z, k, n = parts.shape
    n //= count

    def body(in_ref, *outs):
        for i, ref in enumerate(outs):
            part = in_ref[0, :, i * n : (i + 1) * n].astype(F32)
            ref[...] = jnp.transpose(part) if transposed and i == count - 1 else part

    straight = (pl.BlockSpec((k, n), lambda p: (0, p)), shape((k, z * n), F32))
    turned = (pl.BlockSpec((n, k), lambda p: (p, 0)), shape((z * n, k), F32))
    outs = [straight] * (count - 1) + [turned if transposed else straight]
    return call(
        body,
        (z,),
        [pl.BlockSpec((1, k, count * n), lambda p: (p, 0, 0))],
        tuple(o[0] for o in outs),
        tuple(o[1] for o in outs),
        [],
        1000,
        1000,
        name,
        (),
    )(parts)


def place_blocks(index, sources, dtype):
    counts = [x.shape[0] for x in sources]
    rows, width = sources[0].shape[1:]
    blocks = index.shape[0]

    def body(s_ref, *refs):
        out_ref = refs[-1]
        wanted = s_ref[pl.program_id(0)]
        at = 0
        for n, ref in zip(counts, refs):
            for i in range(n):

                @pl.when(wanted == at)
                def _():
                    out_ref[0] = ref[i].astype(dtype)

                at += 1

    return placed_call(
        body,
        (blocks,),
        [pl.BlockSpec(x.shape, lambda b, s: (0, 0, 0)) for x in sources],
        pl.BlockSpec((1, rows, width), lambda b, s: (b, 0, 0)),
        shape((blocks, rows, width), dtype),
        0,
        12 * blocks * rows * width,
        "place",
        (),
    )(index, *sources)


def after(x, *deps):
    for d in deps:
        corner = lax.slice(d, [n - 1 for n in d.shape], d.shape).reshape(())
        x = x + (corner.astype(F32) * 0.0).astype(x.dtype)
    return x


def tie(x, *deps):
    anywhere = pl.BlockSpec(memory_space=pl.ANY)
    return pl.pallas_call(
        lambda *refs: None,
        in_specs=[anywhere] * (1 + len(deps)),
        out_specs=anywhere,
        out_shape=shape(x.shape, x.dtype),
        input_output_aliases={0: 0},
        name="tie",
    )(x, *deps)


def build(z_size, tp_size):
    shards = 2 * z_size
    ring = [0] + list(range(1, z_size, 2)) + list(range(z_size - 2, 0, -2))
    place = [ring.index(z) for z in range(z_size)]
    forward = [(ring[i], ring[(i + 1) % z_size]) for i in range(z_size)]
    backward = [(b, a) for a, b in forward]
    half_ring = z_size // 2
    offsets = [0]
    for k in range(1, half_ring):
        offsets += [-k, k]
    offsets += [half_ring]
    holder = [[ring[(place[z] + off) % z_size] for off in offsets] for z in range(z_size)]
    swap_core = [(0, 1), (1, 0)]

    def hop(x, bit):
        return lax.ppermute(x, "tp", [(t, t ^ bit) for t in range(tp_size)])

    def swap(x):
        return lax.ppermute(x, "core", swap_core)

    def ring_first(x):
        chunks = [x]
        ahead = back = x
        for _ in range(1, half_ring):
            ahead = lax.ppermute(ahead, "z", forward)
            back = lax.ppermute(back, "z", backward)
            chunks += [ahead, back]
        return chunks

    def ring_last(chunks, *deps):
        ahead, back = chunks[-2:]
        mid = ahead.shape[1] // 2
        one = lax.ppermute(after(ahead[:, :mid], back, *deps), "z", forward)
        two = lax.ppermute(after(back[:, mid:], ahead, *deps), "z", backward)
        return chunks + [one, two]

    def gather_ring(x, *deps):
        return ring_last(ring_first(x), *deps)

    def join_rows(chunks, *deps):
        return after(jnp.concatenate(chunks, axis=1), *deps)

    def scatter_first(parts):
        return (
            lax.ppermute(parts[-2], "z", forward),
            lax.ppermute(parts[-1], "z", backward),
        )

    def scatter_last(parts, came, *deps):
        one, two = came
        mid = parts[0].shape[1] // 2
        for k in range(half_ring - 1, 0, -1):
            fwd, bwd = parts[offsets.index(k)], parts[offsets.index(-k)]
            if k == half_ring - 1:
                fwd = jnp.concatenate([fwd[:, :mid] + one, fwd[:, mid:]], axis=1)
                bwd = jnp.concatenate([bwd[:, :mid], bwd[:, mid:] + two], axis=1)
            else:
                fwd = fwd + one
                bwd = bwd + two
            one = lax.ppermute(fwd, "z", forward)
            two = lax.ppermute(bwd, "z", backward)
        return after(parts[0] + one.astype(F32) + two.astype(F32), *deps)

    def scatter_ring(parts, *deps):
        return scatter_last(parts, scatter_first(parts), *deps)

    def tick(x):
        corner = lax.slice(x.reshape((-1,) + x.shape[-1:]), (0, 0), (16, 128))
        return swap(corner.astype(BF))

    def near_tp(x):
        return (hop(x, 1), hop(x, 2)) if tp_size == 4 else ()

    def far_tp(x, near, *deps):
        if tp_size != 4:
            return ()
        mid = x.shape[0] // 2
        return (
            hop(after(near[1][:mid], *deps), 1),
            hop(after(near[0][mid:], *deps), 2),
        )

    def stack_tp(x, near, far, *deps):
        if tp_size == 4:
            return after(jnp.stack([x, *near, jnp.concatenate(far, axis=0)]), *deps)
        held = x[None]
        bit = 1
        while bit < tp_size:
            held = jnp.concatenate([held, hop(held, bit)], axis=0)
            bit *= 2
        return held

    def gather_tp(x):
        near = near_tp(x)
        return stack_tp(x, near, far_tp(x, near))

    def scatter_tp_first(part):
        if tp_size == 4:
            mid = part.shape[1] // 2
            top, low = part[:, :mid], part[:, mid:]
            return hop(jnp.stack([top[1], top[3]]), 1), hop(jnp.stack([low[2], low[3]]), 2)
        return ()

    def scatter_tp_sums(part, came):
        if tp_size != 4:
            return (part,)
        over_x, over_y = came
        mid = part.shape[1] // 2
        top, low = part[:, :mid], part[:, mid:]
        return top[0] + over_x[0], low[0] + over_y[0], top[2] + over_x[1], low[1] + over_y[1]

    def scatter_tp_last(sums):
        if tp_size == 4:
            top, low, top_on, low_on = sums
            return jnp.concatenate([top + hop(top_on, 2), low + hop(low_on, 1)], axis=0)
        (part,) = sums
        bit = tp_size // 2
        while bit:
            part = part[:bit] + hop(part[bit:], bit)
            bit //= 2
        return part[0]

    def to_z(x):
        return lax.all_to_all(x, "z", split_axis=0, concat_axis=0, tiled=True)

    def on_device(
        layer_in,
        positions,
        seq_ids,
        norm1_gain,
        norm2_gain,
        w_query,
        w_key,
        w_value,
        w_out,
        w_gate,
        w_up,
        w_down,
        out_grad,
    ):
        z, core, tp = lax.axis_index("z"), lax.axis_index("core"), lax.axis_index("tp")
        rows, width = layer_in.shape
        half = width // 2
        block = rows // 4
        own = rows // tp_size
        group = own * z_size
        length = rows * shards // 2
        k_rows = width // shards
        heads = w_query.shape[1] * tp_size // HD
        heads_here = heads // z_size
        plain = w_query.shape[1] == z_size * HD and heads_here == tp_size
        flipped = core == 1

        def split(x):
            lead = x.shape[:-1]
            x = x.reshape(lead + (z_size, 2, k_rows))
            even, odd = x[..., 0, :].reshape(lead + (half,)), x[..., 1, :].reshape(lead + (half,))
            return jnp.stack([jnp.where(flipped, odd, even), jnp.where(flipped, even, odd)])

        def join(x):
            lead = x.shape[1:-1]
            even, odd = jnp.where(flipped, x[1], x[0]), jnp.where(flipped, x[0], x[1])
            even = even.reshape(lead + (z_size, 1, k_rows))
            odd = odd.reshape(lead + (z_size, 1, k_rows))
            return jnp.concatenate([even, odd], axis=-2).reshape(lead + (width,))

        sound = positions[0] >= 0

        def stage(run):
            outs = jax.eval_shape(run)
            blank = lambda: jax.tree.map(lambda o: jnp.zeros(o.shape, o.dtype), outs)
            return lax.cond(sound, run, blank)

        key = seq_ids.reshape(4, block)[:, 0] * (4 * length) + positions.reshape(4, block)[:, 0]
        rank = jnp.sum((key[None, :] < key[:, None]).astype(jnp.int32), axis=1)
        source_core = tp // (tp_size // 2)
        offset = (tp % (tp_size // 2)) * own

        def piece(x, seq):
            wanted = 2 * seq + offset // block
            start = jnp.sum(jnp.where(rank == wanted, jnp.arange(4, dtype=jnp.int32), 0)) * block
            return lax.dynamic_slice(x, (start + offset % block, 0), (own, width))

        def take_own(x):
            return split(jnp.where(core == source_core, piece(x, core), swap(piece(x, 1 - core))))

        x_own = take_own(layer_in).astype(F32)
        gy_own = take_own(out_grad)
        gain1 = split(norm1_gain)[:, None]
        gain2 = split(norm2_gain)[:, None]
        scale1 = lax.rsqrt(jnp.mean(x_own * x_own, axis=(0, 2), keepdims=True) + EPSILON)
        xn1_own = x_own * scale1 * gain1

        quarter = HD // 2
        frequency = jnp.power(F32(10000.0), -jnp.arange(quarter, dtype=F32) / quarter)
        phase = jnp.arange(length, dtype=jnp.int32).astype(F32)[:, None] * frequency[None, :]

        def rotations(*deps):
            turned = after(phase, *deps)
            rot_cos, rot_sin = jnp.cos(turned), jnp.sin(turned)
            cos = jnp.concatenate([rot_cos, rot_cos], axis=1)
            return cos, jnp.concatenate([rot_sin, -rot_sin], axis=1)

        def exchange(w):
            return to_z(w).reshape(half, w.shape[2])

        if plain:
            (low,) = pack_weights(
                (w_query, w_key, w_value), w_out, z_size, False, "pack_heads"
            )
            low = exchange(low)
            xn1_low = after(xn1_own, low).astype(BF)

            def begin():
                chunks = ring_first(xn1_low)
                near = near_tp(low)
                started = tick(low)
                turns = rotations(started)
                far = far_tp(low, near, *chunks[1:3], turns[0])
                ffn_low = pack_weights(
                    (w_gate, w_up), w_down, z_size, True, "pack_ffn", (tick(chunks[-1]),)
                )
                chunks = ring_last(chunks)
                full = stack_tp(low, near, far, *chunks[-2:])
                return join_rows(chunks), (full, swap(full)), turns, ffn_low

            xn1, head_w, (cos, sin), ffn_low = stage(begin)
        else:
            at_head = z * heads_here * HD

            def columns(w):
                w = lax.all_gather(w.astype(BF), "tp", axis=1, tiled=True)
                w = lax.all_gather(w, ("z", "core"), axis=0, tiled=True)
                w = lax.dynamic_slice(w, (0, at_head), (width, heads_here * HD))
                return jnp.swapaxes(split(w.T).reshape(2, heads_here, HD, half), 2, 3)

            low = [columns(w) for w in (w_query, w_key, w_value, w_out.T)]
            low = jnp.concatenate(low, axis=3)
            head_w = (low[0], low[1])
            xn1 = join_rows(gather_ring(xn1_own.astype(BF)))
            cos, sin = rotations()
            ffn_low = pack_weights((w_gate, w_up), w_down, z_size, True, "pack_ffn")
        gate_up_one = exchange(ffn_low[0])

        t_all = jnp.arange(tp_size, dtype=jnp.int32)[:, None]
        if plain:
            t_all = jnp.bitwise_xor(t_all, tp)
        z_all = jnp.asarray(holder, jnp.int32)[z][None, :]
        off_all = (t_all % (tp_size // 2)) * own
        shard_all = 2 * z_all + t_all // (tp_size // 2)
        block_all = jnp.where(off_all < block, shard_all, 2 * shards - 1 - shard_all)
        table = ((block_all * block + off_all % block) // own).reshape(-1)

        def to_heads(x):
            if plain:
                return [x[0]] + [hop(x[k], k) for k in range(1, tp_size)]
            every = lax.all_gather(jnp.stack(x), "tp", axis=0)
            every = lax.dynamic_index_in_dim(
                every, tp * heads_here // tp_size, axis=1, keepdims=False
            )
            return [every[k] for k in range(tp_size)]

        def to_tokens(x):
            if plain:
                return jnp.stack([x[0]] + [hop(x[k], k) for k in range(1, tp_size)])
            every = lax.all_gather(jnp.stack(x), "tp", axis=0)[:: tp_size // heads_here]
            return lax.dynamic_index_in_dim(every, tp, axis=1, keepdims=False)

        qkv = project(xn1, *head_w, 0, 3 * HD, "qkv")
        heads_out, saved = attend(table, to_heads(qkv), cos, sin, own, length)
        mixed = to_tokens(heads_out)
        attn = mm_back(mixed, *head_w, 3 * HD, own, "attn_out")

        def first():
            return x_own + scatter_ring(attn), near_tp(gate_up_one)

        hres, gate_up_near = stage(first)
        down_one = exchange(tie(ffn_low[1], hres))

        scale2 = lax.rsqrt(jnp.mean(hres * hres, axis=(0, 2), keepdims=True) + EPSILON)
        xn2_own = (hres * scale2 * gain2).astype(BF)

        def second():
            chunks = ring_first(xn2_own)
            far = far_tp(gate_up_one, gate_up_near, tick(xn2_own))
            low = stack_tp(gate_up_one, gate_up_near, far, *(tick(x) for x in chunks[1:3]))
            peer = swap(low)
            return join_rows(ring_last(chunks)), (low, peer)

        xn2, gate_up_w = stage(second)

        def third():
            chunks = ring_first(gy_own)
            near = near_tp(down_one)
            xn2_peer = swap(xn2[1])
            out = gate_up(xn2, *gate_up_w)
            far = far_tp(down_one, near, *chunks[1:3], out[0])
            chunks = ring_last(chunks, out[0])
            low = stack_tp(down_one, near, far, *chunks[-2:])
            return join_rows(chunks), (low, swap(low)), out, xn2_peer

        gy, down_w, (hid, to_gate, to_up), xn2_peer = stage(third)
        dgu, *dx = feed_back(gy, to_gate, to_up, *gate_up_w, *down_w, own)
        here = jnp.broadcast_to(tp, (1,)).astype(jnp.int32)

        def fourth():
            came = scatter_first(dx)
            gy_peer, hid_peer, dgu_peer = swap(gy[1]), swap(hid), swap(dgu)
            g_down = weight_grad(here, gy[0], gy_peer, hid[:, None], hid_peer[:, None], "g_down")
            return scatter_last(dx, came, g_down), g_down, dgu_peer

        dxn2, g_down, dgu_peer = stage(fourth)

        def sum_tp(part):
            return lax.psum_scatter(part, "tp", scatter_dimension=0, tiled=False)

        def place_columns(part, *deps):
            return to_z(after(part.reshape(z_size, k_rows, part.shape[1]), *deps))

        gain2_part = jnp.sum(dxn2 * hres * scale2, axis=1)
        e2 = dxn2 * gain2
        dres = (
            gy_own.astype(F32)
            + scale2 * e2
            - hres
            * (scale2 * scale2 * scale2)
            * jnp.mean(e2 * hres, axis=(0, 2), keepdims=True)
        )
        dres_low = dres.astype(BF)
        g_down = tie(sum_tp(g_down))

        def fifth():
            chunks = ring_first(dres_low)
            started = (tick(dres_low),)
            g_gu = weight_grad(here, xn2[0], xn2_peer, dgu, dgu_peer, "g_gate_up", started)
            started = tuple(tick(x) for x in chunks[1:3])
            ffn = mm_back(hid, *down_w, 0, own, "ffn_out", started)
            return join_rows(ring_last(chunks), g_gu), ffn, g_gu

        dres_all, ffn, g_gu = stage(fifth)
        g_gu = tie(sum_tp(g_gu))
        dmix = project(dres_all, *head_w, 3 * HD, HD, "dmix")
        dmix, came = stage(lambda: (to_heads(dmix), scatter_first(ffn)))
        dheads = attend_back(table, dmix, saved, cos, sin, own, length, ())

        def sixth():
            return to_tokens(dheads), hres + scatter_last(ffn, came), place_columns(g_down)

        dqkv, layer_own, g_down = stage(sixth)
        dx = mm_back(dqkv, *head_w, 0, own, "dxn1")

        def seventh():
            came = scatter_first(dx)
            peers = swap(xn1[1]), swap(dqkv), swap(dres_all[1]), swap(mixed)
            g_heads = weight_grad_heads(
                xn1[0], peers[0], dqkv, peers[1], dres_all[0], peers[2], mixed, peers[3]
            )
            if plain:
                g_heads = scatter_tp_sums(g_heads, scatter_tp_first(g_heads))
            return scatter_last(dx, came), g_heads

        dxn1, g_heads = stage(seventh)
        gain1_part = jnp.sum(dxn1 * x_own * scale1, axis=1)
        e1 = dxn1 * gain1
        in_own = (
            dres
            + scale1 * e1
            - x_own
            * (scale1 * scale1 * scale1)
            * jnp.mean(e1 * x_own, axis=(0, 2), keepdims=True)
        )

        in_own = join(in_own).astype(BF)
        gains = join(jnp.stack([gain1_part, gain2_part], axis=1)).reshape(2, shards, 1, k_rows)
        gains = jnp.broadcast_to(gains, (2, shards, tp_size, k_rows))
        gains = jnp.swapaxes(gains.reshape(2, shards * tp_size, k_rows), 0, 1)

        def spread_rows(every, dtype):
            if tp_size == 4 and own == block:
                slot = jnp.bitwise_xor(rank % 2, tp % 2)
                kept = slot + jnp.where(core == tp // 2, 0, 2)
                index = jnp.where(rank // 2 == core, kept, slot + 4)
                return place_blocks(index, every, dtype).reshape(rows, width)
            order = jnp.bitwise_xor(jnp.arange(tp_size, dtype=jnp.int32), tp)
            every = jnp.take(every, order, axis=0, mode="clip").reshape(2, rows // 2, width)
            kept = lax.dynamic_index_in_dim(every, core, axis=0, keepdims=False)
            sent = lax.dynamic_index_in_dim(every, 1 - core, axis=0, keepdims=False)
            blocks = jnp.concatenate([kept, swap(sent)]).reshape(4, block, width)
            index = jnp.where(flipped, jnp.bitwise_xor(rank, 2), rank)
            return jnp.take(blocks, index, axis=0, mode="clip").reshape(rows, width).astype(dtype)

        def eighth():
            near = near_tp(in_own)
            heads = scatter_tp_last(g_heads) if plain else g_heads
            in_all = spread_over(in_own, near)
            layer_low = join(layer_own).astype(BF)
            layer_all = spread_over(layer_low, near_tp(layer_low))
            placed = place_columns(g_gu)
            if plain:
                heads = place_columns(heads)
            in_grad, layer_out = spread_rows(in_all, F32), spread_rows(layer_all, BF)
            gate_up = unpack_columns(placed, 2, False, "unpack_gate_up")
            down = unpack_columns(g_down, 1, True, "unpack_down")
            return in_grad, layer_out, (*gate_up, *down), heads

        def spread_over(x, near, *deps):
            far = far_tp(x, near, *deps)
            if not (tp_size == 4 and own == block):
                return stack_tp(x, near, far)
            far = jnp.concatenate(far, axis=0)
            matched = core == tp // 2
            sent = jnp.where(matched, jnp.stack([near[1], far]), jnp.stack([x, near[0]]))
            return x[None], near[0][None], near[1][None], far[None], swap(sent)

        in_grad, layer_out, (g_gate, g_up, g_down), g_heads = stage(eighth)
        gains = lax.all_to_all(
            gains, ("z", "core", "tp"), split_axis=0, concat_axis=0, tiled=True
        )
        gains = jnp.sum(gains, axis=0)
        if plain:
            g_query, g_key, g_value, g_out = unpack_columns(g_heads, 4, True, "unpack_heads")
        else:

            def back_columns(i):
                part = jnp.swapaxes(g_heads[:, :, i * HD : (i + 1) * HD], 1, 2)
                part = join(jnp.stack([part, swap(part)])).reshape(heads_here * HD, width).T
                out = jnp.zeros((width, heads * HD), BF)
                out = lax.dynamic_update_slice(out, part, (0, at_head))
                out = jnp.where(flipped, jnp.zeros_like(out), out)
                out = lax.psum_scatter(out, ("z", "core"), scatter_dimension=0, tiled=True)
                return lax.psum_scatter(out, "tp", scatter_dimension=1, tiled=True).astype(F32)

            g_query, g_key, g_value, g_out = (back_columns(i) for i in range(4))
            g_out = g_out.T
        return (
            layer_out,
            in_grad,
            gains[0],
            gains[1],
            g_query,
            g_key,
            g_value,
            g_out,
            g_gate,
            g_up,
            g_down,
        )

    return on_device


def solution(mesh):
    tp_size = mesh.shape["tp"]
    z_size = mesh.shape["seq"] // 2
    split = Mesh(mesh.devices.reshape(z_size, 2, tp_size), ("z", "core", "tp"))
    seq = ("z", "core")
    in_specs = (
        P(seq, None),
        P(seq),
        P(seq),
        P(),
        P(),
        P(seq, "tp"),
        P(seq, "tp"),
        P(seq, "tp"),
        P("tp", seq),
        P(seq, "tp"),
        P(seq, "tp"),
        P("tp", seq),
        P(seq, None),
    )
    out_specs = (
        P(seq, None),
        P(seq, None),
        P(seq),
        P(seq),
        P(seq, "tp"),
        P(seq, "tp"),
        P(seq, "tp"),
        P("tp", seq),
        P(seq, "tp"),
        P(seq, "tp"),
        P("tp", seq),
    )
    return jax.shard_map(
        build(z_size, tp_size), mesh=split, in_specs=in_specs, out_specs=out_specs, check_vma=False
    )
```

```python
import functools
import math

import jax
import jax.numpy as jnp
from jax import lax
from jax.experimental import pallas as pl
from jax.experimental.pallas import tpu as pltpu
from jax.sharding import Mesh
from jax.sharding import PartitionSpec as P

HD = 128
EPSILON = 1e-06
LOG2E = 1.4426950408889634
BF = jnp.bfloat16
F32 = jnp.float32
SHARE = 1
VM = pl.BlockSpec(memory_space=pltpu.VMEM)
SM = pl.BlockSpec(memory_space=pltpu.SMEM)


def dot_nt(left, right):
    return lax.dot_general(left, right, (((1,), (1,)), ((), ())), preferred_element_type=F32)


def dot_nn(left, right):
    return lax.dot_general(left, right, (((1,), (0,)), ((), ())), preferred_element_type=F32)


def dot_tn(left, right):
    return lax.dot_general(left, right, (((0,), (0,)), ((), ())), preferred_element_type=F32)


def call(body, grid, in_specs, out_specs, out_shape, scratch, flops, bytes_accessed, name, deps):
    known = len(in_specs)
    skip = len(deps)

    def run(*refs):
        body(*refs[:known], *refs[known + skip :])

    made = pl.pallas_call(
        run,
        grid=grid,
        in_specs=list(in_specs) + [pl.BlockSpec(memory_space=pl.ANY)] * skip,
        out_specs=out_specs,
        out_shape=out_shape,
        scratch_shapes=scratch,
        compiler_params=pltpu.CompilerParams(
            vmem_limit_bytes=48 << 20,
            dimension_semantics=("arbitrary",) * len(grid),
        ),
        cost_estimate=pl.CostEstimate(
            flops=flops // SHARE, transcendentals=0, bytes_accessed=bytes_accessed // SHARE
        ),
        name=name,
    )
    return lambda *args: made(*args, *deps)


def shape(dims, dtype):
    return jax.ShapeDtypeStruct(dims, dtype)


def attend_kernel(tab_ref, *refs, groups, chunk, tile, bias2):
    qkv_refs, (cos_ref, sin_ref) = refs[:groups], refs[groups : groups + 2]
    out_refs = refs[groups + 2 : 2 * groups + 2]
    q_ref, k_ref, v_ref, acc_ref = refs[2 * groups + 2 :]
    rows = qkv_refs[0].shape[0]
    per_group = rows // chunk
    length = groups * rows
    for j in range(length // chunk):
        g, s = divmod(j, per_group)
        here = pl.ds(s * chunk, chunk)
        there = pl.ds(pl.multiple_of(tab_ref[j] * chunk, chunk), chunk)
        cos = cos_ref[there, :]
        sin = sin_ref[there, :]
        q = qkv_refs[g][here, 0:HD].astype(F32)
        k = qkv_refs[g][here, HD : 2 * HD].astype(F32)
        q_ref[there, :] = (q * cos - pltpu.roll(q, HD // 2, 1) * sin).astype(BF)
        k_ref[there, :] = (k * cos - pltpu.roll(k, HD // 2, 1) * sin).astype(BF)
        v_ref[there, :] = qkv_refs[g][here, 2 * HD : 3 * HD]
    slope = -LOG2E / math.sqrt(HD)

    def part(i, j, masked):
        qs = q_ref[pl.ds(i * tile, tile), :]
        ks = k_ref[pl.ds(j * tile, tile), :]
        vs = v_ref[pl.ds(j * tile, tile), :]
        sig = 1.0 / (1.0 + jnp.exp2(dot_nt(qs, ks) * slope + bias2))
        if masked:
            row = lax.broadcasted_iota(jnp.int32, (tile, tile), 0)
            col = lax.broadcasted_iota(jnp.int32, (tile, tile), 1)
            sig = jnp.where(col <= row, sig, 0.0)
        return dot_nn(sig.astype(BF), vs)

    def query(i, carry):
        own = pl.ds(pl.multiple_of(i * tile, tile), tile)
        acc_ref[own, :] = part(i, i, True)

        def key(j, carry):
            acc_ref[own, :] += part(i, j, False)
            return carry

        lax.fori_loop(0, i, key, 0)
        return carry

    lax.fori_loop(0, length // tile, query, 0)
    for j in range(length // chunk):
        g, s = divmod(j, per_group)
        there = pl.ds(pl.multiple_of(tab_ref[j] * chunk, chunk), chunk)
        out_refs[g][pl.ds(s * chunk, chunk), :] = acc_ref[there, :].astype(BF)


def attend_back_kernel(tab_ref, *refs, groups, chunk, tile, bias2):
    grad_refs = refs[:groups]
    q_ref, k_ref, v_ref, cos_ref, sin_ref = refs[groups : groups + 5]
    out_refs = refs[groups + 5 : 2 * groups + 5]
    do_ref, dq_ref, dk_ref, dv_ref = refs[2 * groups + 5 :]
    rows = grad_refs[0].shape[0]
    per_group = rows // chunk
    length = groups * rows
    for j in range(length // chunk):
        g, s = divmod(j, per_group)
        there = pl.ds(pl.multiple_of(tab_ref[j] * chunk, chunk), chunk)
        do_ref[there, :] = grad_refs[g][pl.ds(s * chunk, chunk), :]
    slope = -LOG2E / math.sqrt(HD)
    scale = 1.0 / math.sqrt(HD)

    def part(i, j, masked):
        qi = pl.ds(pl.multiple_of(i * tile, tile), tile)
        kj = pl.ds(pl.multiple_of(j * tile, tile), tile)
        qs, ks, vs, dos = q_ref[qi, :], k_ref[kj, :], v_ref[kj, :], do_ref[qi, :]
        sig = 1.0 / (1.0 + jnp.exp2(dot_nt(ks, qs) * slope + bias2))
        dsc = dot_nt(vs, dos) * sig * (1.0 - sig)
        if masked:
            row = lax.broadcasted_iota(jnp.int32, (tile, tile), 0)
            col = lax.broadcasted_iota(jnp.int32, (tile, tile), 1)
            sig = jnp.where(row <= col, sig, 0.0)
            dsc = jnp.where(row <= col, dsc, 0.0)
        dsc = dsc.astype(BF)
        dv = dot_nn(sig.astype(BF), dos)
        dk = dot_nn(dsc, qs)
        dq = dot_tn(dsc, ks)
        if masked:
            dq_ref[qi, :] = dq
            dk_ref[kj, :] = dk
            dv_ref[kj, :] = dv
        else:
            dq_ref[qi, :] += dq
            dk_ref[kj, :] += dk
            dv_ref[kj, :] += dv

    def query(i, carry):
        part(i, i, True)

        def key(j, carry):
            part(i, j, False)
            return carry

        lax.fori_loop(0, i, key, 0)
        return carry

    lax.fori_loop(0, length // tile, query, 0)
    for j in range(length // chunk):
        g, s = divmod(j, per_group)
        here = pl.ds(s * chunk, chunk)
        there = pl.ds(pl.multiple_of(tab_ref[j] * chunk, chunk), chunk)
        cos = cos_ref[there, :] * scale
        sin = sin_ref[there, :] * scale
        dq = dq_ref[there, :]
        dk = dk_ref[there, :]
        out_refs[g][here, 0:HD] = (dq * cos + pltpu.roll(dq, HD // 2, 1) * sin).astype(BF)
        out_refs[g][here, HD : 2 * HD] = (dk * cos + pltpu.roll(dk, HD // 2, 1) * sin).astype(BF)
        out_refs[g][here, 2 * HD : 3 * HD] = dv_ref[there, :].astype(BF)


def attend(table, qkv, cos, sin, chunk, length):
    groups = len(qkv)
    rows = qkv[0].shape[0]
    tile = min(512, length)
    full = shape((length, HD), BF)
    out = pl.pallas_call(
        functools.partial(
            attend_kernel, groups=groups, chunk=chunk, tile=tile, bias2=math.log2(length)
        ),
        out_shape=(shape((rows, HD), BF),) * groups + (full,) * 3,
        in_specs=[SM] + [VM] * (groups + 2),
        out_specs=(VM,) * (groups + 3),
        scratch_shapes=[pltpu.VMEM((length, HD), F32)],
        compiler_params=pltpu.CompilerParams(vmem_limit_bytes=40 << 20),
        cost_estimate=pl.CostEstimate(
            flops=2 * length * length * HD * 2,
            transcendentals=length * length * 2,
            bytes_accessed=length * HD * 24 * 2,
        ),
        name="attend",
    )(table, *qkv, cos, sin)
    return out[:groups], out[groups:]


def attend_back(table, grad, saved, cos, sin, chunk, length, deps):
    groups = len(grad)
    rows = grad[0].shape[0]
    tile = min(512, length)
    known = groups + 6
    kernel = functools.partial(
        attend_back_kernel, groups=groups, chunk=chunk, tile=tile, bias2=math.log2(length)
    )

    def body(*refs):
        kernel(*refs[:known], *refs[known + len(deps) :])

    return pl.pallas_call(
        body,
        out_shape=(shape((rows, 3 * HD), BF),) * groups,
        in_specs=[SM] + [VM] * (groups + 5) + [pl.BlockSpec(memory_space=pl.ANY)] * len(deps),
        out_specs=(VM,) * groups,
        scratch_shapes=[pltpu.VMEM((length, HD), BF)] + [pltpu.VMEM((length, HD), F32)] * 3,
        compiler_params=pltpu.CompilerParams(vmem_limit_bytes=40 << 20),
        cost_estimate=pl.CostEstimate(
            flops=5 * length * length * HD * 2,
            transcendentals=length * length * 2,
            bytes_accessed=length * HD * 24 * 2,
        ),
        name="attend_back",
    )(table, *grad, *saved, cos, sin, *deps)


def ring_shapes(own, slots, half):
    return (
        (shape((2, own, half), F32),)
        + (shape((2, own, half), BF),) * (slots - 2)
        + (shape((2, own // 2, half), BF),) * 2
    )


def ring_store(refs, h, rows, own):
    refs[0][h] = rows[:own]
    at = own
    for ref in refs[1:]:
        n = ref.shape[1]
        ref[h] = rows[at : at + n].astype(BF)
        at += n


def project(x, w0, w1, at, n, name, deps=()):
    _, g, half = x.shape
    t = w0.shape[0]

    def body(x_ref, a_ref, b_ref, *outs):
        k = pl.program_id(0)
        rows = (dot_nn(x_ref[0], a_ref[0]) + dot_nn(x_ref[1], b_ref[0])).astype(BF)
        for i, out_ref in enumerate(outs):

            @pl.when(k == i)
            def _():
                out_ref[...] = rows

    w_spec = pl.BlockSpec((1, half, n), lambda k: (k, 0, at // n))
    return call(
        body,
        (t,),
        [pl.BlockSpec((2, g, half), lambda k: (0, 0, 0)), w_spec, w_spec],
        (pl.BlockSpec((g, n), lambda k: (0, 0)),) * t,
        (shape((g, n), BF),) * t,
        [],
        4 * g * half * t * n,
        4 * half * t * n + 4 * g * half + 2 * g * t * n,
        name,
        deps,
    )(x, w0, w1)


def mm_back(parts, w0, w1, at, own, name, deps=()):
    t, g, n = parts.shape
    half = w0.shape[1]
    th = min(half, 512)

    def body(p_ref, a_ref, b_ref, *outs):
        for h, w_ref in enumerate((a_ref, b_ref)):
            acc = dot_nt(p_ref[0], w_ref[0])
            for k in range(1, t):
                acc += dot_nt(p_ref[k], w_ref[k])
            ring_store(outs, h, acc, own)

    w_spec = pl.BlockSpec((t, th, n), lambda j: (0, j, at // n))
    shapes = ring_shapes(own, g // own, half)
    return call(
        body,
        (half // th,),
        [pl.BlockSpec((t, g, n), lambda j: (0, 0, 0)), w_spec, w_spec],
        tuple(pl.BlockSpec(o.shape[:2] + (th,), lambda j: (0, 0, j)) for o in shapes),
        shapes,
        [],
        4 * g * half * t * n,
        4 * half * t * n + 2 * g * t * n + 4 * g * half,
        name,
        deps,
    )(parts, w0, w1)


def gate_up(x, w0, w1, deps=()):
    _, g, half = x.shape
    t, _, n = w0.shape
    n //= 2
    tn = min(n, 512)
    steps = n // tn

    def body(x_ref, g0_ref, g1_ref, u0_ref, u1_ref, hid_ref, to_gate_ref, to_up_ref):
        gate = dot_nn(x_ref[0], g0_ref[0]) + dot_nn(x_ref[1], g1_ref[0])
        up = dot_nn(x_ref[0], u0_ref[0]) + dot_nn(x_ref[1], u1_ref[0])
        sig = 1.0 / (1.0 + jnp.exp(-gate))
        act = gate * sig
        hid_ref[0] = (act * up).astype(BF)
        to_gate_ref[0] = (up * (sig * (1.0 + gate * (1.0 - sig)))).astype(BF)
        to_up_ref[0] = act.astype(BF)

    g_spec = pl.BlockSpec((1, half, tn), lambda k, j: (k, 0, j))
    u_spec = pl.BlockSpec((1, half, tn), lambda k, j: (k, 0, j + steps))
    f_spec = pl.BlockSpec((1, g, tn), lambda k, j: (k, 0, j))
    return call(
        body,
        (t, steps),
        [pl.BlockSpec((2, g, half), lambda k, j: (0, 0, 0)), g_spec, g_spec, u_spec, u_spec],
        (f_spec,) * 3,
        (shape((t, g, n), BF),) * 3,
        [],
        1000,
        1000,
        "gate_up",
        deps,
    )(x, w0, w1, w0, w1)


def feed_back(gy, to_gate, to_up, w0, w1, d0, d1, own, deps=()):
    _, g, half = gy.shape
    t, _, n = d0.shape
    tn = min(n, 512)
    steps = n // tn

    def body(y_ref, a_ref, b_ref, g0_ref, g1_ref, u0_ref, u1_ref, d0_ref, d1_ref, *rest):
        out_ref, outs, acc_ref = rest[0], rest[1:-1], rest[-1]
        k, j = pl.program_id(0), pl.program_id(1)
        dh = dot_nn(y_ref[0], d0_ref[0]) + dot_nn(y_ref[1], d1_ref[0])
        dgate = (dh * a_ref[0].astype(F32)).astype(BF)
        dup = (dh * b_ref[0].astype(F32)).astype(BF)
        out_ref[0, 0] = dgate
        out_ref[0, 1] = dup
        first = jnp.logical_and(k == 0, j == 0)
        for h, (p_ref, q_ref) in enumerate(((g0_ref, u0_ref), (g1_ref, u1_ref))):
            part = dot_nt(dgate, p_ref[0]) + dot_nt(dup, q_ref[0])

            @pl.when(first)
            def _():
                acc_ref[h] = part

            @pl.when(jnp.logical_not(first))
            def _():
                acc_ref[h] += part

        @pl.when(jnp.logical_and(k == t - 1, j == steps - 1))
        def _():
            for h in range(2):
                ring_store(outs, h, acc_ref[h], own)

    g_spec = pl.BlockSpec((1, half, tn), lambda k, j: (k, 0, j))
    u_spec = pl.BlockSpec((1, half, tn), lambda k, j: (k, 0, j + steps))
    f_spec = pl.BlockSpec((1, g, tn), lambda k, j: (k, 0, j))
    shapes = ring_shapes(own, g // own, half)
    return call(
        body,
        (t, steps),
        [pl.BlockSpec((2, g, half), lambda k, j: (0, 0, 0)), f_spec, f_spec]
        + [g_spec, g_spec, u_spec, u_spec, g_spec, g_spec],
        (pl.BlockSpec((1, 2, g, tn), lambda k, j: (k, 0, 0, j)),)
        + tuple(pl.BlockSpec(o.shape, lambda k, j: (0, 0, 0)) for o in shapes),
        (shape((t, 2, g, n), BF),) + shapes,
        [pltpu.VMEM((2, g, half), F32)],
        12 * g * half * t * n,
        12 * half * t * n + 8 * g * t * n + 8 * g * half,
        "feed_back",
        deps,
    )(gy, to_gate, to_up, w0, w1, w0, w1, d0, d1)


def weight_grad(place, left, left_peer, right, right_peer, name, deps=()):
    g, half = left.shape
    t, m, _, n = right.shape
    tn = n if n % 256 else min(n, 512)

    def body(s_ref, a_ref, b_ref, c_ref, d_ref, out_ref):
        del s_ref
        out_ref[0] = (
            dot_tn(a_ref[...], c_ref[0, 0]) + dot_tn(b_ref[...], d_ref[0, 0])
        ).astype(BF)

    l_spec = pl.BlockSpec((g, half), lambda k, i, j, s: (0, 0))
    r_spec = pl.BlockSpec((1, 1, g, tn), lambda k, i, j, s: (k, i, 0, j))
    return placed_call(
        body,
        (t, m, n // tn),
        [l_spec, l_spec, r_spec, r_spec],
        pl.BlockSpec((1, half, tn), lambda k, i, j, s: (k ^ s[0], 0, i * (n // tn) + j)),
        shape((t, half, m * n), BF),
        4 * g * half * t * m * n,
        4 * g * t * m * n + 4 * g * half + 2 * half * t * m * n,
        name,
        deps,
    )(place, left, left_peer, right, right_peer)


def weight_grad_heads(xn, xn_peer, dqkv, dqkv_peer, dres, dres_peer, mixed, mixed_peer, deps=()):
    g, half = xn.shape
    t, _, n = dqkv.shape
    m = mixed.shape[2]

    def body(a_ref, b_ref, c_ref, d_ref, e_ref, f_ref, g_ref, h_ref, out_ref):
        out_ref[0, :, :n] = (
            dot_tn(a_ref[...], c_ref[0]) + dot_tn(b_ref[...], d_ref[0])
        ).astype(BF)
        out_ref[0, :, n:] = (
            dot_tn(e_ref[...], g_ref[0]) + dot_tn(f_ref[...], h_ref[0])
        ).astype(BF)

    l_spec = pl.BlockSpec((g, half), lambda k: (0, 0))
    n_spec = pl.BlockSpec((1, g, n), lambda k: (k, 0, 0))
    m_spec = pl.BlockSpec((1, g, m), lambda k: (k, 0, 0))
    return call(
        body,
        (t,),
        [l_spec, l_spec, n_spec, n_spec, l_spec, l_spec, m_spec, m_spec],
        pl.BlockSpec((1, half, n + m), lambda k: (k, 0, 0)),
        shape((t, half, n + m), BF),
        [],
        4 * g * half * t * (n + m),
        4 * g * t * (n + m) + 8 * g * half + 2 * half * t * (n + m),
        "g_heads",
        deps,
    )(xn, xn_peer, dqkv, dqkv_peer, dres, dres_peer, mixed, mixed_peer)


def placed_call(body, grid, in_specs, out_specs, out_shape, flops, bytes_accessed, name, deps):
    known = len(in_specs) + 1
    skip = len(deps)

    def run(*refs):
        body(*refs[:known], *refs[known + skip :])

    made = pl.pallas_call(
        run,
        grid_spec=pltpu.PrefetchScalarGridSpec(
            num_scalar_prefetch=1,
            grid=grid,
            in_specs=list(in_specs) + [pl.BlockSpec(memory_space=pl.ANY)] * skip,
            out_specs=out_specs,
        ),
        out_shape=out_shape,
        compiler_params=pltpu.CompilerParams(
            vmem_limit_bytes=48 << 20,
            dimension_semantics=("arbitrary",) * len(grid),
        ),
        cost_estimate=pl.CostEstimate(
            flops=flops // SHARE, transcendentals=0, bytes_accessed=bytes_accessed // SHARE
        ),
        name=name,
    )
    return lambda *args: made(*args, *deps)


def pack_weights(columns, rows, parts, apart, name, deps=()):
    k, n = columns[0].shape
    n //= parts
    count = len(columns)

    def body(*refs):
        out_ref = refs[count + 1]
        for i, ref in enumerate(refs[:count]):
            out_ref[0, :, i * n : (i + 1) * n] = ref[...].astype(BF)
        turned = jnp.transpose(refs[count][...]).astype(BF)
        if apart:
            refs[-1][0] = turned
        else:
            out_ref[0, :, count * n :] = turned

    widths = (count * n, n) if apart else ((count + 1) * n,)
    return call(
        body,
        (parts,),
        [pl.BlockSpec((k, n), lambda p: (0, p))] * count + [pl.BlockSpec((n, k), lambda p: (p, 0))],
        tuple(pl.BlockSpec((1, k, w), lambda p: (p, 0, 0)) for w in widths),
        tuple(shape((parts, k, w), BF) for w in widths),
        [],
        1000,
        1000,
        name,
        deps,
    )(*columns, rows)


def unpack_columns(parts, count, transposed, name):
    z, k, n = parts.shape
    n //= count

    def body(in_ref, *outs):
        for i, ref in enumerate(outs):
            part = in_ref[0, :, i * n : (i + 1) * n].astype(F32)
            ref[...] = jnp.transpose(part) if transposed and i == count - 1 else part

    straight = (pl.BlockSpec((k, n), lambda p: (0, p)), shape((k, z * n), F32))
    turned = (pl.BlockSpec((n, k), lambda p: (p, 0)), shape((z * n, k), F32))
    outs = [straight] * (count - 1) + [turned if transposed else straight]
    return call(
        body,
        (z,),
        [pl.BlockSpec((1, k, count * n), lambda p: (p, 0, 0))],
        tuple(o[0] for o in outs),
        tuple(o[1] for o in outs),
        [],
        1000,
        1000,
        name,
        (),
    )(parts)


def place_blocks(index, sources, dtype):
    counts = [x.shape[0] for x in sources]
    rows, width = sources[0].shape[1:]
    blocks = index.shape[0]

    def body(s_ref, *refs):
        out_ref = refs[-1]
        wanted = s_ref[pl.program_id(0)]
        at = 0
        for n, ref in zip(counts, refs):
            for i in range(n):

                @pl.when(wanted == at)
                def _():
                    out_ref[0] = ref[i].astype(dtype)

                at += 1

    return placed_call(
        body,
        (blocks,),
        [pl.BlockSpec(x.shape, lambda b, s: (0, 0, 0)) for x in sources],
        pl.BlockSpec((1, rows, width), lambda b, s: (b, 0, 0)),
        shape((blocks, rows, width), dtype),
        0,
        12 * blocks * rows * width,
        "place",
        (),
    )(index, *sources)


def after(x, *deps):
    for d in deps:
        corner = lax.slice(d, [n - 1 for n in d.shape], d.shape).reshape(())
        x = x + (corner.astype(F32) * 0.0).astype(x.dtype)
    return x


def tie(x, *deps):
    anywhere = pl.BlockSpec(memory_space=pl.ANY)
    return pl.pallas_call(
        lambda *refs: None,
        in_specs=[anywhere] * (1 + len(deps)),
        out_specs=anywhere,
        out_shape=shape(x.shape, x.dtype),
        input_output_aliases={0: 0},
        name="tie",
    )(x, *deps)


def build(z_size, tp_size):
    shards = 2 * z_size
    ring = [0] + list(range(1, z_size, 2)) + list(range(z_size - 2, 0, -2))
    place = [ring.index(z) for z in range(z_size)]
    forward = [(ring[i], ring[(i + 1) % z_size]) for i in range(z_size)]
    backward = [(b, a) for a, b in forward]
    half_ring = z_size // 2
    offsets = [0]
    for k in range(1, half_ring):
        offsets += [-k, k]
    offsets += [half_ring]
    holder = [[ring[(place[z] + off) % z_size] for off in offsets] for z in range(z_size)]
    swap_core = [(0, 1), (1, 0)]

    def hop(x, bit):
        return lax.ppermute(x, "tp", [(t, t ^ bit) for t in range(tp_size)])

    def swap(x):
        return lax.ppermute(x, "core", swap_core)

    def ring_first(x):
        chunks = [x]
        ahead = back = x
        for _ in range(1, half_ring):
            ahead = lax.ppermute(ahead, "z", forward)
            back = lax.ppermute(back, "z", backward)
            chunks += [ahead, back]
        return chunks

    def ring_last(chunks, *deps):
        ahead, back = chunks[-2:]
        mid = ahead.shape[1] // 2
        one = lax.ppermute(after(ahead[:, :mid], back, *deps), "z", forward)
        two = lax.ppermute(after(back[:, mid:], ahead, *deps), "z", backward)
        return chunks + [one, two]

    def gather_ring(x, *deps):
        return ring_last(ring_first(x), *deps)

    def join_rows(chunks, *deps):
        return after(jnp.concatenate(chunks, axis=1), *deps)

    def scatter_first(parts):
        return (
            lax.ppermute(parts[-2], "z", forward),
            lax.ppermute(parts[-1], "z", backward),
        )

    def scatter_last(parts, came, *deps):
        one, two = came
        mid = parts[0].shape[1] // 2
        for k in range(half_ring - 1, 0, -1):
            fwd, bwd = parts[offsets.index(k)], parts[offsets.index(-k)]
            if k == half_ring - 1:
                fwd = jnp.concatenate([fwd[:, :mid] + one, fwd[:, mid:]], axis=1)
                bwd = jnp.concatenate([bwd[:, :mid], bwd[:, mid:] + two], axis=1)
            else:
                fwd = fwd + one
                bwd = bwd + two
            one = lax.ppermute(fwd, "z", forward)
            two = lax.ppermute(bwd, "z", backward)
        return after(parts[0] + one.astype(F32) + two.astype(F32), *deps)

    def scatter_ring(parts, *deps):
        return scatter_last(parts, scatter_first(parts), *deps)

    def tick(x):
        corner = lax.slice(x.reshape((-1,) + x.shape[-1:]), (0, 0), (16, 128))
        return swap(corner.astype(BF))

    def near_tp(x):
        return (hop(x, 1), hop(x, 2)) if tp_size == 4 else ()

    def far_tp(x, near, *deps):
        if tp_size != 4:
            return ()
        mid = x.shape[0] // 2
        return (
            hop(after(near[1][:mid], *deps), 1),
            hop(after(near[0][mid:], *deps), 2),
        )

    def stack_tp(x, near, far, *deps):
        if tp_size == 4:
            return after(jnp.stack([x, *near, jnp.concatenate(far, axis=0)]), *deps)
        held = x[None]
        bit = 1
        while bit < tp_size:
            held = jnp.concatenate([held, hop(held, bit)], axis=0)
            bit *= 2
        return held

    def gather_tp(x):
        near = near_tp(x)
        return stack_tp(x, near, far_tp(x, near))

    def scatter_tp_first(part):
        if tp_size == 4:
            mid = part.shape[1] // 2
            top, low = part[:, :mid], part[:, mid:]
            return hop(jnp.stack([top[1], top[3]]), 1), hop(jnp.stack([low[2], low[3]]), 2)
        return ()

    def scatter_tp_sums(part, came):
        if tp_size != 4:
            return (part,)
        over_x, over_y = came
        mid = part.shape[1] // 2
        top, low = part[:, :mid], part[:, mid:]
        return top[0] + over_x[0], low[0] + over_y[0], top[2] + over_x[1], low[1] + over_y[1]

    def scatter_tp_last(sums):
        if tp_size == 4:
            top, low, top_on, low_on = sums
            return jnp.concatenate([top + hop(top_on, 2), low + hop(low_on, 1)], axis=0)
        (part,) = sums
        bit = tp_size // 2
        while bit:
            part = part[:bit] + hop(part[bit:], bit)
            bit //= 2
        return part[0]

    def to_z(x):
        return lax.all_to_all(x, "z", split_axis=0, concat_axis=0, tiled=True)

    def on_device(
        layer_in,
        positions,
        seq_ids,
        norm1_gain,
        norm2_gain,
        w_query,
        w_key,
        w_value,
        w_out,
        w_gate,
        w_up,
        w_down,
        out_grad,
    ):
        z, core, tp = lax.axis_index("z"), lax.axis_index("core"), lax.axis_index("tp")
        rows, width = layer_in.shape
        half = width // 2
        block = rows // 4
        own = rows // tp_size
        group = own * z_size
        length = rows * shards // 2
        k_rows = width // shards
        heads = w_query.shape[1] * tp_size // HD
        heads_here = heads // z_size
        plain = w_query.shape[1] == z_size * HD and heads_here == tp_size
        flipped = core == 1

        def split(x):
            lead = x.shape[:-1]
            x = x.reshape(lead + (z_size, 2, k_rows))
            even, odd = x[..., 0, :].reshape(lead + (half,)), x[..., 1, :].reshape(lead + (half,))
            return jnp.stack([jnp.where(flipped, odd, even), jnp.where(flipped, even, odd)])

        def join(x):
            lead = x.shape[1:-1]
            even, odd = jnp.where(flipped, x[1], x[0]), jnp.where(flipped, x[0], x[1])
            even = even.reshape(lead + (z_size, 1, k_rows))
            odd = odd.reshape(lead + (z_size, 1, k_rows))
            return jnp.concatenate([even, odd], axis=-2).reshape(lead + (width,))

        sound = positions[0] >= 0

        def stage(run):
            outs = jax.eval_shape(run)
            blank = lambda: jax.tree.map(lambda o: jnp.zeros(o.shape, o.dtype), outs)
            return lax.cond(sound, run, blank)

        key = seq_ids.reshape(4, block)[:, 0] * (4 * length) + positions.reshape(4, block)[:, 0]
        rank = jnp.sum((key[None, :] < key[:, None]).astype(jnp.int32), axis=1)
        source_core = tp // (tp_size // 2)
        offset = (tp % (tp_size // 2)) * own

        def piece(x, seq):
            wanted = 2 * seq + offset // block
            start = jnp.sum(jnp.where(rank == wanted, jnp.arange(4, dtype=jnp.int32), 0)) * block
            return lax.dynamic_slice(x, (start + offset % block, 0), (own, width))

        def take_own(x):
            return split(jnp.where(core == source_core, piece(x, core), swap(piece(x, 1 - core))))

        x_own = take_own(layer_in).astype(F32)
        gy_own = take_own(out_grad)
        gain1 = split(norm1_gain)[:, None]
        gain2 = split(norm2_gain)[:, None]
        scale1 = lax.rsqrt(jnp.mean(x_own * x_own, axis=(0, 2), keepdims=True) + EPSILON)
        xn1_own = x_own * scale1 * gain1

        quarter = HD // 2
        frequency = jnp.power(F32(10000.0), -jnp.arange(quarter, dtype=F32) / quarter)
        phase = jnp.arange(length, dtype=jnp.int32).astype(F32)[:, None] * frequency[None, :]

        def rotations(*deps):
            turned = after(phase, *deps)
            rot_cos, rot_sin = jnp.cos(turned), jnp.sin(turned)
            cos = jnp.concatenate([rot_cos, rot_cos], axis=1)
            return cos, jnp.concatenate([rot_sin, -rot_sin], axis=1)

        def exchange(w):
            return to_z(w).reshape(half, w.shape[2])

        if plain:
            (low,) = pack_weights(
                (w_query, w_key, w_value), w_out, z_size, False, "pack_heads"
            )
            low = exchange(low)
            xn1_low = after(xn1_own, low).astype(BF)

            def begin():
                chunks = ring_first(xn1_low)
                near = near_tp(low)
                started = tick(low)
                turns = rotations(started)
                far = far_tp(low, near, *chunks[1:3], turns[0])
                ffn_low = pack_weights(
                    (w_gate, w_up), w_down, z_size, True, "pack_ffn", (tick(chunks[-1]),)
                )
                chunks = ring_last(chunks)
                full = stack_tp(low, near, far, *chunks[-2:])
                return join_rows(chunks), (full, swap(full)), turns, ffn_low

            xn1, head_w, (cos, sin), ffn_low = stage(begin)
        else:
            at_head = z * heads_here * HD

            def columns(w):
                w = lax.all_gather(w.astype(BF), "tp", axis=1, tiled=True)
                w = lax.all_gather(w, ("z", "core"), axis=0, tiled=True)
                w = lax.dynamic_slice(w, (0, at_head), (width, heads_here * HD))
                return jnp.swapaxes(split(w.T).reshape(2, heads_here, HD, half), 2, 3)

            low = [columns(w) for w in (w_query, w_key, w_value, w_out.T)]
            low = jnp.concatenate(low, axis=3)
            head_w = (low[0], low[1])
            xn1 = join_rows(gather_ring(xn1_own.astype(BF)))
            cos, sin = rotations()
            ffn_low = pack_weights((w_gate, w_up), w_down, z_size, True, "pack_ffn")
        gate_up_one = exchange(ffn_low[0])

        t_all = jnp.arange(tp_size, dtype=jnp.int32)[:, None]
        if plain:
            t_all = jnp.bitwise_xor(t_all, tp)
        z_all = jnp.asarray(holder, jnp.int32)[z][None, :]
        off_all = (t_all % (tp_size // 2)) * own
        shard_all = 2 * z_all + t_all // (tp_size // 2)
        block_all = jnp.where(off_all < block, shard_all, 2 * shards - 1 - shard_all)
        table = ((block_all * block + off_all % block) // own).reshape(-1)

        def to_heads(x):
            if plain:
                return [x[0]] + [hop(x[k], k) for k in range(1, tp_size)]
            every = lax.all_gather(jnp.stack(x), "tp", axis=0)
            every = lax.dynamic_index_in_dim(
                every, tp * heads_here // tp_size, axis=1, keepdims=False
            )
            return [every[k] for k in range(tp_size)]

        def to_tokens(x):
            if plain:
                return jnp.stack([x[0]] + [hop(x[k], k) for k in range(1, tp_size)])
            every = lax.all_gather(jnp.stack(x), "tp", axis=0)[:: tp_size // heads_here]
            return lax.dynamic_index_in_dim(every, tp, axis=1, keepdims=False)

        qkv = project(xn1, *head_w, 0, 3 * HD, "qkv")
        heads_out, saved = attend(table, to_heads(qkv), cos, sin, own, length)
        mixed = to_tokens(heads_out)
        attn = mm_back(mixed, *head_w, 3 * HD, own, "attn_out")

        def first():
            return x_own + scatter_ring(attn), near_tp(gate_up_one)

        hres, gate_up_near = stage(first)
        down_one = exchange(tie(ffn_low[1], hres))

        scale2 = lax.rsqrt(jnp.mean(hres * hres, axis=(0, 2), keepdims=True) + EPSILON)
        xn2_own = (hres * scale2 * gain2).astype(BF)

        def second():
            chunks = ring_first(xn2_own)
            far = far_tp(gate_up_one, gate_up_near, tick(xn2_own))
            low = stack_tp(gate_up_one, gate_up_near, far, *(tick(x) for x in chunks[1:3]))
            peer = swap(low)
            return join_rows(ring_last(chunks)), (low, peer)

        xn2, gate_up_w = stage(second)

        def third():
            chunks = ring_first(gy_own)
            near = near_tp(down_one)
            xn2_peer = swap(xn2[1])
            out = gate_up(xn2, *gate_up_w)
            far = far_tp(down_one, near, *chunks[1:3], out[0])
            chunks = ring_last(chunks, out[0])
            low = stack_tp(down_one, near, far, *chunks[-2:])
            return join_rows(chunks), (low, swap(low)), out, xn2_peer

        gy, down_w, (hid, to_gate, to_up), xn2_peer = stage(third)
        dgu, *dx = feed_back(gy, to_gate, to_up, *gate_up_w, *down_w, own)
        here = jnp.broadcast_to(tp, (1,)).astype(jnp.int32)

        def fourth():
            came = scatter_first(dx)
            gy_peer, hid_peer, dgu_peer = swap(gy[1]), swap(hid), swap(dgu)
            g_down = weight_grad(here, gy[0], gy_peer, hid[:, None], hid_peer[:, None], "g_down")
            return scatter_last(dx, came, g_down), g_down, dgu_peer

        dxn2, g_down, dgu_peer = stage(fourth)

        def sum_tp(part):
            return lax.psum_scatter(part, "tp", scatter_dimension=0, tiled=False)

        def place_columns(part, *deps):
            return to_z(after(part.reshape(z_size, k_rows, part.shape[1]), *deps))

        gain2_part = jnp.sum(dxn2 * hres * scale2, axis=1)
        e2 = dxn2 * gain2
        dres = (
            gy_own.astype(F32)
            + scale2 * e2
            - hres
            * (scale2 * scale2 * scale2)
            * jnp.mean(e2 * hres, axis=(0, 2), keepdims=True)
        )
        dres_low = dres.astype(BF)
        g_down = tie(sum_tp(g_down))

        def fifth():
            chunks = ring_first(dres_low)
            started = (tick(dres_low),)
            g_gu = weight_grad(here, xn2[0], xn2_peer, dgu, dgu_peer, "g_gate_up", started)
            started = tuple(tick(x) for x in chunks[1:3])
            ffn = mm_back(hid, *down_w, 0, own, "ffn_out", started)
            return join_rows(ring_last(chunks), g_gu), ffn, g_gu

        dres_all, ffn, g_gu = stage(fifth)
        g_gu = tie(sum_tp(g_gu))
        dmix = project(dres_all, *head_w, 3 * HD, HD, "dmix")
        dmix, came = stage(lambda: (to_heads(dmix), scatter_first(ffn)))
        dheads = attend_back(table, dmix, saved, cos, sin, own, length, ())

        def sixth():
            return to_tokens(dheads), hres + scatter_last(ffn, came), place_columns(g_down)

        dqkv, layer_own, g_down = stage(sixth)
        dx = mm_back(dqkv, *head_w, 0, own, "dxn1")

        def seventh():
            came = scatter_first(dx)
            peers = swap(xn1[1]), swap(dqkv), swap(dres_all[1]), swap(mixed)
            g_heads = weight_grad_heads(
                xn1[0], peers[0], dqkv, peers[1], dres_all[0], peers[2], mixed, peers[3]
            )
            if plain:
                g_heads = scatter_tp_sums(g_heads, scatter_tp_first(g_heads))
            return scatter_last(dx, came), g_heads

        dxn1, g_heads = stage(seventh)
        gain1_part = jnp.sum(dxn1 * x_own * scale1, axis=1)
        e1 = dxn1 * gain1
        in_own = (
            dres
            + scale1 * e1
            - x_own
            * (scale1 * scale1 * scale1)
            * jnp.mean(e1 * x_own, axis=(0, 2), keepdims=True)
        )

        in_own = join(in_own).astype(BF)
        gains = join(jnp.stack([gain1_part, gain2_part], axis=1)).reshape(2, shards, 1, k_rows)
        gains = jnp.broadcast_to(gains, (2, shards, tp_size, k_rows))
        gains = jnp.swapaxes(gains.reshape(2, shards * tp_size, k_rows), 0, 1)

        def spread_rows(every, dtype):
            if tp_size == 4 and own == block:
                slot = jnp.bitwise_xor(rank % 2, tp % 2)
                kept = slot + jnp.where(core == tp // 2, 0, 2)
                index = jnp.where(rank // 2 == core, kept, slot + 4)
                return place_blocks(index, every, dtype).reshape(rows, width)
            order = jnp.bitwise_xor(jnp.arange(tp_size, dtype=jnp.int32), tp)
            every = jnp.take(every, order, axis=0, mode="clip").reshape(2, rows // 2, width)
            kept = lax.dynamic_index_in_dim(every, core, axis=0, keepdims=False)
            sent = lax.dynamic_index_in_dim(every, 1 - core, axis=0, keepdims=False)
            blocks = jnp.concatenate([kept, swap(sent)]).reshape(4, block, width)
            index = jnp.where(flipped, jnp.bitwise_xor(rank, 2), rank)
            return jnp.take(blocks, index, axis=0, mode="clip").reshape(rows, width).astype(dtype)

        def eighth():
            near = near_tp(in_own)
            heads = scatter_tp_last(g_heads) if plain else g_heads
            in_all = spread_over(in_own, near)
            layer_low = join(layer_own).astype(BF)
            layer_all = spread_over(layer_low, near_tp(layer_low))
            placed = place_columns(g_gu)
            if plain:
                heads = place_columns(heads)
            in_grad, layer_out = spread_rows(in_all, F32), spread_rows(layer_all, BF)
            gate_up = unpack_columns(placed, 2, False, "unpack_gate_up")
            down = unpack_columns(g_down, 1, True, "unpack_down")
            return in_grad, layer_out, (*gate_up, *down), heads

        def spread_over(x, near, *deps):
            far = far_tp(x, near, *deps)
            if not (tp_size == 4 and own == block):
                return stack_tp(x, near, far)
            far = jnp.concatenate(far, axis=0)
            matched = core == tp // 2
            sent = jnp.where(matched, jnp.stack([near[1], far]), jnp.stack([x, near[0]]))
            return x[None], near[0][None], near[1][None], far[None], swap(sent)

        in_grad, layer_out, (g_gate, g_up, g_down), g_heads = stage(eighth)
        gains = lax.all_to_all(
            gains, ("z", "core", "tp"), split_axis=0, concat_axis=0, tiled=True
        )
        gains = jnp.sum(gains, axis=0)
        if plain:
            g_query, g_key, g_value, g_out = unpack_columns(g_heads, 4, True, "unpack_heads")
        else:

            def back_columns(i):
                part = jnp.swapaxes(g_heads[:, :, i * HD : (i + 1) * HD], 1, 2)
                part = join(jnp.stack([part, swap(part)])).reshape(heads_here * HD, width).T
                out = jnp.zeros((width, heads * HD), BF)
                out = lax.dynamic_update_slice(out, part, (0, at_head))
                out = jnp.where(flipped, jnp.zeros_like(out), out)
                out = lax.psum_scatter(out, ("z", "core"), scatter_dimension=0, tiled=True)
                return lax.psum_scatter(out, "tp", scatter_dimension=1, tiled=True).astype(F32)

            g_query, g_key, g_value, g_out = (back_columns(i) for i in range(4))
            g_out = g_out.T
        return (
            layer_out,
            in_grad,
            gains[0],
            gains[1],
            g_query,
            g_key,
            g_value,
            g_out,
            g_gate,
            g_up,
            g_down,
        )

    return on_device


def solution(mesh):
    tp_size = mesh.shape["tp"]
    z_size = mesh.shape["seq"] // 2
    split = Mesh(mesh.devices.reshape(z_size, 2, tp_size), ("z", "core", "tp"))
    seq = ("z", "core")
    in_specs = (
        P(seq, None),
        P(seq),
        P(seq),
        P(),
        P(),
        P(seq, "tp"),
        P(seq, "tp"),
        P(seq, "tp"),
        P("tp", seq),
        P(seq, "tp"),
        P(seq, "tp"),
        P("tp", seq),
        P(seq, None),
    )
    out_specs = (
        P(seq, None),
        P(seq, None),
        P(seq),
        P(seq),
        P(seq, "tp"),
        P(seq, "tp"),
        P(seq, "tp"),
        P("tp", seq),
        P(seq, "tp"),
        P(seq, "tp"),
        P("tp", seq),
    )
    return jax.shard_map(
        build(z_size, tp_size), mesh=split, in_specs=in_specs, out_specs=out_specs, check_vma=False
    )
```
